32 devices in a mesh: freq: 4 (over z), plane: 8 (over y, x, core).
Axes of the slice: x: 2, y: 2, z: 4, core: 2. Of those that a mesh axis runs over, the one named last changes fastest.
Arguments:
- wavefield: float32 [4, 2, 2048, 2048], P('freq', None, 'plane'), may hold values from -6 to 6
- inv_table: float32 [4, 8, 2, 128, 128], P('freq'), may hold values from -1 to 1, as said below
- couple_table: float32 [4, 2, 128, 128], P('freq'), may hold values from -1 to 1
- rhs_table: float32 [4, 8, 2], P('freq'), may hold values from -0.25 to 0.25
- recv_index: int32 [2, 16], replicated, may hold values from 0 to 7
- shot_index: int32 [2, 16], replicated, may hold values from 0 to 7
Outputs:
- migrated: float32 [4, 2, 2048, 2048], P('freq', None, 'plane')
- image: float32 [2, 2048], P(None, 'plane')
The draws below stay inside these ranges and needn't reach their ends.
Inputs may be any that keep to these rules, and one draw needn't show every extreme that they name: `inv_table`: real and imaginary parts of the group inverses.
All inputs are finite; a program needn't handle non-finite values.
Results may differ from the reference program's by a relative error of at most 0.0003.
Values sent between devices are 32-bit elements; how exact they have to be, the bound alone decides.
No kernel may reach another device: no remote copies, remote signals or barrier semaphores. Data moves between devices by JAX's collectives and lax.ppermute only.
A program may use at most 64 MiB of HBM per device.

```python
import math
import jax
import jax.numpy as jnp
from jax import lax

NX = 2048
GROUP = 128
NV = 8
DEPTHS = 2
FREQS = 4


def draw_inv_table(key, part):
    noise = jax.random.normal(key, (FREQS, NV, 2, GROUP, GROUP), jnp.float32) * (0.3 / math.sqrt(GROUP))
    unit = jnp.eye(GROUP, dtype=jnp.float32)
    centre = jnp.stack([0.6 * unit, 0.3 * unit])
    return noise + centre[None, None]


def draw_couple_table(key, part):
    centre_value = 0.7
    radius = 0.2
    noise = jax.random.normal(jax.random.fold_in(key, 17), (FREQS, 2, GROUP, GROUP), jnp.float32)
    noise = jnp.clip(noise, -5.0, 5.0) * (radius / math.sqrt(2.0 * GROUP))
    unit = jnp.eye(GROUP, dtype=jnp.float32)
    centre = jnp.stack([centre_value * unit, jnp.zeros_like(unit)])
    return noise + centre[None]


def set_ends(values, stream_key, smallest, largest):
    longest = values.shape.index(max(values.shape))
    spots = []
    for shift in (0, 1):
        where = [jax.random.randint(jax.random.fold_in(stream_key, axis), (), 0, length) for axis, length in enumerate(values.shape)]
        where[longest] = (where[longest] + shift) % values.shape[longest]
        spots.append(tuple(where))
    return values.at[spots[0]].set(smallest).at[spots[1]].set(largest)


def level_of(own_key, dims, pieces, smallest, high):
    level = 1.0
    for dim, shards_of in pieces:
        draws = jax.random.uniform(jax.random.fold_in(jax.random.fold_in(own_key, 6), dim), (shards_of,), jnp.float32, smallest / len(pieces), high / len(pieces))
        level = level * jnp.repeat(jnp.exp(draws), dims[dim] // shards_of).reshape((-1,) + (1,) * (len(dims) - 1 - dim))
    return level


def centred(rng, shape, deviation, limit, cuts=(), kind=jnp.bfloat16):
    drawn = deviation * jax.random.normal(rng, shape, jnp.float32)
    if cuts:
        drawn = drawn * level_of(rng, shape, cuts, -0.22, 0.18)
    return jnp.clip(drawn, -limit, limit).astype(kind)


def setup_inputs(seed: int = 0) -> dict:
    keys = jax.random.split(jax.random.key(seed), 7)
    return {
        "wavefield": centred(keys[0], (FREQS, 2, NX, NX), 1.0, 6.0, ((0, 4), (2, 8)), jnp.float32),
        "inv_table": draw_inv_table(jax.random.fold_in(keys[6], 71), 0),
        "couple_table": draw_couple_table(jax.random.fold_in(keys[6], 71), 0),
        "rhs_table": jnp.clip(jax.random.uniform(keys[3], (FREQS, NV, 2), jnp.float32, -0.25, 0.25) * level_of(keys[3], (FREQS, NV, 2), ((0, 4),), -0.4, 0.0), -0.25, 0.25),
        "recv_index": set_ends(jax.random.randint(keys[4], (DEPTHS, NX // GROUP), 0, NV), jax.random.fold_in(keys[4], 1), 0, NV - 1).astype(jnp.int32),
        "shot_index": set_ends(jax.random.randint(keys[5], (DEPTHS, NX // GROUP), 0, NV), jax.random.fold_in(keys[5], 1), 0, NV - 1).astype(jnp.int32),
    }


highest = lax.Precision.HIGHEST


def complex_product(form, mat_re, mat_im, vec_re, vec_im):
    real_part = jnp.einsum(form, mat_re, vec_re, precision=highest) - jnp.einsum(form, mat_im, vec_im, precision=highest)
    imag_part = jnp.einsum(form, mat_re, vec_im, precision=highest) + jnp.einsum(form, mat_im, vec_re, precision=highest)
    return real_part, imag_part


def line_pass(wave_field, index, inv_table, couple_table, rhs_table):
    freqs = wave_field.shape[0]
    lines = wave_field.shape[2]
    length = wave_field.shape[3]
    group_count = length // GROUP
    levels = jnp.arange(NV, dtype=jnp.int32)
    one_hot = (index[:, None] == levels[None, :]).astype(jnp.float32)
    inv_sel = jnp.einsum('kv,fvcab->fkcab', one_hot, inv_table, precision=highest)
    rhs_sel = jnp.einsum('kv,fvc->fkc', one_hot, rhs_table, precision=highest)
    padded = jnp.pad(wave_field, ((0, 0), (0, 0), (0, 0), (1, 1)))
    second = padded[..., :-2] + padded[..., 2:] - 2.0 * wave_field
    shape = (freqs, lines, group_count, GROUP)
    coef_re = rhs_sel[:, None, :, 0, None]
    coef_im = rhs_sel[:, None, :, 1, None]
    base_re = wave_field[:, 0].reshape(shape)
    base_im = wave_field[:, 1].reshape(shape)
    second_re = second[:, 0].reshape(shape)
    second_im = second[:, 1].reshape(shape)
    source_re = base_re + coef_re * second_re - coef_im * second_im
    source_im = base_im + coef_re * second_im + coef_im * second_re
    local_re, local_im = complex_product('fkab,flkb->flka', inv_sel[:, :, 0], inv_sel[:, :, 1], source_re, source_im)
    couple_re = couple_table[:, 0]
    couple_im = couple_table[:, 1]

    def advance(carry, local):
        add_re, add_im = complex_product('fab,flb->fla', couple_re, couple_im, carry[0], carry[1])
        new_value = (local[0] + add_re, local[1] + add_im)
        return new_value, new_value

    zeros = jnp.zeros((freqs, lines, GROUP), jnp.float32)
    seq_re = jnp.moveaxis(local_re, 2, 0)
    seq_im = jnp.moveaxis(local_im, 2, 0)
    _, (out_re, out_im) = lax.scan(advance, (zeros, zeros), (seq_re, seq_im), reverse=True)
    out_re = jnp.moveaxis(out_re, 0, 2).reshape(freqs, lines, length)
    out_im = jnp.moveaxis(out_im, 0, 2).reshape(freqs, lines, length)
    return jnp.stack([out_re, out_im], axis=1)


def one_frequency(inputs):
    wave_field, inv_table, couple_table, rhs_table, recv_index, shot_index = inputs
    wave_field = wave_field[None]
    inv_table = inv_table[None]
    couple_table = couple_table[None]
    rhs_table = rhs_table[None]
    images = []
    for step_index in range(DEPTHS):
        wave_field = line_pass(wave_field, recv_index[step_index], inv_table, couple_table, rhs_table)
        turned = jnp.swapaxes(wave_field, 2, 3)
        turned = line_pass(turned, shot_index[step_index], inv_table, couple_table, rhs_table)
        wave_field = jnp.swapaxes(turned, 2, 3)
        images.append(jnp.diagonal(wave_field[0, 0]))
    return wave_field[0], jnp.stack(images)


def reference(wavefield, inv_table, couple_table, rhs_table, recv_index, shot_index):
    freqs = wavefield.shape[0]
    recv_all = jnp.broadcast_to(recv_index[None], (freqs,) + recv_index.shape)
    shot_all = jnp.broadcast_to(shot_index[None], (freqs,) + shot_index.shape)
    migrated, images = lax.map(one_frequency, (wavefield, inv_table, couple_table, rhs_table, recv_all, shot_all))
    return migrated, jnp.sum(images, axis=0)
```

```python
import functools

import jax
import jax.numpy as jnp
from jax import lax
from jax.experimental import pallas as pl
from jax.experimental.pallas import tpu as pltpu
from jax.sharding import PartitionSpec as P

NX = 2048
GROUP = 128
DEPTHS = 2


highest = lax.Precision.HIGHEST


def complex_product(form, mat_re, mat_im, vec_re, vec_im):
    real_part = jnp.einsum(form, mat_re, vec_re, precision=highest) - jnp.einsum(
        form, mat_im, vec_im, precision=highest
    )
    imag_part = jnp.einsum(form, mat_re, vec_im, precision=highest) + jnp.einsum(
        form, mat_im, vec_re, precision=highest
    )
    return (real_part, imag_part)


def select_rows(index, table):
    levels = jnp.arange(table.shape[1], dtype=jnp.int32)
    one_hot = (index[:, None] == levels[None, :]).astype(jnp.float32)
    return jnp.einsum("kv,fv...->fk...", one_hot, table, precision=highest)


def coupling_powers(couple_table, group_count):
    power_re = couple_table[:, 0]
    power_im = couple_table[:, 1]
    powers = []
    reach = 1
    while reach < group_count:
        powers.append((power_re, power_im))
        power_re, power_im = complex_product("fab,fbc->fac", power_re, power_im, power_re, power_im)
        reach = reach * 2
    return powers


def shifted_up(values, reach, group_axis):
    count = values.shape[group_axis]
    kept = lax.slice_in_dim(values, reach, count, axis=group_axis)
    zero_shape = list(values.shape)
    zero_shape[group_axis] = reach
    return jnp.concatenate([kept, jnp.zeros(zero_shape, values.dtype)], axis=group_axis)


def line_pass(wave_field, index, inv_table, rhs_table, powers, along_last):
    line_axis = 3 if along_last else 2
    freqs = wave_field.shape[0]
    length = wave_field.shape[line_axis]
    group_count = length // GROUP
    inv_sel = select_rows(index, inv_table)
    rhs_sel = select_rows(index, rhs_table)
    pad_widths = [(0, 0), (0, 0), (0, 0), (0, 0)]
    pad_widths[line_axis] = (1, 1)
    padded = jnp.pad(wave_field, pad_widths)
    beside = lax.slice_in_dim(padded, 0, length, axis=line_axis) + lax.slice_in_dim(
        padded, 2, length + 2, axis=line_axis
    )
    second = beside - 2.0 * wave_field
    if along_last:
        shape = (freqs, wave_field.shape[2], group_count, GROUP)
        coef_re = rhs_sel[:, None, :, 0, None]
        coef_im = rhs_sel[:, None, :, 1, None]
        local_form = "fkab,flkb->flka"
        power_form = "fab,flkb->flka"
        group_axis = 2
    else:
        shape = (freqs, group_count, GROUP, wave_field.shape[3])
        coef_re = rhs_sel[:, :, 0, None, None]
        coef_im = rhs_sel[:, :, 1, None, None]
        local_form = "fkab,fkbm->fkam"
        power_form = "fab,fkbm->fkam"
        group_axis = 1
    base_re = wave_field[:, 0].reshape(shape)
    base_im = wave_field[:, 1].reshape(shape)
    second_re = second[:, 0].reshape(shape)
    second_im = second[:, 1].reshape(shape)
    source_re = base_re + coef_re * second_re - coef_im * second_im
    source_im = base_im + coef_re * second_im + coef_im * second_re
    solved_re, solved_im = complex_product(
        local_form, inv_sel[:, :, 0], inv_sel[:, :, 1], source_re, source_im
    )
    reach = 1
    for power_re, power_im in powers:
        add_re, add_im = complex_product(
            power_form,
            power_re,
            power_im,
            shifted_up(solved_re, reach, group_axis),
            shifted_up(solved_im, reach, group_axis),
        )
        solved_re = solved_re + add_re
        solved_im = solved_im + add_im
        reach = reach * 2
    out_shape = (freqs,) + wave_field.shape[2:]
    return jnp.stack([solved_re.reshape(out_shape), solved_im.reshape(out_shape)], axis=1)


def to_columns(wave_field):
    return lax.all_to_all(wave_field, "plane", split_axis=3, concat_axis=2, tiled=True)


def to_rows(wave_field):
    return lax.all_to_all(wave_field, "plane", split_axis=2, concat_axis=3, tiled=True)


def diagonal_rows(wave_field, first_row):
    count = wave_field.shape[2]
    block = lax.dynamic_slice_in_dim(wave_field[:, 0], first_row, count, axis=2)
    return jnp.sum(jnp.diagonal(block, axis1=1, axis2=2), axis=0)


def diagonal_columns(wave_field, first_row):
    count = wave_field.shape[3]
    block = lax.dynamic_slice_in_dim(wave_field[:, 0], first_row, count, axis=1)
    return jnp.sum(jnp.diagonal(block, axis1=1, axis2=2), axis=0)


def image_part(partial_value):
    return lax.psum(partial_value, "freq")


def shards(wavefield, inv_table, couple_table, rhs_table, recv_index, shot_index):
    powers = coupling_powers(couple_table, NX // GROUP)
    row_count = wavefield.shape[2]
    first_row = lax.axis_index("plane") * row_count
    wave_field = wavefield
    parts = []
    for step_index in range(DEPTHS):
        if step_index % 2 == 0:
            wave_field = line_pass(
                wave_field, recv_index[step_index], inv_table, rhs_table, powers, True
            )
            wave_field = to_columns(wave_field)
            wave_field = line_pass(
                wave_field, shot_index[step_index], inv_table, rhs_table, powers, False
            )
            parts.append(image_part(diagonal_columns(wave_field, first_row)))
        else:
            wave_field = line_pass(
                wave_field, shot_index[step_index], inv_table, rhs_table, powers, False
            )
            wave_field = to_rows(wave_field)
            wave_field = line_pass(
                wave_field, recv_index[step_index], inv_table, rhs_table, powers, True
            )
            parts.append(image_part(diagonal_rows(wave_field, first_row)))
    stacked = jnp.stack(parts)
    return (wave_field, stacked)


f32 = jnp.float32
bf16 = jnp.bfloat16
VMEM_LIMIT = 40 * 1024 * 1024


def halves(value):
    high = value.astype(bf16)
    low = (value - high.astype(f32)).astype(bf16)
    return high, low


def mul(left, right):
    return jnp.dot(left, right, preferred_element_type=f32)


def product(left, right):
    (left_high, left_low), (right_high, right_low) = left, right
    return mul(left_high, right_high) + mul(left_low, right_high) + mul(left_high, right_low)


def explicit_source(value, beside, coef_re, coef_im):
    second_re = beside[0] - 2.0 * value[0]
    second_im = beside[1] - 2.0 * value[1]
    return (
        value[0] + coef_re * second_re - coef_im * second_im,
        value[1] + coef_re * second_im + coef_im * second_re,
    )


def params():
    return pltpu.CompilerParams(vmem_limit_bytes=VMEM_LIMIT)


def whole(shape, dtype=f32):
    return jax.ShapeDtypeStruct(shape, dtype)


def smem():
    return pl.BlockSpec(memory_space=pltpu.SMEM)


def vmem():
    return pl.BlockSpec(memory_space=pltpu.VMEM)


def cost(macs, size):
    return pl.CostEstimate(flops=2 * macs, bytes_accessed=size, transcendentals=0)


def table_kernel(inv_ref, couple_ref, left_high, left_low, right_high, right_low):
    group = couple_ref.shape[-1]
    levels = inv_ref.shape[0]
    for level in range(levels + 1):
        mat_re = inv_ref[level, 0] if level < levels else couple_ref[0]
        mat_im = inv_ref[level, 1] if level < levels else couple_ref[1]
        turned_re = mat_re.T
        turned_im = mat_im.T
        blocks = ((mat_re, -mat_im), (mat_im, mat_re))
        turned = ((turned_re, turned_im), (-turned_im, turned_re))
        for i in range(2):
            for j in range(2):
                where = (level, slice(i * group, (i + 1) * group), slice(j * group, (j + 1) * group))
                left_high[where], left_low[where] = halves(blocks[i][j])
                right_high[where], right_low[where] = halves(turned[i][j])


def make_tables(inv_table, couple_table):
    levels, _, group, _ = inv_table.shape
    shape = whole((levels + 1, 2 * group, 2 * group), bf16)
    return pl.pallas_call(
        table_kernel,
        out_shape=[shape] * 4,
        in_specs=[vmem()] * 2,
        out_specs=[vmem()] * 4,
        compiler_params=params(),
        cost_estimate=cost(0, 6 * 1024 * 1024),
    )(inv_table, couple_table)


def line_groups(read, index_of, rhs_ref, high_ref, low_ref, group_count, group, write):
    couple = (high_ref[high_ref.shape[0] - 1], low_ref[low_ref.shape[0] - 1])
    following = None
    after = None
    for k in reversed(range(group_count)):
        level = index_of(k)
        coef_re = rhs_ref[level, 0]
        coef_im = rhs_ref[level, 1]
        value = read(k)
        before = read(k - 1) if k > 0 else None
        beside = []
        lane = lax.broadcasted_iota(jnp.int32, value[0].shape, 1)
        for part in range(2):
            low_side = pltpu.roll(value[part], 1, 1)
            edge = pltpu.roll(before[part], 1, 1) if k > 0 else jnp.zeros_like(low_side)
            low_side = jnp.where(lane == 0, edge, low_side)
            high_side = pltpu.roll(value[part], group - 1, 1)
            edge = pltpu.roll(after[part], group - 1, 1) if after is not None else jnp.zeros_like(high_side)
            high_side = jnp.where(lane == group - 1, edge, high_side)
            beside.append(low_side + high_side)
        source = halves(jnp.concatenate(explicit_source(value, beside, coef_re, coef_im), axis=1))
        solved = product(source, (high_ref[level], low_ref[level]))
        if following is not None:
            solved = solved + product(following, couple)
        following = halves(solved)
        after = value
        write(k, solved[:, :group], solved[:, group:])


def first_pass_kernel(place_ref, index_ref, rhs_ref, *refs, step, group, with_halo):
    if with_halo:
        field_ref, halo_ref, high_ref, low_ref, keep_ref, send_ref, own = refs
    else:
        field_ref, high_ref, low_ref, keep_ref, send_ref, own = refs
    length = field_ref.shape[-1]
    block = keep_ref.shape[-1]
    per_block = block // group
    core = place_ref[0] % 2

    def read(k):
        columns = slice(k * group, (k + 1) * group)
        parts = [field_ref[0, part, :, columns] for part in range(2)]
        if with_halo:
            for part in range(2):
                row = jnp.broadcast_to(halo_ref[0, part, :, columns], (8, group))
                parts[part] = jnp.concatenate([parts[part], row], axis=0)
        return parts

    def write(k, solved_re, solved_im):
        b = k // per_block
        columns = slice((k % per_block) * group, (k % per_block + 1) * group)
        own[b % 2, b // 2, 0, :, columns] = solved_re
        own[b % 2, b // 2, 1, :, columns] = solved_im

    line_groups(
        read, lambda k: index_ref[step, k], rhs_ref, high_ref, low_ref, length // group, group, write
    )
    keep_ref[...] = own[core]
    send_ref[...] = own[1 - core]


def first_pass(place, recv_index, rhs, field, halo, high, low, part, parts, block, group):
    length = field.shape[3]
    rows = field.shape[2] // parts
    lines = rows + (8 if halo is not None else 0)
    shape = (length // (2 * block), 2, lines, block)
    specs = [smem(), smem(), smem(), pl.BlockSpec((1, 2, rows, length), lambda i: (0, 0, part, 0))]
    args = [place, recv_index, rhs, field]
    if halo is not None:
        specs.append(vmem())
        args.append(halo)
    kernel = functools.partial(first_pass_kernel, step=0, group=group, with_halo=halo is not None)
    return pl.pallas_call(
        kernel,
        grid=(1,),
        out_shape=[whole(shape)] * 2,
        in_specs=specs + [vmem()] * 2,
        out_specs=[vmem()] * 2,
        scratch_shapes=[pltpu.VMEM((2,) + shape, f32)],
        compiler_params=params(),
        cost_estimate=cost(lines * length * group * 24, 8 * lines * length * 2),
    )(*args, high, low)


def shift_rows(ref, start, count):
    value = [ref[part, start : start + count, :] for part in range(2)]
    beside = [
        ref[part, start - 1 : start - 1 + count, :] + ref[part, start + 1 : start + 1 + count, :]
        for part in range(2)
    ]
    return value, beside


def sweep_groups(chip, groups, group, index_ref, rhs_ref, high_ref, low_ref, given, first, second, carry, last_row):
    last = high_ref.shape[0] - 1
    couple = (high_ref[last], low_ref[last])
    width = first.shape[-1]
    base = chip * groups
    total = index_ref.shape[1]

    def second_pass(k, following):
        level = index_ref[1, base + k]
        value, beside = shift_rows(first, 8 + k * group, group)
        source = explicit_source(value, beside, rhs_ref[level, 0], rhs_ref[level, 1])
        solved = product((high_ref[level], low_ref[level]), halves(jnp.concatenate(source, axis=0)))
        solved = solved + product(couple, following)
        second(k, solved)
        return halves(solved)

    zero_row = jnp.zeros((8, width), f32)
    top = 8 + groups * group
    for part in range(2):
        first[part, 0:8, :] = zero_row
        if carry is None:
            first[part, top : top + 8, :] = zero_row
        else:
            first[part, top : top + 8, :] = carry[0, part, 0:8, :]
    following = None
    if carry is not None:
        following = halves(jnp.concatenate([carry[0, 0], carry[0, 1]], axis=0))
    follows_second = None
    solved = None
    for k in reversed(range(groups)):
        parts = []
        if given is not None:
            level = index_ref[0, base + k]
            value, beside = shift_rows(given, 8 + k * group, group)
            source = explicit_source(value, beside, rhs_ref[level, 0], rhs_ref[level, 1])
            parts.append(product((high_ref[level], low_ref[level]), halves(jnp.concatenate(source, axis=0))))
        if following is not None:
            parts.append(product(couple, following))
        solved = sum(parts[1:], parts[0])
        first[0, 8 + k * group : 8 + (k + 1) * group, :] = solved[:group]
        first[1, 8 + k * group : 8 + (k + 1) * group, :] = solved[group:]
        following = halves(solved)
        if k == groups - 1:
            row_re = solved[group - 1 : group]
            row_im = solved[2 * group - 1 : 2 * group]
            after = base + groups
            level = index_ref[1, jnp.minimum(after, total - 1)]
            inside = jnp.where(after < total, 1.0, 0.0)
            coef_re = rhs_ref[level, 0] * inside
            coef_im = rhs_ref[level, 1] * inside
            term_re = coef_re * row_re - coef_im * row_im
            term_im = coef_re * row_im + coef_im * row_re
            column = high_ref[level, :, 0:1].astype(f32) + low_ref[level, :, 0:1].astype(f32)
            column_re, column_im = column[:group], column[group:]
            state = jnp.concatenate(
                [column_re * term_re - column_im * term_im, column_re * term_im + column_im * term_re], axis=0
            )
            if carry is not None:
                state = state + jnp.concatenate([carry[1, 0], carry[1, 1]], axis=0)
            follows_second = halves(state)
        else:
            follows_second = second_pass(k + 1, follows_second)
    if last_row is not None:
        tail = [
            product(
                (high_ref[last, (part + 1) * group - 16 : (part + 1) * group, :],
                 low_ref[last, (part + 1) * group - 16 : (part + 1) * group, :]),
                following,
            )
            for part in range(2)
        ]
        inside = jnp.where(chip > 0, 1.0, 0.0)
        for part in range(2):
            row = (tail[part][15:16] + last_row[part, 0:1, :]) * inside
            first[part, 0:8, :] = jnp.broadcast_to(row, (8, width))
    second_pass(0, follows_second)


def place_rows(core, own, other, given, groups, group):
    half = groups * group // 2
    low = pl.multiple_of(8 + core * half, 8)
    high = pl.multiple_of(8 + (1 - core) * half, 8)
    edge = pl.multiple_of(core * (2 * half + 8), 8)
    far = pl.multiple_of((1 - core) * (2 * half + 8), 8)
    quarter = half // 2
    for part in range(2):
        for rows, halo, (upper, lower) in ((low, edge, own), (high, far, other)):
            given[part, pl.ds(rows, quarter), :] = upper[0, part]
            given[part, pl.ds(pl.multiple_of(rows + quarter, 8), quarter), :] = lower[0, part, 0:quarter]
            given[part, pl.ds(halo, 8), :] = lower[0, part, quarter : quarter + 8]


def open_sweep_kernel(place_ref, index_ref, rhs_ref, high_ref, low_ref, keep_a, keep_b, come_a, come_b,
                      state_ref, row_ref, given, first, *, groups, group):
    device = place_ref[0]
    core = device % 2
    place_rows(core, (keep_a, keep_b), (come_a, come_b), given, groups, group)

    def second(k, solved):
        if k == 0:
            for part in range(2):
                state_ref[1, part] = solved[part * group : (part + 1) * group]

    sweep_groups(device // 2, groups, group, index_ref, rhs_ref, high_ref, low_ref, given, first, second, None, None)
    top = 8 + groups * group
    for part in range(2):
        state_ref[0, part] = first[part, 8 : 8 + group, :]
        row_ref[part] = jnp.broadcast_to(first[part, top - 1 : top, :], row_ref.shape[1:])


def map_kernel(index_ref, rhs_ref, high_ref, low_ref, map_high, map_low, carry, first, *, groups, group):
    rows = lax.broadcasted_iota(jnp.int32, (group, group), 0)
    columns = lax.broadcasted_iota(jnp.int32, (group, group), 1)
    carry[...] = jnp.zeros_like(carry)
    carry[0, 0] = (rows == columns).astype(f32)

    def store(which, mat_re, mat_im):
        blocks = ((mat_re, -mat_im), (mat_im, mat_re))
        for i in range(2):
            for j in range(2):
                where = (which, slice(i * group, (i + 1) * group), slice(j * group, (j + 1) * group))
                map_high[where], map_low[where] = halves(blocks[i][j])

    for chip in range(1, map_high.shape[0]):
        def second(k, solved):
            if k == 0:
                store(chip, solved[:group], solved[group:])

        sweep_groups(chip, groups, group, index_ref, rhs_ref, high_ref, low_ref, None, first, second, carry, None)
        if chip == 1:
            store(0, first[0, 8 : 8 + group, :], first[1, 8 : 8 + group, :])


def scan_kernel(place_ref, map_high, map_low, *refs, chips):
    states, outs, held = refs[:chips], refs[chips : 2 * chips], refs[2 * chips]
    chip = place_ref[0] // 2
    group = held.shape[-2]
    for offset in range(chips):
        held[chip ^ offset] = states[offset][...]
    keep = (map_high[0], map_low[0])
    for q in range(chips - 2, 0, -1):
        base = halves(jnp.concatenate([held[q + 1, 0, 0], held[q + 1, 0, 1]], axis=0))
        other = halves(jnp.concatenate([held[q + 1, 1, 0], held[q + 1, 1, 1]], axis=0))
        add_first = product(keep, base)
        add_second = product((map_high[q], map_low[q]), base) + product(keep, other)
        for part in range(2):
            rows = slice(part * group, (part + 1) * group)
            held[q, 0, part] = held[q, 0, part] + add_first[rows]
            held[q, 1, part] = held[q, 1, part] + add_second[rows]
    held[0] = jnp.zeros_like(held[0])
    for offset in range(chips):
        outs[offset][...] = held[((chip ^ offset) + 1) % chips]


def closed_sweep_kernel(place_ref, index_ref, rhs_ref, high_ref, low_ref, keep_a, keep_b, come_a, come_b,
                        carry_ref, row_ref, own_ref, other_ref, *refs, groups, group):
    image_ref = refs[0] if len(refs) == 4 else None
    given, first, result = refs[-3:]
    device = place_ref[0]
    core = device % 2
    place_rows(core, (keep_a, keep_b), (come_a, come_b), given, groups, group)

    def second(k, solved):
        for part in range(2):
            result[part, k * group : (k + 1) * group, :] = solved[part * group : (part + 1) * group]

    sweep_groups(device // 2, groups, group, index_ref, rhs_ref, high_ref, low_ref, given, first, second, carry_ref, row_ref)
    half = groups * group // 2
    mine = pl.multiple_of(core * half, 8)
    theirs = pl.multiple_of((1 - core) * half, 8)
    for part in range(2):
        own_ref[part] = result[part, pl.ds(mine, half), :]
        other_ref[part] = result[part, pl.ds(theirs, half), :]
    if image_ref is not None:
        square = first[0, pl.ds(pl.multiple_of(mine + 8, 8), half), :]
        image_ref[...] = diagonal_of(square)


def diagonal_of(square):
    rows = lax.broadcasted_iota(jnp.int32, square.shape, 0)
    columns = lax.broadcasted_iota(jnp.int32, square.shape, 1)
    return jnp.sum(jnp.where(rows == columns, square, 0.0), axis=0, keepdims=True)


def last_pass_kernel(place_ref, index_ref, rhs_ref, high_ref, low_ref, *refs, step, group, chips):
    owns, comes = refs[:chips], refs[chips : 2 * chips]
    out_ref, image_ref, field = refs[2 * chips :]
    device = place_ref[0]
    chip, core = device // 2, device % 2
    block = owns[0].shape[-1]
    length = field.shape[-1]
    for offset in range(chips):
        for ref, side in ((owns[offset], core), (comes[offset], 1 - core)):
            start = pl.multiple_of(((chip ^ offset) * 2 + side) * block, block)
            for part in range(2):
                field[part, :, pl.ds(start, block)] = ref[part]

    def read(k):
        return [field[part, :, k * group : (k + 1) * group] for part in range(2)]

    def write(k, solved_re, solved_im):
        out_ref[0, 0, :, k * group : (k + 1) * group] = solved_re
        out_ref[0, 1, :, k * group : (k + 1) * group] = solved_im

    line_groups(
        read, lambda k: index_ref[step, k], rhs_ref, high_ref, low_ref, length // group, group, write
    )
    image_ref[...] = diagonal_of(out_ref[0, 0, :, pl.ds(pl.multiple_of(device * block, block), block)])


def at_block(shape, offset):
    return pl.BlockSpec((1,) + shape, lambda i, place, _: ((place[0] // 2) ^ offset, 0, 0, 0))


def sweep_call(kernel, offset, place, index, rhs, tables, blocks, extra, outs, scratch, groups, group):
    width = blocks[0].shape[-1]
    specs = [smem(), vmem(), vmem()]
    specs += [at_block(item.shape[1:], offset) for item in blocks]
    specs += [vmem()] * len(extra)
    spec = pltpu.PrefetchScalarGridSpec(
        num_scalar_prefetch=2,
        grid=(1,),
        in_specs=specs,
        out_specs=[vmem()] * len(outs),
        scratch_shapes=scratch,
    )
    return pl.pallas_call(
        functools.partial(kernel, groups=groups, group=group),
        grid_spec=spec,
        out_shape=outs,
        compiler_params=params(),
        cost_estimate=cost(groups * group * width * group * 48, 8 * groups * group * width * 2),
    )(place, index, rhs, *tables, *blocks, *extra)


def sum_over(value, axis, count):
    reach = 1
    while reach < count:
        value = value + lax.ppermute(value, axis, [(i, i ^ reach) for i in range(count)])
        reach *= 2
    return value


def fast_shards(wavefield, inv_table, couple_table, rhs_table, recv_index, shot_index, *, devices, freqs):
    group = inv_table.shape[-1]
    rows, length = wavefield.shape[2:]
    block = rows
    chips = devices // 2
    groups = 2 * rows // group
    device = lax.axis_index("plane")
    place = device.reshape(1).astype(jnp.int32)
    rhs = rhs_table[0]
    left_high, left_low, right_high, right_low = make_tables(inv_table[0], couple_table[0])

    edge = lax.dynamic_slice_in_dim(wavefield, (device % 2) * (rows - 1), 1, axis=2)
    swap = [(d, d + 1) for d in range(1, devices - 1, 2)] + [(d + 1, d) for d in range(1, devices - 1, 2)]
    halo = lax.ppermute(edge, "plane", swap)

    partner = [(d, d ^ 1) for d in range(devices)]
    keep_a, send_a = first_pass(place, recv_index, rhs, wavefield, None, right_high, right_low, 0, 2, block, group)
    come_a = lax.ppermute(send_a, "plane", partner)
    keep_b, send_b = first_pass(place, recv_index, rhs, wavefield, halo, right_high, right_low, 1, 2, block, group)
    come_b = lax.ppermute(send_b, "plane", partner)
    blocks = (keep_a, keep_b, come_a, come_b)

    tables = (left_high, left_low)
    rows_scratch = pltpu.VMEM((2, groups * group + 16, block), f32)
    state_shape = whole((2, 2, group, block))
    row_shape = whole((2, 8, block))
    offsets = [3, 1, 2, 0]
    mine, theirs, edges = {}, {}, {}
    for offset in offsets:
        mine[offset], edges[offset] = sweep_call(
            open_sweep_kernel, offset, place, shot_index, rhs, tables, blocks, (),
            [state_shape, row_shape], [rows_scratch, rows_scratch], groups, group,
        )
        if offset:
            theirs[offset] = lax.ppermute(mine[offset], "plane", [(d, d ^ (2 * offset)) for d in range(devices)])
        else:
            theirs[0] = mine[0]
    ordered = jnp.stack([edges[offset] for offset in range(chips)])
    chip = device // 2
    ordered = ordered[jnp.arange(chips) ^ chip]
    above = lax.ppermute(ordered, "plane", [(d, d + 2) for d in range(devices - 2)])
    above = above[jnp.arange(chips) ^ chip]

    map_high, map_low = pl.pallas_call(
        functools.partial(map_kernel, groups=groups, group=group),
        out_shape=[whole((chips - 1, 2 * group, 2 * group), bf16)] * 2,
        in_specs=[smem(), smem(), vmem(), vmem()],
        out_specs=[vmem()] * 2,
        scratch_shapes=[pltpu.VMEM((2, 2, group, group), f32), pltpu.VMEM((2, groups * group + 16, group), f32)],
        compiler_params=params(),
        cost_estimate=cost(groups * group * group * group * 48, 1024 * 1024),
    )(shot_index, rhs, *tables)

    carries = pl.pallas_call(
        functools.partial(scan_kernel, chips=chips),
        out_shape=[state_shape] * chips,
        in_specs=[smem()] + [vmem()] * (2 + chips),
        out_specs=[vmem()] * chips,
        scratch_shapes=[pltpu.VMEM((chips,) + state_shape.shape, f32)],
        compiler_params=params(),
        cost_estimate=cost(3 * group * group * block * 24, 4 * 1024 * 1024),
    )(place, map_high, map_low, *[theirs[offset] for offset in range(chips)])

    owns, comes = {}, {}
    image_first = None
    piece = whole((2, rows, block))
    came = {
        offset: lax.ppermute(carries[offset], "plane", [(d, d ^ (2 * offset)) for d in range(devices)])
        for offset in offsets if offset
    }
    came[0] = carries[0]
    for offset in [0, 1, 2, 3]:
        outs = [piece, piece] + ([whole((1, block))] if offset == 0 else [])
        result = sweep_call(
            closed_sweep_kernel, offset, place, shot_index, rhs, tables, blocks, (came[offset], above[offset]),
            outs, [rows_scratch, rows_scratch, pltpu.VMEM((2, groups * group, block), f32)], groups, group,
        )
        owns[offset] = result[0]
        comes[offset] = lax.ppermute(result[1], "plane", partner)
        if offset == 0:
            image_first = sum_over(result[2], "freq", freqs)

    migrated, image_last = pl.pallas_call(
        functools.partial(last_pass_kernel, step=1, group=group, chips=chips),
        out_shape=[whole(wavefield.shape), whole((1, block))],
        in_specs=[smem(), smem(), smem()] + [vmem()] * (2 + 2 * chips),
        out_specs=[vmem()] * 2,
        scratch_shapes=[pltpu.VMEM((2, rows, length), f32)],
        compiler_params=params(),
        cost_estimate=cost(rows * length * group * 24, 8 * rows * length * 2),
    )(place, recv_index, rhs, right_high, right_low, *[owns[o] for o in range(chips)], *[comes[o] for o in range(chips)])
    image_last = sum_over(image_last, "freq", freqs)
    return migrated, jnp.concatenate([image_first, image_last], axis=0)


def solution(mesh):
    placed = (
        P("freq", None, "plane", None),
        P("freq", None, None, None, None),
        P("freq", None, None, None),
        P("freq", None, None),
        P(),
        P(),
    )
    devices = mesh.shape["plane"]
    freqs = mesh.shape["freq"]

    def body(*arrays):
        if devices == 8 and arrays[0].shape[2] == 2 * GROUP and arrays[0].shape[0] == 1 and freqs & (freqs - 1) == 0:
            return fast_shards(*arrays, devices=devices, freqs=freqs)
        return shards(*arrays)

    return jax.shard_map(
        body,
        mesh=mesh,
        in_specs=placed,
        out_specs=(P("freq", None, "plane", None), P(None, "plane")),
        check_vma=False,
    )
```

```python
import functools

import jax
import jax.numpy as jnp
from jax import lax
from jax.experimental import pallas as pl
from jax.experimental.pallas import tpu as pltpu
from jax.sharding import PartitionSpec as P

NX = 2048
GROUP = 128
DEPTHS = 2


highest = lax.Precision.HIGHEST


def complex_product(form, mat_re, mat_im, vec_re, vec_im):
    real_part = jnp.einsum(form, mat_re, vec_re, precision=highest) - jnp.einsum(
        form, mat_im, vec_im, precision=highest
    )
    imag_part = jnp.einsum(form, mat_re, vec_im, precision=highest) + jnp.einsum(
        form, mat_im, vec_re, precision=highest
    )
    return (real_part, imag_part)


def select_rows(index, table):
    levels = jnp.arange(table.shape[1], dtype=jnp.int32)
    one_hot = (index[:, None] == levels[None, :]).astype(jnp.float32)
    return jnp.einsum("kv,fv...->fk...", one_hot, table, precision=highest)


def coupling_powers(couple_table, group_count):
    power_re = couple_table[:, 0]
    power_im = couple_table[:, 1]
    powers = []
    reach = 1
    while reach < group_count:
        powers.append((power_re, power_im))
        power_re, power_im = complex_product("fab,fbc->fac", power_re, power_im, power_re, power_im)
        reach = reach * 2
    return powers


def shifted_up(values, reach, group_axis):
    count = values.shape[group_axis]
    kept = lax.slice_in_dim(values, reach, count, axis=group_axis)
    zero_shape = list(values.shape)
    zero_shape[group_axis] = reach
    return jnp.concatenate([kept, jnp.zeros(zero_shape, values.dtype)], axis=group_axis)


def line_pass(wave_field, index, inv_table, rhs_table, powers, along_last):
    line_axis = 3 if along_last else 2
    freqs = wave_field.shape[0]
    length = wave_field.shape[line_axis]
    group_count = length // GROUP
    inv_sel = select_rows(index, inv_table)
    rhs_sel = select_rows(index, rhs_table)
    pad_widths = [(0, 0), (0, 0), (0, 0), (0, 0)]
    pad_widths[line_axis] = (1, 1)
    padded = jnp.pad(wave_field, pad_widths)
    beside = lax.slice_in_dim(padded, 0, length, axis=line_axis) + lax.slice_in_dim(
        padded, 2, length + 2, axis=line_axis
    )
    second = beside - 2.0 * wave_field
    if along_last:
        shape = (freqs, wave_field.shape[2], group_count, GROUP)
        coef_re = rhs_sel[:, None, :, 0, None]
        coef_im = rhs_sel[:, None, :, 1, None]
        local_form = "fkab,flkb->flka"
        power_form = "fab,flkb->flka"
        group_axis = 2
    else:
        shape = (freqs, group_count, GROUP, wave_field.shape[3])
        coef_re = rhs_sel[:, :, 0, None, None]
        coef_im = rhs_sel[:, :, 1, None, None]
        local_form = "fkab,fkbm->fkam"
        power_form = "fab,fkbm->fkam"
        group_axis = 1
    base_re = wave_field[:, 0].reshape(shape)
    base_im = wave_field[:, 1].reshape(shape)
    second_re = second[:, 0].reshape(shape)
    second_im = second[:, 1].reshape(shape)
    source_re = base_re + coef_re * second_re - coef_im * second_im
    source_im = base_im + coef_re * second_im + coef_im * second_re
    solved_re, solved_im = complex_product(
        local_form, inv_sel[:, :, 0], inv_sel[:, :, 1], source_re, source_im
    )
    reach = 1
    for power_re, power_im in powers:
        add_re, add_im = complex_product(
            power_form,
            power_re,
            power_im,
            shifted_up(solved_re, reach, group_axis),
            shifted_up(solved_im, reach, group_axis),
        )
        solved_re = solved_re + add_re
        solved_im = solved_im + add_im
        reach = reach * 2
    out_shape = (freqs,) + wave_field.shape[2:]
    return jnp.stack([solved_re.reshape(out_shape), solved_im.reshape(out_shape)], axis=1)


def to_columns(wave_field):
    return lax.all_to_all(wave_field, "plane", split_axis=3, concat_axis=2, tiled=True)


def to_rows(wave_field):
    return lax.all_to_all(wave_field, "plane", split_axis=2, concat_axis=3, tiled=True)


def diagonal_rows(wave_field, first_row):
    count = wave_field.shape[2]
    block = lax.dynamic_slice_in_dim(wave_field[:, 0], first_row, count, axis=2)
    return jnp.sum(jnp.diagonal(block, axis1=1, axis2=2), axis=0)


def diagonal_columns(wave_field, first_row):
    count = wave_field.shape[3]
    block = lax.dynamic_slice_in_dim(wave_field[:, 0], first_row, count, axis=1)
    return jnp.sum(jnp.diagonal(block, axis1=1, axis2=2), axis=0)


def image_part(partial_value):
    return lax.psum(partial_value, "freq")


def shards(wavefield, inv_table, couple_table, rhs_table, recv_index, shot_index):
    powers = coupling_powers(couple_table, NX // GROUP)
    row_count = wavefield.shape[2]
    first_row = lax.axis_index("plane") * row_count
    wave_field = wavefield
    parts = []
    for step_index in range(DEPTHS):
        if step_index % 2 == 0:
            wave_field = line_pass(
                wave_field, recv_index[step_index], inv_table, rhs_table, powers, True
            )
            wave_field = to_columns(wave_field)
            wave_field = line_pass(
                wave_field, shot_index[step_index], inv_table, rhs_table, powers, False
            )
            parts.append(image_part(diagonal_columns(wave_field, first_row)))
        else:
            wave_field = line_pass(
                wave_field, shot_index[step_index], inv_table, rhs_table, powers, False
            )
            wave_field = to_rows(wave_field)
            wave_field = line_pass(
                wave_field, recv_index[step_index], inv_table, rhs_table, powers, True
            )
            parts.append(image_part(diagonal_rows(wave_field, first_row)))
    stacked = jnp.stack(parts)
    return (wave_field, stacked)


f32 = jnp.float32
bf16 = jnp.bfloat16


def halves(value):
    high = value.astype(bf16)
    low = (value - high.astype(f32)).astype(bf16)
    return high, low


def mul(left, right):
    return jnp.dot(left, right, preferred_element_type=f32)


def product(left, right):
    (left_high, left_low), (right_high, right_low) = left, right
    return mul(left_high, right_high) + mul(left_low, right_high) + mul(left_high, right_low)


def params(mebibytes):
    return pltpu.CompilerParams(vmem_limit_bytes=mebibytes * 1024 * 1024)


def whole(shape, dtype=f32):
    return jax.ShapeDtypeStruct(shape, dtype)


def smem():
    return pl.BlockSpec(memory_space=pltpu.SMEM)


def vmem():
    return pl.BlockSpec(memory_space=pltpu.VMEM)


def cost(macs, size):
    return pl.CostEstimate(flops=2 * macs, bytes_accessed=size, transcendentals=0)


def folded(level, inv_ref, rhs_ref):
    mat_re, mat_im = inv_ref[level, 0], inv_ref[level, 1]
    coef_re, coef_im = rhs_ref[level, 0], rhs_ref[level, 1]
    group = mat_re.shape[-1]
    lane = lax.broadcasted_iota(jnp.int32, mat_re.shape, 1)

    def differences(mat):
        low_side = jnp.where(lane == 0, 0.0, pltpu.roll(mat, 1, 1))
        high_side = jnp.where(lane == group - 1, 0.0, pltpu.roll(mat, group - 1, 1))
        return low_side + high_side - 2.0 * mat

    diff_re, diff_im = differences(mat_re), differences(mat_im)
    inner_re = mat_re + coef_re * diff_re - coef_im * diff_im
    inner_im = mat_im + coef_re * diff_im + coef_im * diff_re
    scaled_re = coef_re * mat_re - coef_im * mat_im
    scaled_im = coef_re * mat_im + coef_im * mat_re
    return inner_re, inner_im, scaled_re, scaled_im


def store_left(high_ref, low_ref, index, mat_re, mat_im):
    group = mat_re.shape[-1]
    blocks = ((mat_re, -mat_im), (mat_im, mat_re))
    for i in range(2):
        for j in range(2):
            where = (index, slice(i * group, (i + 1) * group), slice(j * group, (j + 1) * group))
            high_ref[where], low_ref[where] = halves(blocks[i][j])


def left_table_kernel(rhs_ref, inv_ref, couple_ref, high_ref, low_ref, edge_ref):
    levels, _, group, _ = inv_ref.shape
    for level in range(levels):
        inner_re, inner_im, scaled_re, scaled_im = folded(level, inv_ref, rhs_ref)
        store_left(high_ref, low_ref, level, inner_re, inner_im)
        for part, scaled in enumerate((scaled_re, scaled_im)):
            rows = slice(part * group, (part + 1) * group)
            edge_ref[level, 0, rows, :] = jnp.broadcast_to(scaled[:, 0:1], (group, group))
            edge_ref[level, 1, rows, :] = jnp.broadcast_to(scaled[:, group - 1 : group], (group, group))
    store_left(high_ref, low_ref, levels, couple_ref[0], couple_ref[1])


def right_table_kernel(rhs_ref, inv_ref, couple_ref, high_ref, low_ref, edge_ref):
    levels, _, group, _ = inv_ref.shape
    for level in range(levels + 1):
        if level < levels:
            inner_re, inner_im, scaled_re, scaled_im = folded(level, inv_ref, rhs_ref)
            scaled_re, scaled_im = scaled_re.T, scaled_im.T
            for side, row in enumerate((0, group - 1)):
                edge_re, edge_im = scaled_re[row : row + 1], scaled_im[row : row + 1]
                edge_ref[level, 2 * side : 2 * side + 1, :] = jnp.concatenate([edge_re, edge_im], axis=1)
                edge_ref[level, 2 * side + 1 : 2 * side + 2, :] = jnp.concatenate([-edge_im, edge_re], axis=1)
        else:
            inner_re, inner_im = couple_ref[0], couple_ref[1]
        turned_re, turned_im = inner_re.T, inner_im.T
        store_left(high_ref, low_ref, level, turned_re, -turned_im)


def make_tables(kernel, rhs, inv_table, couple_table, edge_shape):
    levels, _, group, _ = inv_table.shape
    shape = whole((levels + 1, 2 * group, 2 * group), bf16)
    return pl.pallas_call(
        kernel,
        out_shape=[shape, shape, whole(edge_shape)],
        in_specs=[smem(), vmem(), vmem()],
        out_specs=[vmem()] * 3,
        compiler_params=params(16),
        cost_estimate=cost(0, 4 * 1024 * 1024),
    )(rhs, inv_table, couple_table)


def line_groups(read, level_of, tables, low, high, following, below, above, write):
    high_ref, low_ref, edge_ref = tables
    last = high_ref.shape[0] - 1
    couple = (high_ref[last], low_ref[last])
    for k in reversed(range(low, high)):
        level = level_of(k)
        value_re, value_im = read(k)
        group = value_re.shape[1]
        solved = product(halves(jnp.concatenate([value_re, value_im], axis=1)), (high_ref[level], low_ref[level]))
        if following is not None:
            solved = solved + product(following, couple)
        before = [item[:, group - 1 : group] for item in read(k - 1)] if k > low else below
        for side, column in ((0, before), (1, above)):
            if column is not None:
                for part in range(2):
                    row = edge_ref[level, 2 * side + part : 2 * side + part + 1, :]
                    solved = solved + column[part] * row
        write(k, solved)
        following = halves(solved)
        above = [value_re[:, 0:1], value_im[:, 0:1]]


def rows_with_halo(field_ref, halo_ref, part, columns, halo_columns):
    row = jnp.broadcast_to(halo_ref[0, part, :, halo_columns], (8, columns.stop - columns.start))
    return jnp.concatenate([field_ref[0, part, :, columns], row], axis=0)


def first_pass_kernel(place_ref, index_ref, field_ref, beside_ref, halo_ref, high_ref, low_ref, edge_ref, *refs,
                      half, group, block):
    if half:
        carry_ref, keep_ref, send_ref, own = None, refs[1], refs[2], refs[3]
        state_ref = refs[0]
    else:
        carry_ref, keep_ref, send_ref, own = refs
        state_ref = None
    width = field_ref.shape[-1]
    count = width // group
    low = half * count
    core = place_ref[0] % 2

    def read(k):
        columns = slice((k - low) * group, (k - low + 1) * group)
        wide = slice(k * group, (k + 1) * group)
        return [rows_with_halo(field_ref, halo_ref, part, columns, wide) for part in range(2)]

    inside = slice(0, group)
    wide = slice((low - 1) * group, low * group) if half else slice(count * group, (count + 1) * group)
    beyond = [rows_with_halo(beside_ref, halo_ref, part, inside, wide) for part in range(2)]
    if half:
        below, above, following = [item[:, group - 1 : group] for item in beyond], None, None
    else:
        below, above, following = None, [item[:, 0:1] for item in beyond], halves(carry_ref[...])

    def write(k, solved):
        start = (k - low) * group
        b, inner = start // block, start % block
        own[b % 2, b // 2, 0, :, inner : inner + group] = solved[:, :group]
        own[b % 2, b // 2, 1, :, inner : inner + group] = solved[:, group:]
        if half and k == low:
            state_ref[...] = solved

    line_groups(
        read, lambda k: index_ref[0, k], (high_ref, low_ref, edge_ref), low, low + count, following, below, above, write
    )
    keep_ref[...] = own[core]
    send_ref[...] = own[1 - core]


def first_pass(place, recv_index, field, halo, tables, half, carry, block, group):
    rows, length = field.shape[2:]
    width = length // 2
    lines = rows + 8
    count = width // group
    shape = (width // (2 * block), 2, lines, block)
    beside = count - 1 if half else count
    args = [place, recv_index, field, field, halo, *tables]
    specs = [
        smem(), smem(),
        pl.BlockSpec((1, 2, rows, width), lambda i: (0, 0, 0, half)),
        pl.BlockSpec((1, 2, rows, group), lambda i: (0, 0, 0, beside)),
    ] + [vmem()] * 4
    outs = [whole(shape)] * 2
    if half:
        outs = [whole((lines, 2 * group))] + outs
    else:
        args.append(carry)
        specs.append(vmem())
    return pl.pallas_call(
        functools.partial(first_pass_kernel, half=half, group=group, block=block),
        grid=(1,),
        out_shape=outs,
        in_specs=specs,
        out_specs=[vmem()] * len(outs),
        scratch_shapes=[pltpu.VMEM((2,) + shape, f32)],
        compiler_params=params(36),
        cost_estimate=cost(lines * width * group * 24, 8 * lines * width * 2),
    )(*args)


def add_edge(solved, edge_ref, level, side, row_re, row_im):
    group = edge_ref.shape[-1]
    wide = row_re.shape[-1]
    column = [edge_ref[level, side, part * group : (part + 1) * group, :] for part in range(2)]
    if wide > group:
        column = [jnp.concatenate([item] * (wide // group), axis=1) for item in column]
    term_re = column[0] * row_re - column[1] * row_im
    term_im = column[0] * row_im + column[1] * row_re
    both = jnp.concatenate([term_re, term_im], axis=0)
    return both if solved is None else solved + both


def second_groups(chip, groups, group, index_ref, tables):
    high_ref, low_ref, edge_ref = tables
    last = high_ref.shape[0] - 1
    couple = (high_ref[last], low_ref[last])
    base = chip * groups
    total = index_ref.shape[1]

    def open_state(row_re, row_im):
        after = base + groups
        level = index_ref[1, jnp.minimum(after, total - 1)]
        inside = jnp.where(after < total, 1.0, 0.0)
        return add_edge(None, edge_ref, level, 0, row_re * inside, row_im * inside)

    def step(k, value, following, before, after):
        level = index_ref[1, base + k]
        solved = product((high_ref[level], low_ref[level]), value)
        solved = solved + product(couple, following)
        if before is not None:
            solved = add_edge(solved, edge_ref, level, 0, *before)
        if after is not None:
            solved = add_edge(solved, edge_ref, level, 1, *after)
        return solved

    return open_state, step


def first_row(value, group):
    return value[0:1], value[group : group + 1]


def last_row(value, group):
    return value[group - 1 : group], value[2 * group - 1 : 2 * group]


def open_sweep_kernel(place_ref, index_ref, high_ref, low_ref, edge_ref, keep_ref, come_ref, state_ref, local_ref, *refs,
                      groups, group):
    base_ref = refs[0] if refs else None
    device = place_ref[0]
    chip, core = device // 2, device % 2
    tables = (high_ref, low_ref, edge_ref)
    last = high_ref.shape[0] - 1
    couple = (high_ref[last], low_ref[last])
    half = groups // 2
    lines = half * group
    width = keep_ref.shape[-1]

    def rows(upper, start, count):
        mine = upper == core
        return [
            jnp.where(mine, keep_ref[0, part, start : start + count, :], come_ref[0, part, start : start + count, :])
            for part in range(2)
        ]

    def given(k):
        return rows(k // half, (k % half) * group, group)

    open_state, step = second_groups(chip, groups, group, index_ref, tables)
    above = [item[0:1] for item in rows(1, lines, 8)]
    solved = following = state = None
    value = given(groups - 1)
    earlier = None
    for k in reversed(range(groups)):
        level = index_ref[0, chip * groups + k]
        below_value = given(k - 1) if k else None
        before = [item[group - 1 : group] for item in below_value] if k else [item[0:1] for item in rows(0, lines, 8)]
        now = product((high_ref[level], low_ref[level]), halves(jnp.concatenate(value, axis=0)))
        if following is not None:
            now = now + product(couple, following)
        now = add_edge(now, edge_ref, level, 0, *before)
        now = add_edge(now, edge_ref, level, 1, *above)
        above = [item[0:1] for item in value]
        value = below_value
        if base_ref is not None:
            base_ref[k] = now[:group]
        if k == groups - 1:
            row_re, row_im = last_row(now, group)
            for part, row in enumerate((row_re, row_im)):
                state_ref[4 * group + 8 * part : 4 * group + 8 * part + 8, :] = jnp.broadcast_to(row, (8, width))
            state = halves(open_state(row_re, row_im))
        else:
            done = step(k + 1, following, state, last_row(now, group), first_row(earlier, group) if earlier is not None else None)
            local_ref[k + 1] = done
            state = halves(done)
        earlier = solved
        solved = now
        following = halves(now)
    done = step(0, following, state, None, first_row(earlier, group))
    local_ref[0] = done
    state_ref[0 : 2 * group, :] = solved
    state_ref[2 * group : 4 * group, :] = done


def map_kernel(place_ref, index_ref, high_ref, low_ref, edge_ref, power_high, power_low, map_high, map_low,
               chip_high, chip_low, *, groups, group):
    tables = (high_ref, low_ref, edge_ref)
    last = high_ref.shape[0] - 1
    couple = (high_ref[last], low_ref[last])
    rows = lax.broadcasted_iota(jnp.int32, (2 * group, group), 0)
    columns = lax.broadcasted_iota(jnp.int32, (2 * group, group), 1)
    unit = (rows == columns).astype(f32)
    values = [None] * groups + [unit]
    split = [None] * groups
    for k in reversed(range(groups)):
        values[k] = product(couple, halves(values[k + 1]))
        split[k] = halves(values[k])
        store_left(power_high, power_low, k, values[k][:group], values[k][group:])
    for q in range(chip_high.shape[0] + 1):
        mine = q == chip_high.shape[0]
        chip = place_ref[0] // 2 if mine else q + 1
        open_state, step = second_groups(chip, groups, group, index_ref, tables)
        state = halves(open_state(*last_row(values[groups - 1], group)))
        for k in reversed(range(groups)):
            before = last_row(values[k - 1], group) if k else None
            done = step(k, split[k], state, before, first_row(values[k + 1], group))
            state = halves(done)
            if mine:
                store_left(map_high, map_low, k, done[:group], done[group:])
            elif k == 0:
                store_left(chip_high, chip_low, q, done[:group], done[group:])


def scan_kernel(place_ref, high_ref, low_ref, power_high, power_low, chip_high, chip_low, *refs, chips, group):
    pieces, outs, held, rows = refs[:chips], refs[chips : 2 * chips], refs[2 * chips], refs[2 * chips + 1]
    chip = place_ref[0] // 2
    last = high_ref.shape[0] - 1
    size = 4 * group
    for offset in range(chips):
        held[chip ^ offset] = pieces[offset][...]
    keep = (power_high[0], power_low[0])
    rows[0] = jnp.zeros_like(rows[0])
    for q in range(chips - 1, 0, -1):
        first = halves(held[q, 0 : 2 * group, :])
        for part in range(2):
            tail = slice((part + 1) * group - 16, (part + 1) * group)
            row = product((high_ref[last, tail, :], low_ref[last, tail, :]), first)[15:16]
            base = size + 8 * part
            rows[q, 8 * part : 8 * part + 8, :] = held[q - 1, base : base + 8, :] + row
        if q > 1:
            second = halves(held[q, 2 * group : size, :])
            held[q - 1, 0 : 2 * group, :] = held[q - 1, 0 : 2 * group, :] + product(keep, first)
            held[q - 1, 2 * group : size, :] = (
                held[q - 1, 2 * group : size, :]
                + product((chip_high[q - 2], chip_low[q - 2]), first)
                + product(keep, second)
            )
    held[0] = jnp.zeros_like(held[0])
    for offset in range(chips):
        target = chip ^ offset
        outs[offset][0:size, :] = held[(target + 1) % chips, 0:size, :]
        outs[offset][size : size + 16, :] = rows[target]


def close_sweep_kernel(place_ref, index_ref, edge_ref, power_high, power_low, map_high, map_low, local_ref, carry_ref, *refs,
                       groups, group):
    base_ref = refs[0] if len(refs) == 5 else None
    own_ref, other_ref = refs[-4:-2] if base_ref is not None else refs[0:2]
    image_ref = refs[-2] if base_ref is not None else None
    result = refs[-1]
    device = place_ref[0]
    chip, core = device // 2, device % 2
    first = halves(carry_ref[0 : 2 * group, :])
    second = halves(carry_ref[2 * group : 4 * group, :])
    half = groups // 2
    for k in reversed(range(groups)):
        done = local_ref[k] + (
            product((map_high[k], map_low[k]), first) + product((power_high[k], power_low[k]), second)
        )
        if k == 0:
            level = index_ref[1, chip * groups]
            base = 4 * group
            done = add_edge(done, edge_ref, level, 0, carry_ref[base : base + 1, :], carry_ref[base + 8 : base + 9, :])
        rows = slice((k % half) * group, (k % half + 1) * group)
        result[k // half, 0, rows, :] = done[:group]
        result[k // half, 1, rows, :] = done[group:]
    own_ref[...] = result[core]
    other_ref[...] = result[1 - core]
    if image_ref is not None:
        for i in range(half):
            k = core * half + i
            columns = slice(i * group, (i + 1) * group)
            square = base_ref[k, :, columns] + product(
                (power_high[k, 0:group, :], power_low[k, 0:group, :]), [item[:, columns] for item in first]
            )
            image_ref[:, columns] = diagonal_of(square)


def diagonal_of(square):
    rows = lax.broadcasted_iota(jnp.int32, square.shape, 0)
    columns = lax.broadcasted_iota(jnp.int32, square.shape, 1)
    return jnp.sum(jnp.where(rows == columns, square, 0.0), axis=0, keepdims=True)


def last_pass_kernel(place_ref, index_ref, high_ref, low_ref, edge_ref, *refs, step, group, chips):
    owns, comes = refs[:chips], refs[chips : 2 * chips]
    out_ref, image_ref, field = refs[2 * chips :]
    device = place_ref[0]
    chip, core = device // 2, device % 2
    block = owns[0].shape[-1]
    length = field.shape[-1]
    for offset in range(chips):
        for ref, side in ((owns[offset], core), (comes[offset], 1 - core)):
            start = pl.multiple_of(((chip ^ offset) * 2 + side) * block, block)
            for part in range(2):
                field[part, :, pl.ds(start, block)] = ref[part]

    def read(k):
        return [field[part, :, k * group : (k + 1) * group] for part in range(2)]

    def write(k, solved):
        out_ref[0, 0, :, k * group : (k + 1) * group] = solved[:, :group]
        out_ref[0, 1, :, k * group : (k + 1) * group] = solved[:, group:]

    line_groups(
        read, lambda k: index_ref[step, k], (high_ref, low_ref, edge_ref), 0, length // group, None, None, None, write
    )
    image_ref[...] = diagonal_of(out_ref[0, 0, :, pl.ds(pl.multiple_of(device * block, block), block)])


def sum_over(value, axis, count):
    reach = 1
    while reach < count:
        value = value + lax.ppermute(value, axis, [(i, i ^ reach) for i in range(count)])
        reach *= 2
    return value


def fast_shards(wavefield, inv_table, couple_table, rhs_table, recv_index, shot_index, *, devices, freqs):
    levels, _, group, _ = inv_table.shape[1:]
    rows, length = wavefield.shape[2:]
    block = rows
    chips = devices // 2
    groups = 2 * rows // group
    device = lax.axis_index("plane")
    place = device.reshape(1).astype(jnp.int32)
    rhs = rhs_table[0]
    double = 2 * group

    edge = lax.dynamic_slice_in_dim(wavefield, (device % 2) * (rows - 1), 1, axis=2)
    swap = [(d, d + 1) for d in range(1, devices - 1, 2)] + [(d + 1, d) for d in range(1, devices - 1, 2)]
    halo = lax.ppermute(edge, "plane", swap)
    right = make_tables(right_table_kernel, rhs, inv_table[0], couple_table[0], (levels, 4, double))

    partner = [(d, d ^ 1) for d in range(devices)]
    carry, keep_b, send_b = first_pass(place, recv_index, wavefield, halo, right, 1, None, block, group)
    come_b = lax.ppermute(send_b, "plane", partner)
    keep_a, send_a = first_pass(place, recv_index, wavefield, halo, right, 0, carry, block, group)
    come_a = lax.ppermute(send_a, "plane", partner)
    left = make_tables(left_table_kernel, rhs, inv_table[0], couple_table[0], (levels, 2, double, group))
    keep = jnp.concatenate([keep_a, keep_b], axis=0)
    come = jnp.concatenate([come_a, come_b], axis=0)

    piece = whole((4 * group + 16, block))
    local = whole((groups, double, block))
    offsets = [3, 1, 2, 0]
    locals_, theirs, base = {}, {}, None
    for offset in offsets:
        spec = pltpu.PrefetchScalarGridSpec(
            num_scalar_prefetch=2,
            grid=(1,),
            in_specs=[vmem()] * 3
            + [pl.BlockSpec((1,) + keep.shape[1:], lambda i, at, _, o=offset: ((at[0] // 2) ^ o, 0, 0, 0))] * 2,
            out_specs=[vmem()] * (2 if offset else 3),
        )
        result = pl.pallas_call(
            functools.partial(open_sweep_kernel, groups=groups, group=group),
            grid_spec=spec,
            out_shape=[piece, local] + ([] if offset else [whole((groups, group, block))]),
            compiler_params=params(24),
            cost_estimate=cost(groups * group * block * group * 48, 8 * groups * group * block * 3),
        )(place, shot_index, *left, keep, come)
        locals_[offset] = result[1]
        if offset:
            theirs[offset] = lax.ppermute(result[0], "plane", [(d, d ^ (2 * offset)) for d in range(devices)])
        else:
            theirs[0], base = result[0], result[2]

    matrices = whole((groups, double, double), bf16)
    middle = whole((chips - 2, double, double), bf16)
    power_high, power_low, map_high, map_low, chip_high, chip_low = pl.pallas_call(
        functools.partial(map_kernel, groups=groups, group=group),
        out_shape=[matrices] * 4 + [middle] * 2,
        in_specs=[smem()] * 2 + [vmem()] * 3,
        out_specs=[vmem()] * 6,
        compiler_params=params(20),
        cost_estimate=cost(groups * group * group * group * 96, 4 * 1024 * 1024),
    )(place, shot_index, *left)

    carries = pl.pallas_call(
        functools.partial(scan_kernel, chips=chips, group=group),
        out_shape=[piece] * chips,
        in_specs=[smem()] + [vmem()] * (6 + chips),
        out_specs=[vmem()] * chips,
        scratch_shapes=[pltpu.VMEM((chips,) + piece.shape, f32), pltpu.VMEM((chips, 16, block), f32)],
        compiler_params=params(20),
        cost_estimate=cost(3 * group * group * block * 24, 4 * 1024 * 1024),
    )(place, left[0], left[1], power_high, power_low, chip_high, chip_low, *[theirs[o] for o in range(chips)])

    came = {
        offset: lax.ppermute(carries[offset], "plane", [(d, d ^ (2 * offset)) for d in range(devices)])
        for offset in offsets if offset
    }
    came[0] = carries[0]
    owns, comes = {}, {}
    part = whole((2, rows, block))
    for offset in range(chips):
        extra = [] if offset else [base]
        outs = [part, part] + ([] if offset else [whole((1, block))])
        result = pl.pallas_call(
            functools.partial(close_sweep_kernel, groups=groups, group=group),
            out_shape=outs,
            in_specs=[smem()] * 2 + [vmem()] * (7 + len(extra)),
            out_specs=[vmem()] * len(outs),
            scratch_shapes=[pltpu.VMEM((2, 2, rows, block), f32)],
            compiler_params=params(20),
            cost_estimate=cost(groups * group * block * group * 24, 8 * groups * group * block * 2),
        )(place, shot_index, left[2], power_high, power_low, map_high, map_low, locals_[offset], came[offset], *extra)
        owns[offset] = result[0]
        comes[offset] = lax.ppermute(result[1], "plane", partner)
        if offset == 0:
            image_first = sum_over(result[2], "freq", freqs)

    migrated, image_last = pl.pallas_call(
        functools.partial(last_pass_kernel, step=1, group=group, chips=chips),
        out_shape=[whole(wavefield.shape), whole((1, block))],
        in_specs=[smem(), smem()] + [vmem()] * (3 + 2 * chips),
        out_specs=[vmem()] * 2,
        scratch_shapes=[pltpu.VMEM((2, rows, length), f32)],
        compiler_params=params(32),
        cost_estimate=cost(rows * length * group * 24, 8 * rows * length * 2),
    )(place, recv_index, *right, *[owns[o] for o in range(chips)], *[comes[o] for o in range(chips)])
    image_last = sum_over(image_last, "freq", freqs)
    return migrated, jnp.concatenate([image_first, image_last], axis=0)


def solution(mesh):
    placed = (
        P("freq", None, "plane", None),
        P("freq", None, None, None, None),
        P("freq", None, None, None),
        P("freq", None, None),
        P(),
        P(),
    )
    devices = mesh.shape["plane"]
    freqs = mesh.shape["freq"]

    def body(*arrays):
        if devices == 8 and arrays[0].shape[2] == 2 * GROUP and arrays[0].shape[0] == 1 and freqs & (freqs - 1) == 0:
            return fast_shards(*arrays, devices=devices, freqs=freqs)
        return shards(*arrays)

    return jax.shard_map(
        body,
        mesh=mesh,
        in_specs=placed,
        out_specs=(P("freq", None, "plane", None), P(None, "plane")),
        check_vma=False,
    )
```

```python
import functools

import jax
import jax.numpy as jnp
from jax import lax
from jax.experimental import pallas as pl
from jax.experimental.pallas import tpu as pltpu
from jax.sharding import PartitionSpec as P

NX = 2048
GROUP = 128
DEPTHS = 2


highest = lax.Precision.HIGHEST


def complex_product(form, mat_re, mat_im, vec_re, vec_im):
    real_part = jnp.einsum(form, mat_re, vec_re, precision=highest) - jnp.einsum(
        form, mat_im, vec_im, precision=highest
    )
    imag_part = jnp.einsum(form, mat_re, vec_im, precision=highest) + jnp.einsum(
        form, mat_im, vec_re, precision=highest
    )
    return (real_part, imag_part)


def select_rows(index, table):
    levels = jnp.arange(table.shape[1], dtype=jnp.int32)
    one_hot = (index[:, None] == levels[None, :]).astype(jnp.float32)
    return jnp.einsum("kv,fv...->fk...", one_hot, table, precision=highest)


def coupling_powers(couple_table, group_count):
    power_re = couple_table[:, 0]
    power_im = couple_table[:, 1]
    powers = []
    reach = 1
    while reach < group_count:
        powers.append((power_re, power_im))
        power_re, power_im = complex_product("fab,fbc->fac", power_re, power_im, power_re, power_im)
        reach = reach * 2
    return powers


def shifted_up(values, reach, group_axis):
    count = values.shape[group_axis]
    kept = lax.slice_in_dim(values, reach, count, axis=group_axis)
    zero_shape = list(values.shape)
    zero_shape[group_axis] = reach
    return jnp.concatenate([kept, jnp.zeros(zero_shape, values.dtype)], axis=group_axis)


def line_pass(wave_field, index, inv_table, rhs_table, powers, along_last):
    line_axis = 3 if along_last else 2
    freqs = wave_field.shape[0]
    length = wave_field.shape[line_axis]
    group_count = length // GROUP
    inv_sel = select_rows(index, inv_table)
    rhs_sel = select_rows(index, rhs_table)
    pad_widths = [(0, 0), (0, 0), (0, 0), (0, 0)]
    pad_widths[line_axis] = (1, 1)
    padded = jnp.pad(wave_field, pad_widths)
    beside = lax.slice_in_dim(padded, 0, length, axis=line_axis) + lax.slice_in_dim(
        padded, 2, length + 2, axis=line_axis
    )
    second = beside - 2.0 * wave_field
    if along_last:
        shape = (freqs, wave_field.shape[2], group_count, GROUP)
        coef_re = rhs_sel[:, None, :, 0, None]
        coef_im = rhs_sel[:, None, :, 1, None]
        local_form = "fkab,flkb->flka"
        power_form = "fab,flkb->flka"
        group_axis = 2
    else:
        shape = (freqs, group_count, GROUP, wave_field.shape[3])
        coef_re = rhs_sel[:, :, 0, None, None]
        coef_im = rhs_sel[:, :, 1, None, None]
        local_form = "fkab,fkbm->fkam"
        power_form = "fab,fkbm->fkam"
        group_axis = 1
    base_re = wave_field[:, 0].reshape(shape)
    base_im = wave_field[:, 1].reshape(shape)
    second_re = second[:, 0].reshape(shape)
    second_im = second[:, 1].reshape(shape)
    source_re = base_re + coef_re * second_re - coef_im * second_im
    source_im = base_im + coef_re * second_im + coef_im * second_re
    solved_re, solved_im = complex_product(
        local_form, inv_sel[:, :, 0], inv_sel[:, :, 1], source_re, source_im
    )
    reach = 1
    for power_re, power_im in powers:
        add_re, add_im = complex_product(
            power_form,
            power_re,
            power_im,
            shifted_up(solved_re, reach, group_axis),
            shifted_up(solved_im, reach, group_axis),
        )
        solved_re = solved_re + add_re
        solved_im = solved_im + add_im
        reach = reach * 2
    out_shape = (freqs,) + wave_field.shape[2:]
    return jnp.stack([solved_re.reshape(out_shape), solved_im.reshape(out_shape)], axis=1)


def to_columns(wave_field):
    return lax.all_to_all(wave_field, "plane", split_axis=3, concat_axis=2, tiled=True)


def to_rows(wave_field):
    return lax.all_to_all(wave_field, "plane", split_axis=2, concat_axis=3, tiled=True)


def diagonal_rows(wave_field, first_row):
    count = wave_field.shape[2]
    block = lax.dynamic_slice_in_dim(wave_field[:, 0], first_row, count, axis=2)
    return jnp.sum(jnp.diagonal(block, axis1=1, axis2=2), axis=0)


def diagonal_columns(wave_field, first_row):
    count = wave_field.shape[3]
    block = lax.dynamic_slice_in_dim(wave_field[:, 0], first_row, count, axis=1)
    return jnp.sum(jnp.diagonal(block, axis1=1, axis2=2), axis=0)


def image_part(partial_value):
    return lax.psum(partial_value, "freq")


def shards(wavefield, inv_table, couple_table, rhs_table, recv_index, shot_index):
    powers = coupling_powers(couple_table, NX // GROUP)
    row_count = wavefield.shape[2]
    first_row = lax.axis_index("plane") * row_count
    wave_field = wavefield
    parts = []
    for step_index in range(DEPTHS):
        if step_index % 2 == 0:
            wave_field = line_pass(
                wave_field, recv_index[step_index], inv_table, rhs_table, powers, True
            )
            wave_field = to_columns(wave_field)
            wave_field = line_pass(
                wave_field, shot_index[step_index], inv_table, rhs_table, powers, False
            )
            parts.append(image_part(diagonal_columns(wave_field, first_row)))
        else:
            wave_field = line_pass(
                wave_field, shot_index[step_index], inv_table, rhs_table, powers, False
            )
            wave_field = to_rows(wave_field)
            wave_field = line_pass(
                wave_field, recv_index[step_index], inv_table, rhs_table, powers, True
            )
            parts.append(image_part(diagonal_rows(wave_field, first_row)))
    stacked = jnp.stack(parts)
    return (wave_field, stacked)


f32 = jnp.float32
bf16 = jnp.bfloat16


def halves(value):
    high = value.astype(bf16)
    low = (value - high.astype(f32)).astype(bf16)
    return high, low


def mul(left, right):
    return jnp.dot(left, right, preferred_element_type=f32)


def product(left, right):
    (left_high, left_low), (right_high, right_low) = left, right
    return mul(left_high, right_high) + mul(left_low, right_high) + mul(left_high, right_low)


def params(mebibytes):
    return pltpu.CompilerParams(vmem_limit_bytes=mebibytes * 1024 * 1024)


def whole(shape, dtype=f32):
    return jax.ShapeDtypeStruct(shape, dtype)


def smem():
    return pl.BlockSpec(memory_space=pltpu.SMEM)


def vmem():
    return pl.BlockSpec(memory_space=pltpu.VMEM)


def cost(macs, size):
    return pl.CostEstimate(flops=2 * macs, bytes_accessed=size, transcendentals=0)


def folded(level, inv_ref, rhs_ref):
    mat_re, mat_im = inv_ref[level, 0], inv_ref[level, 1]
    coef_re, coef_im = rhs_ref[level, 0], rhs_ref[level, 1]
    group = mat_re.shape[-1]
    lane = lax.broadcasted_iota(jnp.int32, mat_re.shape, 1)

    def differences(mat):
        low_side = jnp.where(lane == 0, 0.0, pltpu.roll(mat, 1, 1))
        high_side = jnp.where(lane == group - 1, 0.0, pltpu.roll(mat, group - 1, 1))
        return low_side + high_side - 2.0 * mat

    diff_re, diff_im = differences(mat_re), differences(mat_im)
    inner_re = mat_re + coef_re * diff_re - coef_im * diff_im
    inner_im = mat_im + coef_re * diff_im + coef_im * diff_re
    scaled_re = coef_re * mat_re - coef_im * mat_im
    scaled_im = coef_re * mat_im + coef_im * mat_re
    return inner_re, inner_im, scaled_re, scaled_im


def store_left(high_ref, low_ref, index, mat_re, mat_im):
    group = mat_re.shape[-1]
    blocks = ((mat_re, -mat_im), (mat_im, mat_re))
    for i in range(2):
        for j in range(2):
            where = (index, slice(i * group, (i + 1) * group), slice(j * group, (j + 1) * group))
            high_ref[where], low_ref[where] = halves(blocks[i][j])


def left_table_kernel(rhs_ref, inv_ref, couple_ref, high_ref, low_ref, edge_ref):
    levels, _, group, _ = inv_ref.shape
    for level in range(levels):
        inner_re, inner_im, scaled_re, scaled_im = folded(level, inv_ref, rhs_ref)
        store_left(high_ref, low_ref, level, inner_re, inner_im)
        for part, scaled in enumerate((scaled_re, scaled_im)):
            rows = slice(part * group, (part + 1) * group)
            edge_ref[level, 0, rows, :] = jnp.broadcast_to(scaled[:, 0:1], (group, group))
            edge_ref[level, 1, rows, :] = jnp.broadcast_to(scaled[:, group - 1 : group], (group, group))
    store_left(high_ref, low_ref, levels, couple_ref[0], couple_ref[1])


def right_table_kernel(rhs_ref, inv_ref, couple_ref, high_ref, low_ref, edge_ref):
    levels, _, group, _ = inv_ref.shape
    for level in range(levels + 1):
        if level < levels:
            inner_re, inner_im, scaled_re, scaled_im = folded(level, inv_ref, rhs_ref)
            scaled_re, scaled_im = scaled_re.T, scaled_im.T
            for side, row in enumerate((0, group - 1)):
                edge_re, edge_im = scaled_re[row : row + 1], scaled_im[row : row + 1]
                edge_ref[level, 2 * side : 2 * side + 1, :] = jnp.concatenate([edge_re, edge_im], axis=1)
                edge_ref[level, 2 * side + 1 : 2 * side + 2, :] = jnp.concatenate([-edge_im, edge_re], axis=1)
        else:
            inner_re, inner_im = couple_ref[0], couple_ref[1]
        turned_re, turned_im = inner_re.T, inner_im.T
        store_left(high_ref, low_ref, level, turned_re, -turned_im)


def make_tables(kernel, rhs, inv_table, couple_table, edge_shape):
    levels, _, group, _ = inv_table.shape
    shape = whole((levels + 1, 2 * group, 2 * group), bf16)
    return pl.pallas_call(
        kernel,
        out_shape=[shape, shape, whole(edge_shape)],
        in_specs=[smem(), vmem(), vmem()],
        out_specs=[vmem()] * 3,
        compiler_params=params(16),
        cost_estimate=cost(0, 4 * 1024 * 1024),
    )(rhs, inv_table, couple_table)


def line_groups(read, level_of, tables, low, high, following, below, above, write):
    high_ref, low_ref, edge_ref = tables
    last = high_ref.shape[0] - 1
    couple = (high_ref[last], low_ref[last])
    for k in reversed(range(low, high)):
        level = level_of(k)
        value_re, value_im = read(k)
        group = value_re.shape[1]
        solved = product(halves(jnp.concatenate([value_re, value_im], axis=1)), (high_ref[level], low_ref[level]))
        if following is not None:
            solved = solved + product(following, couple)
        before = [item[:, group - 1 : group] for item in read(k - 1)] if k > low else below
        for side, column in ((0, before), (1, above)):
            if column is not None:
                for part in range(2):
                    row = edge_ref[level, 2 * side + part : 2 * side + part + 1, :]
                    solved = solved + column[part] * row
        write(k, solved)
        following = halves(solved)
        above = [value_re[:, 0:1], value_im[:, 0:1]]


def rows_with_halo(field_ref, halo_ref, part, columns, halo_columns):
    row = jnp.broadcast_to(halo_ref[0, part, :, halo_columns], (8, columns.stop - columns.start))
    return jnp.concatenate([field_ref[0, part, :, columns], row], axis=0)


def first_pass_kernel(place_ref, index_ref, field_ref, beside_ref, halo_ref, high_ref, low_ref, edge_ref, *refs,
                      half, group, block):
    if half:
        carry_ref, keep_ref, send_ref, own = None, refs[1], refs[2], refs[3]
        state_ref = refs[0]
    else:
        carry_ref, keep_ref, send_ref, own = refs
        state_ref = None
    width = field_ref.shape[-1]
    count = width // group
    low = half * count
    core = place_ref[0] % 2

    def read(k):
        columns = slice((k - low) * group, (k - low + 1) * group)
        wide = slice(k * group, (k + 1) * group)
        return [rows_with_halo(field_ref, halo_ref, part, columns, wide) for part in range(2)]

    inside = slice(0, group)
    wide = slice((low - 1) * group, low * group) if half else slice(count * group, (count + 1) * group)
    beyond = [rows_with_halo(beside_ref, halo_ref, part, inside, wide) for part in range(2)]
    if half:
        below, above, following = [item[:, group - 1 : group] for item in beyond], None, None
    else:
        below, above, following = None, [item[:, 0:1] for item in beyond], halves(carry_ref[...])

    def write(k, solved):
        start = (k - low) * group
        b, inner = start // block, start % block
        own[b % 2, b // 2, 0, :, inner : inner + group] = solved[:, :group]
        own[b % 2, b // 2, 1, :, inner : inner + group] = solved[:, group:]
        if half and k == low:
            state_ref[...] = solved

    line_groups(
        read, lambda k: index_ref[0, k], (high_ref, low_ref, edge_ref), low, low + count, following, below, above, write
    )
    keep_ref[...] = own[core]
    send_ref[...] = own[1 - core]


def first_pass(place, recv_index, field, halo, tables, half, carry, block, group):
    rows, length = field.shape[2:]
    width = length // 2
    lines = rows + 8
    count = width // group
    shape = (width // (2 * block), 2, lines, block)
    beside = count - 1 if half else count
    args = [place, recv_index, field, field, halo, *tables]
    specs = [
        smem(), smem(),
        pl.BlockSpec((1, 2, rows, width), lambda i: (0, 0, 0, half)),
        pl.BlockSpec((1, 2, rows, group), lambda i: (0, 0, 0, beside)),
    ] + [vmem()] * 4
    outs = [whole(shape)] * 2
    if half:
        outs = [whole((lines, 2 * group))] + outs
    else:
        args.append(carry)
        specs.append(vmem())
    return pl.pallas_call(
        functools.partial(first_pass_kernel, half=half, group=group, block=block),
        grid=(1,),
        out_shape=outs,
        in_specs=specs,
        out_specs=[vmem()] * len(outs),
        scratch_shapes=[pltpu.VMEM((2,) + shape, f32)],
        compiler_params=params(36),
        cost_estimate=cost(lines * width * group * 24, 8 * lines * width * 2),
    )(*args)


def add_edge(solved, edge_ref, level, side, row_re, row_im):
    group = edge_ref.shape[-1]
    wide = row_re.shape[-1]
    column = [edge_ref[level, side, part * group : (part + 1) * group, :] for part in range(2)]
    if wide > group:
        column = [jnp.concatenate([item] * (wide // group), axis=1) for item in column]
    term_re = column[0] * row_re - column[1] * row_im
    term_im = column[0] * row_im + column[1] * row_re
    both = jnp.concatenate([term_re, term_im], axis=0)
    return both if solved is None else solved + both


def second_groups(chip, groups, group, index_ref, tables):
    high_ref, low_ref, edge_ref = tables
    last = high_ref.shape[0] - 1
    couple = (high_ref[last], low_ref[last])
    base = chip * groups
    total = index_ref.shape[1]

    def open_state(row_re, row_im):
        after = base + groups
        level = index_ref[1, jnp.minimum(after, total - 1)]
        inside = jnp.where(after < total, 1.0, 0.0)
        return add_edge(None, edge_ref, level, 0, row_re * inside, row_im * inside)

    def step(k, value, following, before, after):
        level = index_ref[1, base + k]
        solved = product((high_ref[level], low_ref[level]), value)
        solved = solved + product(couple, following)
        if before is not None:
            solved = add_edge(solved, edge_ref, level, 0, *before)
        if after is not None:
            solved = add_edge(solved, edge_ref, level, 1, *after)
        return solved

    return open_state, step


def first_row(value, group):
    return value[0:1], value[group : group + 1]


def last_row(value, group):
    return value[group - 1 : group], value[2 * group - 1 : 2 * group]


def open_sweep_kernel(place_ref, index_ref, high_ref, low_ref, edge_ref, keep_ref, come_ref, near_ref, far_ref, local_ref,
                      base_ref, pair, *, groups, group):
    device = place_ref[0]
    chip, core = device // 2, device % 2
    tables = (high_ref, low_ref, edge_ref)
    last = high_ref.shape[0] - 1
    couple = (high_ref[last], low_ref[last])
    half = groups // 2
    lines = half * group
    width = keep_ref.shape[-1]

    def rows(upper, start, count):
        mine = upper == core
        return [
            jnp.where(mine, keep_ref[0, part, start : start + count, :], come_ref[0, part, start : start + count, :])
            for part in range(2)
        ]

    def store_pair(where, value):
        for sub in range(2):
            pair[sub, where, :] = value[:, sub * (width // 2) : (sub + 1) * (width // 2)]

    def given(k):
        return rows(k // half, (k % half) * group, group)

    open_state, step = second_groups(chip, groups, group, index_ref, tables)
    above = [item[0:1] for item in rows(1, lines, 8)]
    solved = following = state = None
    value = given(groups - 1)
    earlier = None
    for k in reversed(range(groups)):
        level = index_ref[0, chip * groups + k]
        below_value = given(k - 1) if k else None
        before = [item[group - 1 : group] for item in below_value] if k else [item[0:1] for item in rows(0, lines, 8)]
        now = product((high_ref[level], low_ref[level]), halves(jnp.concatenate(value, axis=0)))
        if following is not None:
            now = now + product(couple, following)
        now = add_edge(now, edge_ref, level, 0, *before)
        now = add_edge(now, edge_ref, level, 1, *above)
        above = [item[0:1] for item in value]
        value = below_value

        @pl.when(core == k // half)
        def _(now=now, columns=slice((k % half) * group, (k % half + 1) * group)):
            base_ref[k % half] = now[:group, columns]

        if k == groups - 1:
            row_re, row_im = last_row(now, group)
            for part, row in enumerate((row_re, row_im)):
                store_pair(slice(4 * group + 8 * part, 4 * group + 8 * part + 8), jnp.broadcast_to(row, (8, width)))
            state = halves(open_state(row_re, row_im))
        else:
            done = step(k + 1, following, state, last_row(now, group), first_row(earlier, group) if earlier is not None else None)
            local_ref[k + 1] = done
            state = halves(done)
        earlier = solved
        solved = now
        following = halves(now)
    done = step(0, following, state, None, first_row(earlier, group))
    local_ref[0] = done
    store_pair(slice(0, 2 * group), solved)
    store_pair(slice(2 * group, 4 * group), done)
    near_ref[...] = pair[chip % 2]
    far_ref[...] = pair[1 - chip % 2]


def map_kernel(place_ref, index_ref, high_ref, low_ref, edge_ref, power_high, power_low, map_high, map_low,
               chip_high, chip_low, *, groups, group):
    tables = (high_ref, low_ref, edge_ref)
    last = high_ref.shape[0] - 1
    couple = (high_ref[last], low_ref[last])
    rows = lax.broadcasted_iota(jnp.int32, (2 * group, group), 0)
    columns = lax.broadcasted_iota(jnp.int32, (2 * group, group), 1)
    unit = (rows == columns).astype(f32)
    values = [None] * groups + [unit]
    split = [None] * groups
    for k in reversed(range(groups)):
        values[k] = product(couple, halves(values[k + 1]))
        split[k] = halves(values[k])
        store_left(power_high, power_low, k, values[k][:group], values[k][group:])
    for q in range(chip_high.shape[0] + 1):
        mine = q == chip_high.shape[0]
        chip = place_ref[0] // 2 if mine else q + 1
        open_state, step = second_groups(chip, groups, group, index_ref, tables)
        state = halves(open_state(*last_row(values[groups - 1], group)))
        for k in reversed(range(groups)):
            before = last_row(values[k - 1], group) if k else None
            done = step(k, split[k], state, before, first_row(values[k + 1], group))
            state = halves(done)
            if mine:
                store_left(map_high, map_low, k, done[:group], done[group:])
            elif k == 0:
                store_left(chip_high, chip_low, q, done[:group], done[group:])


def scan_kernel(place_ref, high_ref, low_ref, power_high, power_low, chip_high, chip_low, *refs, chips, group):
    pieces, outs, held, rows = refs[:chips], refs[chips : 2 * chips], refs[2 * chips], refs[2 * chips + 1]
    chip = place_ref[0] // 2
    last = high_ref.shape[0] - 1
    size = 4 * group
    for offset in range(chips):
        held[chip ^ offset] = pieces[offset][...]
    keep = (power_high[0], power_low[0])
    rows[0] = jnp.zeros_like(rows[0])
    for q in range(chips - 1, 0, -1):
        first = halves(held[q, 0 : 2 * group, :])
        for part in range(2):
            tail = slice((part + 1) * group - 16, (part + 1) * group)
            row = product((high_ref[last, tail, :], low_ref[last, tail, :]), first)[15:16]
            base = size + 8 * part
            rows[q, 8 * part : 8 * part + 8, :] = held[q - 1, base : base + 8, :] + row
        if q > 1:
            second = halves(held[q, 2 * group : size, :])
            held[q - 1, 0 : 2 * group, :] = held[q - 1, 0 : 2 * group, :] + product(keep, first)
            held[q - 1, 2 * group : size, :] = (
                held[q - 1, 2 * group : size, :]
                + product((chip_high[q - 2], chip_low[q - 2]), first)
                + product(keep, second)
            )
    held[0] = jnp.zeros_like(held[0])
    for offset in range(chips):
        target = chip ^ offset
        outs[offset][0:size, :] = held[(target + 1) % chips, 0:size, :]
        outs[offset][size : size + 16, :] = rows[target]


def close_sweep_kernel(place_ref, index_ref, edge_ref, power_high, power_low, map_high, map_low, local_ref, base_ref,
                       near_ref, far_ref, own_ref, other_ref, image_ref, pair, result, *, groups, group, part_of, second_pair):
    device = place_ref[0]
    chip, core = device // 2, device % 2
    pair[chip % 2] = near_ref[...]
    pair[1 - chip % 2] = far_ref[...]

    def carried(start, count):
        return jnp.concatenate([pair[0, start : start + count, :], pair[1, start : start + count, :]], axis=1)

    first = halves(carried(0, 2 * group))
    second = halves(carried(2 * group, 2 * group))
    half = groups // 2
    for k in reversed(range(groups)):
        done = local_ref[k] + (
            product((map_high[k], map_low[k]), first) + product((power_high[k], power_low[k]), second)
        )
        if k == 0:
            level = index_ref[1, chip * groups]
            base = 4 * group
            done = add_edge(done, edge_ref, level, 0, carried(base, 8)[0:1], carried(base + 8, 8)[0:1])
        rows = slice((k % half) * group, (k % half + 1) * group)
        result[k // half, 0, rows, :] = done[:group]
        result[k // half, 1, rows, :] = done[group:]
    own_ref[...] = result[core]
    other_ref[...] = result[1 - core]
    image_ref[...] = jnp.zeros_like(image_ref)

    @pl.when((chip // 2 == part_of) & ((chip % 2) ^ (chip // 2) == second_pair))
    def _():
        for i in range(half):
            k = core * half + i
            columns = slice(i * group, (i + 1) * group)
            square = base_ref[i] + product(
                (power_high[k, 0:group, :], power_low[k, 0:group, :]), [item[:, columns] for item in first]
            )
            image_ref[:, columns] = diagonal_of(square)


def diagonal_of(square):
    rows = lax.broadcasted_iota(jnp.int32, square.shape, 0)
    columns = lax.broadcasted_iota(jnp.int32, square.shape, 1)
    return jnp.sum(jnp.where(rows == columns, square, 0.0), axis=0, keepdims=True)


def last_pass_kernel(place_ref, index_ref, high_ref, low_ref, edge_ref, *refs, half, step, group):
    owns, comes = refs[0:2], refs[2:4]
    if half:
        out_ref, state_ref, column_ref, image_ref, field, result, sems = refs[4:]
    else:
        carry_ref, beside_ref, _, out_ref, image_ref, field, result, sems = refs[4:]
    device = place_ref[0]
    chip, core = device // 2, device % 2
    block = owns[0].shape[-1]
    width = field.shape[-1]
    count = width // group
    low = half * count
    for second_pair in range(2):
        for ref, side in ((owns[second_pair], core), (comes[second_pair], 1 - core)):
            start = pl.multiple_of(((chip // 2 ^ second_pair) * 2 + side) * block, block)
            for part in range(2):
                field[part, :, pl.ds(start, block)] = ref[part]
    first = count + 1 if half else 0
    copies = []

    def read(k):
        return [field[part, :, (k - low) * group : (k - low + 1) * group] for part in range(2)]

    def write(k, solved):
        if half and k == low:
            state_ref[...] = solved
            return
        where = k - first
        result[where, 0] = solved[:, :group]
        result[where, 1] = solved[:, group:]
        copy = pltpu.make_async_copy(
            result.at[where], out_ref.at[0, :, :, k * group : (k + 1) * group], sems.at[where]
        )
        copy.start()
        copies.append(copy)

    tables = (high_ref, low_ref, edge_ref)
    following, above = None, None
    if half:
        for part, value in enumerate(read(low)):
            column_ref[part] = jnp.broadcast_to(value[:, 0:1], column_ref.shape[1:])
    else:
        level = index_ref[step, count]
        solved = carry_ref[...]
        for part, value in enumerate(read(count - 1)):
            solved = solved + value[:, group - 1 : group] * edge_ref[level, part : part + 1, :]
        write(count, solved)
        following = halves(solved)
        above = [beside_ref[part, :, 0:1] for part in range(2)]
    line_groups(read, lambda k: index_ref[step, k], tables, low, low + count, following, None, above, write)
    image_ref[...] = jnp.zeros_like(image_ref)
    for i in range(block // group):
        mine = device * (block // group) + i
        here = mine > count if half else mine <= count

        @pl.when(here)
        def _():
            square = result[jnp.where(here, mine - first, 0), 0, i * group : (i + 1) * group, :]
            image_ref[:, i * group : (i + 1) * group] = diagonal_of(square)

    for copy in copies:
        copy.wait()


def last_pass(place, recv_index, tables, owns, comes, half, passed, shape, step, group):
    rows, length = shape[2:]
    width = length // 2
    count = width // group
    block = owns[0].shape[-1]
    args = [place, recv_index, *tables, *owns, *comes]
    any_space = pl.BlockSpec(memory_space=pl.ANY)
    specs = [smem()] * 2 + [vmem()] * 7
    outs = [whole(shape)]
    out_specs = [any_space]
    aliases = {}
    results = count - 1 if half else count + 1
    if half:
        outs += [whole((rows, 2 * group)), whole((2, rows, group))]
        out_specs += [vmem()] * 2
    else:
        migrated, state, column = passed
        args += [state, column, migrated]
        specs += [vmem(), vmem(), any_space]
        aliases = {len(args) - 1: 0}
    return pl.pallas_call(
        functools.partial(last_pass_kernel, half=half, step=step, group=group),
        out_shape=outs + [whole((1, block))],
        in_specs=specs,
        out_specs=out_specs + [vmem()],
        scratch_shapes=[
            pltpu.VMEM((2, rows, width), f32),
            pltpu.VMEM((results, 2, rows, group), f32),
            pltpu.SemaphoreType.DMA((results,)),
        ],
        input_output_aliases=aliases,
        compiler_params=params(24),
        cost_estimate=cost(rows * width * group * 24, 8 * rows * width * 2),
    )(*args)


def sum_over(value, axis, count):
    reach = 1
    while reach < count:
        value = value + lax.ppermute(value, axis, [(i, i ^ reach) for i in range(count)])
        reach *= 2
    return value


def fast_shards(wavefield, inv_table, couple_table, rhs_table, recv_index, shot_index, *, devices, freqs):
    levels, _, group, _ = inv_table.shape[1:]
    rows, length = wavefield.shape[2:]
    block = rows
    chips = devices // 2
    groups = 2 * rows // group
    device = lax.axis_index("plane")
    place = device.reshape(1).astype(jnp.int32)
    rhs = rhs_table[0]
    double = 2 * group
    partner = [(d, d ^ 1) for d in range(devices)]

    edge = lax.dynamic_slice_in_dim(wavefield, (device % 2) * (rows - 1), 1, axis=2)
    swap = [(d, d + 1) for d in range(1, devices - 1, 2)] + [(d + 1, d) for d in range(1, devices - 1, 2)]
    halo = lax.ppermute(edge, "plane", swap)
    right = make_tables(right_table_kernel, rhs, inv_table[0], couple_table[0], (levels, 4, double))

    keep, come = {}, {}
    carry = None
    for half in (1, 0):
        with jax.named_scope("first_%d" % half):
            result = first_pass(place, recv_index, wavefield, halo, right, half, carry, block, group)
        carry, keep[half], send = result if half else (None, *result)
        with jax.named_scope("swap_%d" % half):
            come[half] = lax.ppermute(send, "plane", partner)
    with jax.named_scope("left"):
        left = make_tables(left_table_kernel, rhs, inv_table[0], couple_table[0], (levels, 2, double, group))

    wide = block // 2
    piece = whole((4 * group + 16, wide))
    local = whole((groups, double, block))
    base = whole((2, group, group))
    locals_, bases, theirs = {}, {}, {}
    for half in (1, 0):
        for second_pair in (1, 0):
            spec = pltpu.PrefetchScalarGridSpec(
                num_scalar_prefetch=2,
                grid=(1,),
                in_specs=[vmem()] * 3
                + [pl.BlockSpec((1,) + keep[half].shape[1:], lambda i, at, _, o=second_pair: ((at[0] // 4) ^ o, 0, 0, 0))] * 2,
                out_specs=[vmem()] * 4,
                scratch_shapes=[pltpu.VMEM((2,) + piece.shape, f32)],
            )
            name = "%d_%d" % (half, second_pair)
            with jax.named_scope("open_" + name):
                near, far, locals_[name], bases[name] = pl.pallas_call(
                    functools.partial(open_sweep_kernel, groups=groups, group=group),
                    grid_spec=spec,
                    out_shape=[piece, piece, local, base],
                    compiler_params=params(24),
                    cost_estimate=cost(groups * group * block * group * 48, 8 * groups * group * block * 3),
                )(place, shot_index, *left, keep[half], come[half])
            for offset, item in ((2 * second_pair + 1, far), (2 * second_pair, near)):
                with jax.named_scope("out_%d_%d" % (half, offset)):
                    moves = [(d, d ^ (2 * offset)) for d in range(devices)]
                    theirs[half, offset] = lax.ppermute(item, "plane", moves) if offset else item

    matrices = whole((groups, double, double), bf16)
    middle = whole((chips - 2, double, double), bf16)
    with jax.named_scope("maps"):
        power_high, power_low, map_high, map_low, chip_high, chip_low = pl.pallas_call(
            functools.partial(map_kernel, groups=groups, group=group),
            out_shape=[matrices] * 4 + [middle] * 2,
            in_specs=[smem()] * 2 + [vmem()] * 3,
            out_specs=[vmem()] * 6,
            compiler_params=params(20),
            cost_estimate=cost(groups * group * group * group * 96, 4 * 1024 * 1024),
        )(place, shot_index, *left)

    came = {}
    for half in (1, 0):
        with jax.named_scope("scan_%d" % half):
            carries = pl.pallas_call(
                functools.partial(scan_kernel, chips=chips, group=group),
                out_shape=[piece] * chips,
                in_specs=[smem()] + [vmem()] * (6 + chips),
                out_specs=[vmem()] * chips,
                scratch_shapes=[pltpu.VMEM((chips,) + piece.shape, f32), pltpu.VMEM((chips, 16, wide), f32)],
                compiler_params=params(20),
                cost_estimate=cost(3 * group * group * wide * 24, 4 * 1024 * 1024),
            )(place, left[0], left[1], power_high, power_low, chip_high, chip_low, *[theirs[half, o] for o in range(chips)])
        for offset in (3, 1, 2, 0):
            with jax.named_scope("back_%d_%d" % (half, offset)):
                moves = [(d, d ^ (2 * offset)) for d in range(devices)]
                came[half, offset] = lax.ppermute(carries[offset], "plane", moves) if offset else carries[0]

    image_first, image_last = None, None
    passed = None
    part = whole((2, rows, block))
    for half in (1, 0):
        owns, comes = [], []
        for second_pair in (0, 1):
            name = "%d_%d" % (half, second_pair)
            with jax.named_scope("close_" + name):
                own, other, image = pl.pallas_call(
                    functools.partial(
                        close_sweep_kernel, groups=groups, group=group, part_of=half, second_pair=second_pair
                    ),
                    out_shape=[part, part, whole((1, block))],
                    in_specs=[smem()] * 2 + [vmem()] * 9,
                    out_specs=[vmem()] * 3,
                    scratch_shapes=[pltpu.VMEM((2,) + piece.shape, f32), pltpu.VMEM((2, 2, rows, block), f32)],
                    compiler_params=params(20),
                    cost_estimate=cost(groups * group * block * group * 24, 8 * groups * group * block * 2),
                )(
                    place, shot_index, left[2], power_high, power_low, map_high, map_low, locals_[name], bases[name],
                    came[half, 2 * second_pair], came[half, 2 * second_pair + 1],
                )
            owns.append(own)
            with jax.named_scope("return_" + name):
                comes.append(lax.ppermute(other, "plane", partner))
            image_first = image if image_first is None else image_first + image
        with jax.named_scope("last_%d" % half):
            *passed, image = last_pass(
                place, recv_index, right, owns, comes, half, passed, wavefield.shape, 1, group
            )
        image_last = image if image_last is None else image_last + image
    with jax.named_scope("image_0"):
        image_first = sum_over(image_first, "freq", freqs)
    with jax.named_scope("image_1"):
        image_last = sum_over(image_last, "freq", freqs)
    return passed[0], jnp.concatenate([image_first, image_last], axis=0)


def solution(mesh):
    placed = (
        P("freq", None, "plane", None),
        P("freq", None, None, None, None),
        P("freq", None, None, None),
        P("freq", None, None),
        P(),
        P(),
    )
    devices = mesh.shape["plane"]
    freqs = mesh.shape["freq"]

    def body(*arrays):
        if devices == 8 and arrays[0].shape[2] == 2 * GROUP and arrays[0].shape[0] == 1 and freqs & (freqs - 1) == 0:
            return fast_shards(*arrays, devices=devices, freqs=freqs)
        return shards(*arrays)

    return jax.shard_map(
        body,
        mesh=mesh,
        in_specs=placed,
        out_specs=(P("freq", None, "plane", None), P(None, "plane")),
        check_vma=False,
    )
```

```python
import functools

import jax
import jax.numpy as jnp
from jax import lax
from jax.experimental import pallas as pl
from jax.experimental.pallas import tpu as pltpu
from jax.sharding import PartitionSpec as P

NX = 2048
GROUP = 128
DEPTHS = 2


highest = lax.Precision.HIGHEST


def complex_product(form, mat_re, mat_im, vec_re, vec_im):
    real_part = jnp.einsum(form, mat_re, vec_re, precision=highest) - jnp.einsum(
        form, mat_im, vec_im, precision=highest
    )
    imag_part = jnp.einsum(form, mat_re, vec_im, precision=highest) + jnp.einsum(
        form, mat_im, vec_re, precision=highest
    )
    return (real_part, imag_part)


def select_rows(index, table):
    levels = jnp.arange(table.shape[1], dtype=jnp.int32)
    one_hot = (index[:, None] == levels[None, :]).astype(jnp.float32)
    return jnp.einsum("kv,fv...->fk...", one_hot, table, precision=highest)


def coupling_powers(couple_table, group_count):
    power_re = couple_table[:, 0]
    power_im = couple_table[:, 1]
    powers = []
    reach = 1
    while reach < group_count:
        powers.append((power_re, power_im))
        power_re, power_im = complex_product("fab,fbc->fac", power_re, power_im, power_re, power_im)
        reach = reach * 2
    return powers


def shifted_up(values, reach, group_axis):
    count = values.shape[group_axis]
    kept = lax.slice_in_dim(values, reach, count, axis=group_axis)
    zero_shape = list(values.shape)
    zero_shape[group_axis] = reach
    return jnp.concatenate([kept, jnp.zeros(zero_shape, values.dtype)], axis=group_axis)


def line_pass(wave_field, index, inv_table, rhs_table, powers, along_last):
    line_axis = 3 if along_last else 2
    freqs = wave_field.shape[0]
    length = wave_field.shape[line_axis]
    group_count = length // GROUP
    inv_sel = select_rows(index, inv_table)
    rhs_sel = select_rows(index, rhs_table)
    pad_widths = [(0, 0), (0, 0), (0, 0), (0, 0)]
    pad_widths[line_axis] = (1, 1)
    padded = jnp.pad(wave_field, pad_widths)
    beside = lax.slice_in_dim(padded, 0, length, axis=line_axis) + lax.slice_in_dim(
        padded, 2, length + 2, axis=line_axis
    )
    second = beside - 2.0 * wave_field
    if along_last:
        shape = (freqs, wave_field.shape[2], group_count, GROUP)
        coef_re = rhs_sel[:, None, :, 0, None]
        coef_im = rhs_sel[:, None, :, 1, None]
        local_form = "fkab,flkb->flka"
        power_form = "fab,flkb->flka"
        group_axis = 2
    else:
        shape = (freqs, group_count, GROUP, wave_field.shape[3])
        coef_re = rhs_sel[:, :, 0, None, None]
        coef_im = rhs_sel[:, :, 1, None, None]
        local_form = "fkab,fkbm->fkam"
        power_form = "fab,fkbm->fkam"
        group_axis = 1
    base_re = wave_field[:, 0].reshape(shape)
    base_im = wave_field[:, 1].reshape(shape)
    second_re = second[:, 0].reshape(shape)
    second_im = second[:, 1].reshape(shape)
    source_re = base_re + coef_re * second_re - coef_im * second_im
    source_im = base_im + coef_re * second_im + coef_im * second_re
    solved_re, solved_im = complex_product(
        local_form, inv_sel[:, :, 0], inv_sel[:, :, 1], source_re, source_im
    )
    reach = 1
    for power_re, power_im in powers:
        add_re, add_im = complex_product(
            power_form,
            power_re,
            power_im,
            shifted_up(solved_re, reach, group_axis),
            shifted_up(solved_im, reach, group_axis),
        )
        solved_re = solved_re + add_re
        solved_im = solved_im + add_im
        reach = reach * 2
    out_shape = (freqs,) + wave_field.shape[2:]
    return jnp.stack([solved_re.reshape(out_shape), solved_im.reshape(out_shape)], axis=1)


def to_columns(wave_field):
    return lax.all_to_all(wave_field, "plane", split_axis=3, concat_axis=2, tiled=True)


def to_rows(wave_field):
    return lax.all_to_all(wave_field, "plane", split_axis=2, concat_axis=3, tiled=True)


def diagonal_rows(wave_field, first_row):
    count = wave_field.shape[2]
    block = lax.dynamic_slice_in_dim(wave_field[:, 0], first_row, count, axis=2)
    return jnp.sum(jnp.diagonal(block, axis1=1, axis2=2), axis=0)


def diagonal_columns(wave_field, first_row):
    count = wave_field.shape[3]
    block = lax.dynamic_slice_in_dim(wave_field[:, 0], first_row, count, axis=1)
    return jnp.sum(jnp.diagonal(block, axis1=1, axis2=2), axis=0)


def image_part(partial_value):
    return lax.psum(partial_value, "freq")


def shards(wavefield, inv_table, couple_table, rhs_table, recv_index, shot_index):
    powers = coupling_powers(couple_table, NX // GROUP)
    row_count = wavefield.shape[2]
    first_row = lax.axis_index("plane") * row_count
    wave_field = wavefield
    parts = []
    for step_index in range(DEPTHS):
        if step_index % 2 == 0:
            wave_field = line_pass(
                wave_field, recv_index[step_index], inv_table, rhs_table, powers, True
            )
            wave_field = to_columns(wave_field)
            wave_field = line_pass(
                wave_field, shot_index[step_index], inv_table, rhs_table, powers, False
            )
            parts.append(image_part(diagonal_columns(wave_field, first_row)))
        else:
            wave_field = line_pass(
                wave_field, shot_index[step_index], inv_table, rhs_table, powers, False
            )
            wave_field = to_rows(wave_field)
            wave_field = line_pass(
                wave_field, recv_index[step_index], inv_table, rhs_table, powers, True
            )
            parts.append(image_part(diagonal_rows(wave_field, first_row)))
    stacked = jnp.stack(parts)
    return (wave_field, stacked)


f32 = jnp.float32
bf16 = jnp.bfloat16


def halves(value):
    high = value.astype(bf16)
    low = (value - high.astype(f32)).astype(bf16)
    return high, low


def mul(left, right):
    return jnp.dot(left, right, preferred_element_type=f32)


def product(left, right):
    (left_high, left_low), (right_high, right_low) = left, right
    return mul(left_high, right_high) + mul(left_low, right_high) + mul(left_high, right_low)


def params(mebibytes):
    return pltpu.CompilerParams(vmem_limit_bytes=mebibytes * 1024 * 1024)


def whole(shape, dtype=f32):
    return jax.ShapeDtypeStruct(shape, dtype)


def smem():
    return pl.BlockSpec(memory_space=pltpu.SMEM)


def vmem():
    return pl.BlockSpec(memory_space=pltpu.VMEM)


def anywhere():
    return pl.BlockSpec(memory_space=pl.ANY)


def cost(macs, size):
    return pl.CostEstimate(flops=2 * macs, bytes_accessed=size, transcendentals=0)


def folded(level, inv_ref, rhs_ref):
    mat_re, mat_im = inv_ref[level, 0], inv_ref[level, 1]
    coef_re, coef_im = rhs_ref[0, level, 0], rhs_ref[0, level, 1]
    group = mat_re.shape[-1]
    lane = lax.broadcasted_iota(jnp.int32, mat_re.shape, 1)

    def differences(mat):
        low_side = jnp.where(lane == 0, 0.0, pltpu.roll(mat, 1, 1))
        high_side = jnp.where(lane == group - 1, 0.0, pltpu.roll(mat, group - 1, 1))
        return low_side + high_side - 2.0 * mat

    diff_re, diff_im = differences(mat_re), differences(mat_im)
    inner_re = mat_re + coef_re * diff_re - coef_im * diff_im
    inner_im = mat_im + coef_re * diff_im + coef_im * diff_re
    scaled_re = coef_re * mat_re - coef_im * mat_im
    scaled_im = coef_re * mat_im + coef_im * mat_re
    return inner_re, inner_im, scaled_re, scaled_im


def store_left(high_ref, low_ref, index, mat_re, mat_im):
    group = mat_re.shape[-1]
    blocks = ((mat_re, -mat_im), (mat_im, mat_re))
    for i in range(2):
        for j in range(2):
            where = (index, slice(i * group, (i + 1) * group), slice(j * group, (j + 1) * group))
            high_ref[where], low_ref[where] = halves(blocks[i][j])


def left_table_kernel(rhs_ref, inv_ref, couple_ref, high_ref, low_ref, edge_ref):
    levels, _, group, _ = inv_ref.shape
    for level in range(levels):
        inner_re, inner_im, scaled_re, scaled_im = folded(level, inv_ref, rhs_ref)
        store_left(high_ref, low_ref, level, inner_re, inner_im)
        for part, scaled in enumerate((scaled_re, scaled_im)):
            rows = slice(part * group, (part + 1) * group)
            edge_ref[level, 0, rows, :] = jnp.broadcast_to(scaled[:, 0:1], (group, group))
            edge_ref[level, 1, rows, :] = jnp.broadcast_to(scaled[:, group - 1 : group], (group, group))
    store_left(high_ref, low_ref, levels, couple_ref[0], couple_ref[1])


def right_table_kernel(rhs_ref, inv_ref, couple_ref, high_ref, low_ref, edge_ref):
    levels, _, group, _ = inv_ref.shape
    for level in range(levels + 1):
        if level < levels:
            inner_re, inner_im, scaled_re, scaled_im = folded(level, inv_ref, rhs_ref)
            scaled_re, scaled_im = scaled_re.T, scaled_im.T
            for side, row in enumerate((0, group - 1)):
                edge_re, edge_im = scaled_re[row : row + 1], scaled_im[row : row + 1]
                edge_ref[level, 2 * side : 2 * side + 1, :] = jnp.concatenate([edge_re, edge_im], axis=1)
                edge_ref[level, 2 * side + 1 : 2 * side + 2, :] = jnp.concatenate([-edge_im, edge_re], axis=1)
        else:
            inner_re, inner_im = couple_ref[0], couple_ref[1]
        turned_re, turned_im = inner_re.T, inner_im.T
        store_left(high_ref, low_ref, level, turned_re, -turned_im)


def make_tables(kernel, rhs, inv_table, couple_table, edge_shape):
    levels, _, group, _ = inv_table.shape
    shape = whole((levels + 1, 2 * group, 2 * group), bf16)
    return pl.pallas_call(
        kernel,
        out_shape=[shape, shape, whole(edge_shape)],
        in_specs=[smem(), vmem(), vmem()],
        out_specs=[vmem()] * 3,
        compiler_params=params(16),
        cost_estimate=cost(10**10, 4 * 1024 * 1024),
    )(rhs, inv_table, couple_table)


def edge_row_kernel(place_ref, field_ref, row_ref, held, sem):
    rows = field_ref.shape[2]
    odd = place_ref[0] % 2
    start = pl.multiple_of(odd * (rows - 8), 8)
    copy = pltpu.make_async_copy(field_ref.at[0, :, pl.ds(start, 8), :], held, sem)
    copy.start()
    copy.wait()
    for part in range(2):
        row_ref[0, part] = jnp.where(odd == 1, held[part, 7:8, :], held[part, 0:1, :])


def edge_row(place, field):
    length = field.shape[3]
    return pl.pallas_call(
        edge_row_kernel,
        out_shape=whole((1, 2, 1, length)),
        in_specs=[smem(), anywhere()],
        out_specs=vmem(),
        scratch_shapes=[pltpu.VMEM((2, 8, length), f32), pltpu.SemaphoreType.DMA],
        compiler_params=params(60),
        cost_estimate=cost(10**10, 1024 * 1024),
    )(place, field)


def line_groups(read, level_of, tables, low, high, following, below, above, write):
    high_ref, low_ref, edge_ref = tables
    last = high_ref.shape[0] - 1
    couple = (high_ref[last], low_ref[last])
    for k in reversed(range(low, high)):
        level = level_of(k)
        value_re, value_im = read(k)
        group = value_re.shape[1]
        solved = product(halves(jnp.concatenate([value_re, value_im], axis=1)), (high_ref[level], low_ref[level]))
        if following is not None:
            solved = solved + product(following, couple)
        before = [item[:, group - 1 : group] for item in read(k - 1)] if k > low else below
        for side, column in ((0, before), (1, above)):
            if column is not None:
                for part in range(2):
                    row = edge_ref[level, 2 * side + part : 2 * side + part + 1, :]
                    solved = solved + column[part] * row
        write(k, solved)
        following = halves(solved)
        above = [value_re[:, 0:1], value_im[:, 0:1]]


def rows_with_halo(field_ref, halo_ref, part, columns, halo_columns):
    row = jnp.broadcast_to(halo_ref[0, part, :, halo_columns], (8, columns.stop - columns.start))
    return jnp.concatenate([field_ref[0, part, :, columns], row], axis=0)


def first_pass_kernel(place_ref, index_ref, field_ref, beside_ref, halo_ref, high_ref, low_ref, edge_ref, *refs,
                      half, group, block):
    if half:
        carry_ref, keep_ref, send_ref, own = None, refs[1], refs[2], refs[3]
        state_ref = refs[0]
    else:
        carry_ref, _, keep_ref, send_ref, own = refs
        state_ref = None
    width = field_ref.shape[-1]
    count = width // group
    low = half * count
    core = place_ref[0] % 2

    def read(k):
        columns = slice((k - low) * group, (k - low + 1) * group)
        wide = slice(k * group, (k + 1) * group)
        return [rows_with_halo(field_ref, halo_ref, part, columns, wide) for part in range(2)]

    inside = slice(0, group)
    wide = slice((low - 1) * group, low * group) if half else slice(count * group, (count + 1) * group)
    beyond = [rows_with_halo(beside_ref, halo_ref, part, inside, wide) for part in range(2)]
    if half:
        below, above, following = [item[:, group - 1 : group] for item in beyond], None, None
    else:
        below, above, following = None, [item[:, 0:1] for item in beyond], halves(carry_ref[...])

    def write(k, solved):
        start = (k - low) * group
        b, inner = start // block, start % block
        own[b % 2, b // 2, 0, :, inner : inner + group] = solved[:, :group]
        own[b % 2, b // 2, 1, :, inner : inner + group] = solved[:, group:]
        if half and k == low:
            state_ref[...] = solved

    line_groups(
        read, lambda k: index_ref[0, k], (high_ref, low_ref, edge_ref), low, low + count, following, below, above, write
    )
    keep_ref[...] = own[core]
    send_ref[...] = own[1 - core]


def first_pass(place, recv_index, field, halo, tables, half, carry, after, block, group):
    rows, length = field.shape[2:]
    width = length // 2
    lines = rows + 8
    count = width // group
    shape = (width // (2 * block), 2, lines, block)
    beside = count - 1 if half else count
    args = [place, recv_index, field, field, halo, *tables]
    specs = [
        smem(), smem(),
        pl.BlockSpec((1, 2, rows, width), lambda i: (0, 0, 0, half)),
        pl.BlockSpec((1, 2, rows, group), lambda i: (0, 0, 0, beside)),
    ] + [vmem()] * 4
    outs = [whole(shape)] * 2
    if half:
        outs = [whole((lines, 2 * group))] + outs
    else:
        args += [carry, after]
        specs += [vmem(), anywhere()]
    return pl.pallas_call(
        functools.partial(first_pass_kernel, half=half, group=group, block=block),
        grid=(1,),
        out_shape=outs,
        in_specs=specs,
        out_specs=[vmem()] * len(outs),
        scratch_shapes=[pltpu.VMEM((2,) + shape, f32)],
        compiler_params=params(36),
        cost_estimate=cost(lines * width * group * 24, 8 * lines * width * 2),
    )(*args)


def add_edge(solved, edge_ref, level, side, row_re, row_im):
    group = edge_ref.shape[-1]
    wide = row_re.shape[-1]
    column = [edge_ref[level, side, part * group : (part + 1) * group, :] for part in range(2)]
    if wide > group:
        column = [jnp.concatenate([item] * (wide // group), axis=1) for item in column]
    term_re = column[0] * row_re - column[1] * row_im
    term_im = column[0] * row_im + column[1] * row_re
    both = jnp.concatenate([term_re, term_im], axis=0)
    return both if solved is None else solved + both


def second_groups(chip, groups, index_ref, tables):
    high_ref, low_ref, edge_ref = tables
    last = high_ref.shape[0] - 1
    couple = (high_ref[last], low_ref[last])
    base = chip * groups
    total = index_ref.shape[1]

    def open_state(row_re, row_im):
        after = base + groups
        level = index_ref[1, jnp.minimum(after, total - 1)]
        inside = jnp.where(after < total, 1.0, 0.0)
        return add_edge(None, edge_ref, level, 0, row_re * inside, row_im * inside)

    def step(k, value, following, before, after):
        level = index_ref[1, base + k]
        solved = product((high_ref[level], low_ref[level]), value)
        solved = solved + product(couple, following)
        if before is not None:
            solved = add_edge(solved, edge_ref, level, 0, *before)
        if after is not None:
            solved = add_edge(solved, edge_ref, level, 1, *after)
        return solved

    return open_state, step


def first_row(value, group):
    return value[0:1], value[group : group + 1]


def last_row(value, group):
    return value[group - 1 : group], value[2 * group - 1 : 2 * group]


def open_sweep_kernel(place_ref, index_ref, high_ref, low_ref, edge_ref, keep_ref, come_ref, _, near_ref, far_ref, local_ref,
                      base_ref, pair, *, groups, group):
    device = place_ref[0]
    chip, core = device // 2, device % 2
    tables = (high_ref, low_ref, edge_ref)
    last = high_ref.shape[0] - 1
    couple = (high_ref[last], low_ref[last])
    half = groups // 2
    lines = half * group
    width = keep_ref.shape[-1]

    def rows(upper, start, count):
        mine = upper == core
        return [
            jnp.where(mine, keep_ref[0, part, start : start + count, :], come_ref[0, part, start : start + count, :])
            for part in range(2)
        ]

    def store_pair(where, value):
        for sub in range(2):
            pair[sub, where, :] = value[:, sub * (width // 2) : (sub + 1) * (width // 2)]

    def given(k):
        return rows(k // half, (k % half) * group, group)

    open_state, step = second_groups(chip, groups, index_ref, tables)
    above = [item[0:1] for item in rows(1, lines, 8)]
    solved = following = state = None
    value = given(groups - 1)
    earlier = None
    for k in reversed(range(groups)):
        level = index_ref[0, chip * groups + k]
        below_value = given(k - 1) if k else None
        before = [item[group - 1 : group] for item in below_value] if k else [item[0:1] for item in rows(0, lines, 8)]
        now = product((high_ref[level], low_ref[level]), halves(jnp.concatenate(value, axis=0)))
        if following is not None:
            now = now + product(couple, following)
        now = add_edge(now, edge_ref, level, 0, *before)
        now = add_edge(now, edge_ref, level, 1, *above)
        above = [item[0:1] for item in value]
        value = below_value
        base_ref[k // half, k % half] = now[:group, (k % half) * group : (k % half + 1) * group]
        if k == groups - 1:
            row_re, row_im = last_row(now, group)
            for part, row in enumerate((row_re, row_im)):
                store_pair(slice(4 * group + 8 * part, 4 * group + 8 * part + 8), jnp.broadcast_to(row, (8, width)))
            state = halves(open_state(row_re, row_im))
        else:
            done = step(k + 1, following, state, last_row(now, group), first_row(earlier, group) if earlier is not None else None)
            local_ref[k + 1] = done
            state = halves(done)
        earlier = solved
        solved = now
        following = halves(now)
    done = step(0, following, state, None, first_row(earlier, group))
    local_ref[0] = done
    store_pair(slice(0, 2 * group), solved)
    store_pair(slice(2 * group, 4 * group), done)
    near_ref[...] = pair[chip % 2]
    far_ref[...] = pair[1 - chip % 2]


def power_kernel(index_ref, high_ref, low_ref, edge_ref, _, power_high, power_low, chip_high, chip_low, *, groups, group):
    last = high_ref.shape[0] - 1
    couple = (high_ref[last], low_ref[last])
    rows = lax.broadcasted_iota(jnp.int32, (2 * group, group), 0)
    columns = lax.broadcasted_iota(jnp.int32, (2 * group, group), 1)
    values = [None] * groups + [(rows == columns).astype(f32)]
    split = [None] * groups
    for k in reversed(range(groups)):
        values[k] = product(couple, halves(values[k + 1]))
        split[k] = halves(values[k])
        store_left(power_high, power_low, k, values[k][:group], values[k][group:])
    for q in range(chip_high.shape[0]):

        def store(k, done, q=q):
            if k == 0:
                store_left(chip_high, chip_low, q, done[:group], done[group:])

        linear_part(q + 1, groups, group, index_ref, (high_ref, low_ref, edge_ref), values, split, store)


def own_map_kernel(place_ref, index_ref, high_ref, low_ref, edge_ref, power_high, power_low, _, map_high, map_low,
                   *, groups, group):
    rows = lax.broadcasted_iota(jnp.int32, (2 * group, group), 0)
    columns = lax.broadcasted_iota(jnp.int32, (2 * group, group), 1)
    split = [(power_high[k, :, 0:group], power_low[k, :, 0:group]) for k in range(groups)]
    values = [high.astype(f32) + low.astype(f32) for high, low in split]
    values.append((rows == columns).astype(f32))

    def store(k, done):
        store_left(map_high, map_low, k, done[:group], done[group:])

    linear_part(place_ref[0] // 2, groups, group, index_ref, (high_ref, low_ref, edge_ref), values, split, store)


def linear_part(chip, groups, group, index_ref, tables, values, split, store):
    open_state, step = second_groups(chip, groups, index_ref, tables)
    state = halves(open_state(*last_row(values[groups - 1], group)))
    for k in reversed(range(groups)):
        before = last_row(values[k - 1], group) if k else None
        done = step(k, split[k], state, before, first_row(values[k + 1], group))
        state = halves(done)
        store(k, done)


def scan_kernel(place_ref, high_ref, low_ref, power_high, power_low, chip_high, chip_low, *refs, chips, group):
    pieces, outs, (held, rows) = refs[:chips], refs[-chips - 2 : -2], refs[-2:]
    chip = place_ref[0] // 2
    last = high_ref.shape[0] - 1
    size = 4 * group
    for offset in range(chips):
        held[chip ^ offset] = pieces[offset][...]
    keep = (power_high[0], power_low[0])
    rows[0] = jnp.zeros_like(rows[0])
    for q in range(chips - 1, 0, -1):
        first = halves(held[q, 0 : 2 * group, :])
        for part in range(2):
            tail = slice((part + 1) * group - 16, (part + 1) * group)
            row = product((high_ref[last, tail, :], low_ref[last, tail, :]), first)[15:16]
            base = size + 8 * part
            rows[q, 8 * part : 8 * part + 8, :] = held[q - 1, base : base + 8, :] + row
        if q > 1:
            second = halves(held[q, 2 * group : size, :])
            held[q - 1, 0 : 2 * group, :] = held[q - 1, 0 : 2 * group, :] + product(keep, first)
            held[q - 1, 2 * group : size, :] = (
                held[q - 1, 2 * group : size, :]
                + product((chip_high[q - 2], chip_low[q - 2]), first)
                + product(keep, second)
            )
    held[0] = jnp.zeros_like(held[0])
    for offset in range(chips):
        target = chip ^ offset
        outs[offset][0:size, :] = held[(target + 1) % chips, 0:size, :]
        outs[offset][size : size + 16, :] = rows[target]


def close_sweep_kernel(place_ref, index_ref, edge_ref, power_high, power_low, map_high, map_low, local_ref, base_ref,
                       near_ref, far_ref, _, own_ref, other_ref, image_ref, pair, result, *, groups, group, part_of, second_pair):
    device = place_ref[0]
    chip, core = device // 2, device % 2
    pair[chip % 2] = near_ref[...]
    pair[1 - chip % 2] = far_ref[...]

    def carried(start, count):
        return jnp.concatenate([pair[0, start : start + count, :], pair[1, start : start + count, :]], axis=1)

    first = halves(carried(0, 2 * group))
    second = halves(carried(2 * group, 2 * group))
    half = groups // 2
    for k in reversed(range(groups)):
        done = local_ref[k] + (
            product((map_high[k], map_low[k]), first) + product((power_high[k], power_low[k]), second)
        )
        if k == 0:
            level = index_ref[1, chip * groups]
            base = 4 * group
            done = add_edge(done, edge_ref, level, 0, carried(base, 8)[0:1], carried(base + 8, 8)[0:1])
        rows = slice((k % half) * group, (k % half + 1) * group)
        result[k // half, 0, rows, :] = done[:group]
        result[k // half, 1, rows, :] = done[group:]
    own_ref[...] = result[core]
    other_ref[...] = result[1 - core]
    image_ref[...] = jnp.zeros_like(image_ref)

    @pl.when((chip // 2 == part_of) & ((chip % 2) ^ (chip // 2) == second_pair))
    def _():
        for i in range(half):
            k = core * half + i
            columns = slice(i * group, (i + 1) * group)
            square = base_ref[core, i] + product(
                (power_high[k, 0:group, :], power_low[k, 0:group, :]), [item[:, columns] for item in first]
            )
            image_ref[:, columns] = diagonal_of(square)


def diagonal_of(square):
    rows = lax.broadcasted_iota(jnp.int32, square.shape, 0)
    columns = lax.broadcasted_iota(jnp.int32, square.shape, 1)
    return jnp.sum(jnp.where(rows == columns, square, 0.0), axis=0, keepdims=True)


def last_pass_kernel(place_ref, index_ref, high_ref, low_ref, edge_ref, *refs, half, step, group):
    owns, comes = refs[0:2], refs[2:4]
    if half:
        out_ref, state_ref, column_ref, image_ref, field, result, sems = refs[4:]
    else:
        carry_ref, beside_ref, _, *images = refs[4:-5]
        out_ref, image_ref, field, result, sems = refs[-5:]
    device = place_ref[0]
    chip, core = device // 2, device % 2
    block = owns[0].shape[-1]
    width = field.shape[-1]
    count = width // group
    low = half * count
    for second_pair in range(2):
        for ref, side in ((owns[second_pair], core), (comes[second_pair], 1 - core)):
            start = pl.multiple_of(((chip // 2 ^ second_pair) * 2 + side) * block, block)
            for part in range(2):
                field[part, :, pl.ds(start, block)] = ref[part]
    first = count + 1 if half else 0
    copies = []

    def read(k):
        return [field[part, :, (k - low) * group : (k - low + 1) * group] for part in range(2)]

    def write(k, solved):
        if half and k == low:
            state_ref[...] = solved
            return
        where = k - first
        result[where, 0] = solved[:, :group]
        result[where, 1] = solved[:, group:]
        copy = pltpu.make_async_copy(
            result.at[where], out_ref.at[0, :, :, k * group : (k + 1) * group], sems.at[where]
        )
        copy.start()
        copies.append(copy)

    tables = (high_ref, low_ref, edge_ref)
    following, above = None, None
    if half:
        for part, value in enumerate(read(low)):
            column_ref[part] = jnp.broadcast_to(value[:, 0:1], column_ref.shape[1:])
    else:
        level = index_ref[step, count]
        solved = carry_ref[...]
        for part, value in enumerate(read(count - 1)):
            solved = solved + value[:, group - 1 : group] * edge_ref[level, part : part + 1, :]
        write(count, solved)
        following = halves(solved)
        above = [beside_ref[part, :, 0:1] for part in range(2)]
    line_groups(read, lambda k: index_ref[step, k], tables, low, low + count, following, None, above, write)
    if half:
        image_ref[...] = jnp.zeros_like(image_ref)
    else:
        image_ref[1:2] = images[0][...]
        image_ref[0:1] = sum((item[...] for item in images[2:]), images[1][...])
    row = image_ref.shape[0] - 1
    for i in range(block // group):
        mine = device * (block // group) + i
        here = mine > count if half else mine <= count

        @pl.when(here)
        def _():
            square = result[jnp.where(here, mine - first, 0), 0, i * group : (i + 1) * group, :]
            image_ref[row : row + 1, i * group : (i + 1) * group] = diagonal_of(square)

    for copy in copies:
        copy.wait()


def last_pass(place, recv_index, tables, owns, comes, half, passed, shape, step, group):
    rows, length = shape[2:]
    width = length // 2
    count = width // group
    block = owns[0].shape[-1]
    args = [place, recv_index, *tables, *owns, *comes]
    any_space = pl.BlockSpec(memory_space=pl.ANY)
    specs = [smem()] * 2 + [vmem()] * 7
    outs = [whole(shape)]
    out_specs = [any_space]
    aliases = {}
    results = count - 1 if half else count + 1
    if half:
        outs += [whole((rows, 2 * group)), whole((2, rows, group))]
        out_specs += [vmem()] * 2
    else:
        migrated, state, column, *images = passed
        args += [state, column, migrated, *images]
        specs += [vmem(), vmem(), any_space] + [vmem()] * len(images)
        aliases = {len(args) - 1 - len(images): 0}
    return pl.pallas_call(
        functools.partial(last_pass_kernel, half=half, step=step, group=group),
        out_shape=outs + [whole((1 if half else 2, block))],
        in_specs=specs,
        out_specs=out_specs + [vmem()],
        scratch_shapes=[
            pltpu.VMEM((2, rows, width), f32),
            pltpu.VMEM((results, 2, rows, group), f32),
            pltpu.SemaphoreType.DMA((results,)),
        ],
        input_output_aliases=aliases,
        compiler_params=params(24),
        cost_estimate=cost(rows * width * group * 24, 8 * rows * width * 2),
    )(*args)


def sum_over(value, axis, count):
    reach = 1
    while reach < count:
        value = value + lax.ppermute(value, axis, [(i, i ^ reach) for i in range(count)])
        reach *= 2
    return value


def fast_shards(wavefield, inv_table, couple_table, rhs_table, recv_index, shot_index, *, devices, freqs):
    levels, _, group, _ = inv_table.shape[1:]
    rows, _ = wavefield.shape[2:]
    block = rows
    chips = devices // 2
    groups = 2 * rows // group
    device = lax.axis_index("plane")
    place = device.reshape(1).astype(jnp.int32)
    double = 2 * group
    partner = [(d, d ^ 1) for d in range(devices)]

    edge = edge_row(place, wavefield)
    swap = [(d, d + 1) for d in range(1, devices - 1, 2)] + [(d + 1, d) for d in range(1, devices - 1, 2)]
    halo = lax.ppermute(edge, "plane", swap)
    right = make_tables(right_table_kernel, rhs_table, inv_table[0], couple_table[0], (levels, 4, double))

    left = make_tables(left_table_kernel, rhs_table, inv_table[0], couple_table[0], (levels, 2, double, group))

    wide = block // 2
    piece = whole((4 * group + 16, wide))
    local = whole((groups, double, block))
    base = whole((2, groups // 2, group, group))
    matrices = whole((groups, double, double), bf16)
    middle = whole((chips - 2, double, double), bf16)
    powers = []

    def make_powers(ready):
        powers.extend(
            pl.pallas_call(
                functools.partial(power_kernel, groups=groups, group=group),
                out_shape=[matrices] * 2 + [middle] * 2,
                in_specs=[smem()] + [vmem()] * 3 + [anywhere()],
                out_specs=[vmem()] * 4,
                compiler_params=params(20),
                cost_estimate=cost(groups * group * group * group * 64, 4 * 1024 * 1024),
            )(shot_index, *left, ready)
        )
        return powers[0]

    keep, come = {}, {}
    locals_, bases, theirs = {}, {}, {}
    carry = after = None
    for half in (1, 0):
        result = first_pass(place, recv_index, wavefield, halo, right, half, carry, after, block, group)
        carry, keep[half], send = result if half else (None, *result)
        after = carry if half else make_powers(keep[half])
        come[half] = lax.ppermute(send, "plane", partner)
        for second_pair in (1, 0):
            spec = pltpu.PrefetchScalarGridSpec(
                num_scalar_prefetch=2,
                grid=(1,),
                in_specs=[vmem()] * 3
                + [pl.BlockSpec((1,) + keep[half].shape[1:], lambda i, at, _, o=second_pair: ((at[0] // 4) ^ o, 0, 0, 0))] * 2
                + [anywhere()],
                out_specs=[vmem()] * 4,
                scratch_shapes=[pltpu.VMEM((2,) + piece.shape, f32)],
            )
            name = "%d_%d" % (half, second_pair)
            near, far, locals_[name], bases[name] = pl.pallas_call(
                functools.partial(open_sweep_kernel, groups=groups, group=group),
                grid_spec=spec,
                out_shape=[piece, piece, local, base],
                compiler_params=params(24),
                cost_estimate=cost(groups * group * block * group * 48, 8 * groups * group * block * 3),
            )(place, shot_index, *left, keep[half], come[half], after)
            after = near
            for offset, item in ((2 * second_pair + 1, far), (2 * second_pair, near)):
                moves = [(d, d ^ (2 * offset)) for d in range(devices)]
                theirs[half, offset] = lax.ppermute(item, "plane", moves) if offset else item

    power_high, power_low, chip_high, chip_low = powers
    came = {}
    for half in (1, 0):
        carries = pl.pallas_call(
            functools.partial(scan_kernel, chips=chips, group=group),
            out_shape=[piece] * chips,
            in_specs=[smem()] + [vmem()] * (6 + chips) + [anywhere()],
            out_specs=[vmem()] * chips,
            scratch_shapes=[pltpu.VMEM((chips,) + piece.shape, f32), pltpu.VMEM((chips, 16, wide), f32)],
            compiler_params=params(20),
            cost_estimate=cost(3 * group * group * wide * 24, 4 * 1024 * 1024),
        )(place, left[0], left[1], power_high, power_low, chip_high, chip_low, *[theirs[half, o] for o in range(chips)], after)
        after = carries[0]
        if half:
            map_high, map_low = pl.pallas_call(
                functools.partial(own_map_kernel, groups=groups, group=group),
                out_shape=[matrices] * 2,
                in_specs=[smem()] * 2 + [vmem()] * 5 + [anywhere()],
                out_specs=[vmem()] * 2,
                compiler_params=params(20),
                cost_estimate=cost(groups * group * group * group * 32, 4 * 1024 * 1024),
            )(place, shot_index, *left, power_high, power_low, after)
            after = map_high
        for offset in (3, 1, 2, 0):
            moves = [(d, d ^ (2 * offset)) for d in range(devices)]
            came[half, offset] = lax.ppermute(carries[offset], "plane", moves) if offset else carries[0]

    images, image_last = [], None
    passed = None
    part = whole((2, rows, block))
    for half in (1, 0):
        owns, comes = [], []
        for second_pair in (0, 1):
            name = "%d_%d" % (half, second_pair)
            own, other, image = pl.pallas_call(
                functools.partial(
                    close_sweep_kernel, groups=groups, group=group, part_of=half, second_pair=second_pair
                ),
                out_shape=[part, part, whole((1, block))],
                in_specs=[smem()] * 2 + [vmem()] * 9 + [anywhere()],
                out_specs=[vmem()] * 3,
                scratch_shapes=[pltpu.VMEM((2,) + piece.shape, f32), pltpu.VMEM((2, 2, rows, block), f32)],
                compiler_params=params(20),
                cost_estimate=cost(groups * group * block * group * 24, 8 * groups * group * block * 2),
            )(
                place, shot_index, left[2], power_high, power_low, map_high, map_low, locals_[name], bases[name],
                came[half, 2 * second_pair], came[half, 2 * second_pair + 1], after,
            )
            after = image
            owns.append(own)
            comes.append(lax.ppermute(other, "plane", partner))
            images.append(image)
        if not half:
            passed = [*passed, image_last, *images]
        *passed, image_last = last_pass(place, recv_index, right, owns, comes, half, passed, wavefield.shape, 1, group)
        after = image_last
    image_last = sum_over(image_last, "freq", freqs)
    return passed[0], image_last


def solution(mesh):
    placed = (
        P("freq", None, "plane", None),
        P("freq", None, None, None, None),
        P("freq", None, None, None),
        P("freq", None, None),
        P(),
        P(),
    )
    devices = mesh.shape["plane"]
    freqs = mesh.shape["freq"]

    def body(*arrays):
        if devices == 8 and arrays[0].shape[2] == 2 * GROUP and arrays[0].shape[0] == 1 and freqs & (freqs - 1) == 0:
            return fast_shards(*arrays, devices=devices, freqs=freqs)
        return shards(*arrays)

    return jax.shard_map(
        body,
        mesh=mesh,
        in_specs=placed,
        out_specs=(P("freq", None, "plane", None), P(None, "plane")),
        check_vma=False,
    )
```

```python
import functools

import jax
import jax.numpy as jnp
from jax import lax
from jax.experimental import pallas as pl
from jax.experimental.pallas import tpu as pltpu
from jax.sharding import PartitionSpec as P

NX = 2048
GROUP = 128
DEPTHS = 2


highest = lax.Precision.HIGHEST


def complex_product(form, mat_re, mat_im, vec_re, vec_im):
    real_part = jnp.einsum(form, mat_re, vec_re, precision=highest) - jnp.einsum(
        form, mat_im, vec_im, precision=highest
    )
    imag_part = jnp.einsum(form, mat_re, vec_im, precision=highest) + jnp.einsum(
        form, mat_im, vec_re, precision=highest
    )
    return (real_part, imag_part)


def select_rows(index, table):
    levels = jnp.arange(table.shape[1], dtype=jnp.int32)
    one_hot = (index[:, None] == levels[None, :]).astype(jnp.float32)
    return jnp.einsum("kv,fv...->fk...", one_hot, table, precision=highest)


def coupling_powers(couple_table, group_count):
    power_re = couple_table[:, 0]
    power_im = couple_table[:, 1]
    powers = []
    reach = 1
    while reach < group_count:
        powers.append((power_re, power_im))
        power_re, power_im = complex_product("fab,fbc->fac", power_re, power_im, power_re, power_im)
        reach = reach * 2
    return powers


def shifted_up(values, reach, group_axis):
    count = values.shape[group_axis]
    kept = lax.slice_in_dim(values, reach, count, axis=group_axis)
    zero_shape = list(values.shape)
    zero_shape[group_axis] = reach
    return jnp.concatenate([kept, jnp.zeros(zero_shape, values.dtype)], axis=group_axis)


def line_pass(wave_field, index, inv_table, rhs_table, powers, along_last):
    line_axis = 3 if along_last else 2
    freqs = wave_field.shape[0]
    length = wave_field.shape[line_axis]
    group_count = length // GROUP
    inv_sel = select_rows(index, inv_table)
    rhs_sel = select_rows(index, rhs_table)
    pad_widths = [(0, 0), (0, 0), (0, 0), (0, 0)]
    pad_widths[line_axis] = (1, 1)
    padded = jnp.pad(wave_field, pad_widths)
    beside = lax.slice_in_dim(padded, 0, length, axis=line_axis) + lax.slice_in_dim(
        padded, 2, length + 2, axis=line_axis
    )
    second = beside - 2.0 * wave_field
    if along_last:
        shape = (freqs, wave_field.shape[2], group_count, GROUP)
        coef_re = rhs_sel[:, None, :, 0, None]
        coef_im = rhs_sel[:, None, :, 1, None]
        local_form = "fkab,flkb->flka"
        power_form = "fab,flkb->flka"
        group_axis = 2
    else:
        shape = (freqs, group_count, GROUP, wave_field.shape[3])
        coef_re = rhs_sel[:, :, 0, None, None]
        coef_im = rhs_sel[:, :, 1, None, None]
        local_form = "fkab,fkbm->fkam"
        power_form = "fab,fkbm->fkam"
        group_axis = 1
    base_re = wave_field[:, 0].reshape(shape)
    base_im = wave_field[:, 1].reshape(shape)
    second_re = second[:, 0].reshape(shape)
    second_im = second[:, 1].reshape(shape)
    source_re = base_re + coef_re * second_re - coef_im * second_im
    source_im = base_im + coef_re * second_im + coef_im * second_re
    solved_re, solved_im = complex_product(
        local_form, inv_sel[:, :, 0], inv_sel[:, :, 1], source_re, source_im
    )
    reach = 1
    for power_re, power_im in powers:
        add_re, add_im = complex_product(
            power_form,
            power_re,
            power_im,
            shifted_up(solved_re, reach, group_axis),
            shifted_up(solved_im, reach, group_axis),
        )
        solved_re = solved_re + add_re
        solved_im = solved_im + add_im
        reach = reach * 2
    out_shape = (freqs,) + wave_field.shape[2:]
    return jnp.stack([solved_re.reshape(out_shape), solved_im.reshape(out_shape)], axis=1)


def to_columns(wave_field):
    return lax.all_to_all(wave_field, "plane", split_axis=3, concat_axis=2, tiled=True)


def to_rows(wave_field):
    return lax.all_to_all(wave_field, "plane", split_axis=2, concat_axis=3, tiled=True)


def diagonal_rows(wave_field, first_row):
    count = wave_field.shape[2]
    block = lax.dynamic_slice_in_dim(wave_field[:, 0], first_row, count, axis=2)
    return jnp.sum(jnp.diagonal(block, axis1=1, axis2=2), axis=0)


def diagonal_columns(wave_field, first_row):
    count = wave_field.shape[3]
    block = lax.dynamic_slice_in_dim(wave_field[:, 0], first_row, count, axis=1)
    return jnp.sum(jnp.diagonal(block, axis1=1, axis2=2), axis=0)


def image_part(partial_value):
    return lax.psum(partial_value, "freq")


def shards(wavefield, inv_table, couple_table, rhs_table, recv_index, shot_index):
    powers = coupling_powers(couple_table, NX // GROUP)
    row_count = wavefield.shape[2]
    first_row = lax.axis_index("plane") * row_count
    wave_field = wavefield
    parts = []
    for step_index in range(DEPTHS):
        if step_index % 2 == 0:
            wave_field = line_pass(
                wave_field, recv_index[step_index], inv_table, rhs_table, powers, True
            )
            wave_field = to_columns(wave_field)
            wave_field = line_pass(
                wave_field, shot_index[step_index], inv_table, rhs_table, powers, False
            )
            parts.append(image_part(diagonal_columns(wave_field, first_row)))
        else:
            wave_field = line_pass(
                wave_field, shot_index[step_index], inv_table, rhs_table, powers, False
            )
            wave_field = to_rows(wave_field)
            wave_field = line_pass(
                wave_field, recv_index[step_index], inv_table, rhs_table, powers, True
            )
            parts.append(image_part(diagonal_rows(wave_field, first_row)))
    stacked = jnp.stack(parts)
    return (wave_field, stacked)


f32 = jnp.float32
bf16 = jnp.bfloat16


def halves(value):
    high = value.astype(bf16)
    low = (value - high.astype(f32)).astype(bf16)
    return high, low


def mul(left, right):
    return jnp.dot(left, right, preferred_element_type=f32)


def product(left, right):
    (left_high, left_low), (right_high, right_low) = left, right
    return mul(left_high, right_high) + mul(left_low, right_high) + mul(left_high, right_low)


def params(mebibytes):
    return pltpu.CompilerParams(vmem_limit_bytes=mebibytes * 1024 * 1024)


def whole(shape, dtype=f32):
    return jax.ShapeDtypeStruct(shape, dtype)


def smem():
    return pl.BlockSpec(memory_space=pltpu.SMEM)


def vmem():
    return pl.BlockSpec(memory_space=pltpu.VMEM)


def anywhere():
    return pl.BlockSpec(memory_space=pl.ANY)


def cost(macs, size):
    return pl.CostEstimate(flops=2 * macs, bytes_accessed=size, transcendentals=0)


def folded(level, inv_ref, rhs_ref):
    mat_re, mat_im = inv_ref[level, 0], inv_ref[level, 1]
    coef_re, coef_im = rhs_ref[0, level, 0], rhs_ref[0, level, 1]
    group = mat_re.shape[-1]
    lane = lax.broadcasted_iota(jnp.int32, mat_re.shape, 1)

    def differences(mat):
        low_side = jnp.where(lane == 0, 0.0, pltpu.roll(mat, 1, 1))
        high_side = jnp.where(lane == group - 1, 0.0, pltpu.roll(mat, group - 1, 1))
        return low_side + high_side - 2.0 * mat

    diff_re, diff_im = differences(mat_re), differences(mat_im)
    inner_re = mat_re + coef_re * diff_re - coef_im * diff_im
    inner_im = mat_im + coef_re * diff_im + coef_im * diff_re
    scaled_re = coef_re * mat_re - coef_im * mat_im
    scaled_im = coef_re * mat_im + coef_im * mat_re
    return inner_re, inner_im, scaled_re, scaled_im


def store_left(high_ref, low_ref, index, mat_re, mat_im):
    group = mat_re.shape[-1]
    blocks = ((mat_re, -mat_im), (mat_im, mat_re))
    for i in range(2):
        for j in range(2):
            where = (index, slice(i * group, (i + 1) * group), slice(j * group, (j + 1) * group))
            high_ref[where], low_ref[where] = halves(blocks[i][j])


def left_table_kernel(rhs_ref, inv_ref, couple_ref, high_ref, low_ref, edge_ref):
    levels, _, group, _ = inv_ref.shape
    for level in range(levels):
        inner_re, inner_im, scaled_re, scaled_im = folded(level, inv_ref, rhs_ref)
        store_left(high_ref, low_ref, level, inner_re, inner_im)
        for part, scaled in enumerate((scaled_re, scaled_im)):
            rows = slice(part * group, (part + 1) * group)
            edge_ref[level, 0, rows, :] = jnp.broadcast_to(scaled[:, 0:1], (group, group))
            edge_ref[level, 1, rows, :] = jnp.broadcast_to(scaled[:, group - 1 : group], (group, group))
    store_left(high_ref, low_ref, levels, couple_ref[0], couple_ref[1])


def right_table_kernel(rhs_ref, inv_ref, couple_ref, high_ref, low_ref, edge_ref):
    levels, _, group, _ = inv_ref.shape
    for level in range(levels + 1):
        if level < levels:
            inner_re, inner_im, scaled_re, scaled_im = folded(level, inv_ref, rhs_ref)
            scaled_re, scaled_im = scaled_re.T, scaled_im.T
            for side, row in enumerate((0, group - 1)):
                edge_re, edge_im = scaled_re[row : row + 1], scaled_im[row : row + 1]
                edge_ref[level, 2 * side : 2 * side + 1, :] = jnp.concatenate([edge_re, edge_im], axis=1)
                edge_ref[level, 2 * side + 1 : 2 * side + 2, :] = jnp.concatenate([-edge_im, edge_re], axis=1)
        else:
            inner_re, inner_im = couple_ref[0], couple_ref[1]
        turned_re, turned_im = inner_re.T, inner_im.T
        store_left(high_ref, low_ref, level, turned_re, -turned_im)


def make_tables(kernel, rhs, inv_table, couple_table, edge_shape):
    levels, _, group, _ = inv_table.shape
    shape = whole((levels + 1, 2 * group, 2 * group), bf16)
    return pl.pallas_call(
        kernel,
        out_shape=[shape, shape, whole(edge_shape)],
        in_specs=[smem(), vmem(), vmem()],
        out_specs=[vmem()] * 3,
        compiler_params=params(16),
        cost_estimate=cost(10**10, 4 * 1024 * 1024),
    )(rhs, inv_table, couple_table)


def edge_row_kernel(place_ref, field_ref, row_ref, held, sem):
    rows = field_ref.shape[2]
    odd = place_ref[0] % 2
    start = pl.multiple_of(odd * (rows - 8), 8)
    copy = pltpu.make_async_copy(field_ref.at[0, :, pl.ds(start, 8), :], held, sem)
    copy.start()
    copy.wait()
    for part in range(2):
        row_ref[0, part] = jnp.where(odd == 1, held[part, 7:8, :], held[part, 0:1, :])


def edge_row(place, field):
    length = field.shape[3]
    return pl.pallas_call(
        edge_row_kernel,
        out_shape=whole((1, 2, 1, length)),
        in_specs=[smem(), anywhere()],
        out_specs=vmem(),
        scratch_shapes=[pltpu.VMEM((2, 8, length), f32), pltpu.SemaphoreType.DMA],
        compiler_params=params(60),
        cost_estimate=cost(10**10, 1024 * 1024),
    )(place, field)


def line_groups(read, level_of, tables, low, high, following, below, above, write):
    high_ref, low_ref, edge_ref = tables
    last = high_ref.shape[0] - 1
    couple = (high_ref[last], low_ref[last])
    for k in reversed(range(low, high)):
        level = level_of(k)
        value_re, value_im = read(k)
        group = value_re.shape[1]
        solved = product(halves(jnp.concatenate([value_re, value_im], axis=1)), (high_ref[level], low_ref[level]))
        if following is not None:
            solved = solved + product(following, couple)
        before = [item[:, group - 1 : group] for item in read(k - 1)] if k > low else below
        for side, column in ((0, before), (1, above)):
            if column is not None:
                for part in range(2):
                    row = edge_ref[level, 2 * side + part : 2 * side + part + 1, :]
                    solved = solved + column[part] * row
        write(k, solved)
        following = halves(solved)
        above = [value_re[:, 0:1], value_im[:, 0:1]]


def rows_with_halo(field_ref, halo_ref, part, columns, halo_columns):
    row = jnp.broadcast_to(halo_ref[0, part, :, halo_columns], (8, columns.stop - columns.start))
    return jnp.concatenate([field_ref[0, part, :, columns], row], axis=0)


def first_pass_kernel(place_ref, index_ref, field_ref, beside_ref, halo_ref, high_ref, low_ref, edge_ref, *refs,
                      half, group, block):
    if half:
        carry_ref, keep_ref, send_ref, own = None, refs[1], refs[2], refs[3]
        state_ref = refs[0]
    else:
        carry_ref, _, keep_ref, send_ref, own = refs
        state_ref = None
    width = field_ref.shape[-1]
    count = width // group
    low = half * count
    core = place_ref[0] % 2

    def read(k):
        columns = slice((k - low) * group, (k - low + 1) * group)
        wide = slice(k * group, (k + 1) * group)
        return [rows_with_halo(field_ref, halo_ref, part, columns, wide) for part in range(2)]

    inside = slice(0, group)
    wide = slice((low - 1) * group, low * group) if half else slice(count * group, (count + 1) * group)
    beyond = [rows_with_halo(beside_ref, halo_ref, part, inside, wide) for part in range(2)]
    if half:
        below, above, following = [item[:, group - 1 : group] for item in beyond], None, None
    else:
        below, above, following = None, [item[:, 0:1] for item in beyond], halves(carry_ref[...])

    def write(k, solved):
        start = (k - low) * group
        b, inner = start // block, start % block
        own[b % 2, b // 2, 0, :, inner : inner + group] = solved[:, :group]
        own[b % 2, b // 2, 1, :, inner : inner + group] = solved[:, group:]
        if half and k == low:
            state_ref[...] = solved

    line_groups(
        read, lambda k: index_ref[0, k], (high_ref, low_ref, edge_ref), low, low + count, following, below, above, write
    )
    keep_ref[...] = own[core]
    send_ref[...] = own[1 - core]


def first_pass(place, recv_index, field, halo, tables, half, carry, after, block, group):
    rows, length = field.shape[2:]
    width = length // 2
    lines = rows + 8
    count = width // group
    shape = (width // (2 * block), 2, lines, block)
    beside = count - 1 if half else count
    args = [place, recv_index, field, field, halo, *tables]
    specs = [
        smem(), smem(),
        pl.BlockSpec((1, 2, rows, width), lambda i: (0, 0, 0, half)),
        pl.BlockSpec((1, 2, rows, group), lambda i: (0, 0, 0, beside)),
    ] + [vmem()] * 4
    outs = [whole(shape)] * 2
    if half:
        outs = [whole((lines, 2 * group))] + outs
    else:
        args += [carry, after]
        specs += [vmem(), anywhere()]
    return pl.pallas_call(
        functools.partial(first_pass_kernel, half=half, group=group, block=block),
        grid=(1,),
        out_shape=outs,
        in_specs=specs,
        out_specs=[vmem()] * len(outs),
        scratch_shapes=[pltpu.VMEM((2,) + shape, f32)],
        compiler_params=params(36),
        cost_estimate=cost(lines * width * group * 24, 8 * lines * width * 2),
    )(*args)


def add_edge(solved, edge_ref, level, side, row_re, row_im):
    group = edge_ref.shape[-1]
    wide = row_re.shape[-1]
    column = [edge_ref[level, side, part * group : (part + 1) * group, :] for part in range(2)]
    if wide > group:
        column = [jnp.concatenate([item] * (wide // group), axis=1) for item in column]
    term_re = column[0] * row_re - column[1] * row_im
    term_im = column[0] * row_im + column[1] * row_re
    both = jnp.concatenate([term_re, term_im], axis=0)
    return both if solved is None else solved + both


def second_groups(chip, groups, index_ref, tables):
    high_ref, low_ref, edge_ref = tables
    last = high_ref.shape[0] - 1
    couple = (high_ref[last], low_ref[last])
    base = chip * groups
    total = index_ref.shape[1]

    def open_state(row_re, row_im):
        after = base + groups
        level = index_ref[1, jnp.minimum(after, total - 1)]
        inside = jnp.where(after < total, 1.0, 0.0)
        return add_edge(None, edge_ref, level, 0, row_re * inside, row_im * inside)

    def step(k, value, following, before, after):
        level = index_ref[1, base + k]
        solved = product((high_ref[level], low_ref[level]), value)
        solved = solved + product(couple, following)
        if before is not None:
            solved = add_edge(solved, edge_ref, level, 0, *before)
        if after is not None:
            solved = add_edge(solved, edge_ref, level, 1, *after)
        return solved

    return open_state, step


def first_row(value, group):
    return value[0:1], value[group : group + 1]


def last_row(value, group):
    return value[group - 1 : group], value[2 * group - 1 : 2 * group]


def open_sweep_kernel(place_ref, index_ref, high_ref, low_ref, edge_ref, keep_ref, come_ref, _, near_ref, far_ref, local_ref,
                      base_ref, pair, *, groups, group):
    device = place_ref[0]
    chip, core = device // 2, device % 2
    tables = (high_ref, low_ref, edge_ref)
    last = high_ref.shape[0] - 1
    couple = (high_ref[last], low_ref[last])
    half = groups // 2
    lines = half * group
    width = keep_ref.shape[-1]

    def rows(upper, start, count):
        mine = upper == core
        return [
            jnp.where(mine, keep_ref[0, part, start : start + count, :], come_ref[0, part, start : start + count, :])
            for part in range(2)
        ]

    def store_pair(where, value):
        for sub in range(2):
            pair[sub, where, :] = value[:, sub * (width // 2) : (sub + 1) * (width // 2)]

    def given(k):
        return rows(k // half, (k % half) * group, group)

    open_state, step = second_groups(chip, groups, index_ref, tables)
    above = [item[0:1] for item in rows(1, lines, 8)]
    solved = following = state = None
    value = given(groups - 1)
    earlier = None
    for k in reversed(range(groups)):
        level = index_ref[0, chip * groups + k]
        below_value = given(k - 1) if k else None
        before = [item[group - 1 : group] for item in below_value] if k else [item[0:1] for item in rows(0, lines, 8)]
        now = product((high_ref[level], low_ref[level]), halves(jnp.concatenate(value, axis=0)))
        if following is not None:
            now = now + product(couple, following)
        now = add_edge(now, edge_ref, level, 0, *before)
        now = add_edge(now, edge_ref, level, 1, *above)
        above = [item[0:1] for item in value]
        value = below_value
        base_ref[k // half, k % half] = now[:group, (k % half) * group : (k % half + 1) * group]
        if k == groups - 1:
            row_re, row_im = last_row(now, group)
            store_pair(
                slice(4 * group, 4 * group + 8),
                jnp.concatenate([row_re, row_im, jnp.zeros((6, width), f32)], axis=0),
            )
            state = halves(open_state(row_re, row_im))
        else:
            done = step(k + 1, following, state, last_row(now, group), first_row(earlier, group) if earlier is not None else None)
            local_ref[k + 1] = done
            state = halves(done)
        earlier = solved
        solved = now
        following = halves(now)
    done = step(0, following, state, None, first_row(earlier, group))
    local_ref[0] = done
    store_pair(slice(0, 2 * group), solved)
    store_pair(slice(2 * group, 4 * group), done)
    near_ref[...] = pair[chip % 2]
    far_ref[...] = pair[1 - chip % 2]


def power_kernel(index_ref, high_ref, low_ref, edge_ref, _, power_high, power_low, chip_high, chip_low, *, groups, group):
    last = high_ref.shape[0] - 1
    couple = (high_ref[last], low_ref[last])
    rows = lax.broadcasted_iota(jnp.int32, (2 * group, group), 0)
    columns = lax.broadcasted_iota(jnp.int32, (2 * group, group), 1)
    values = [None] * groups + [(rows == columns).astype(f32)]
    split = [None] * groups
    for k in reversed(range(groups)):
        values[k] = product(couple, halves(values[k + 1]))
        split[k] = halves(values[k])
        store_left(power_high, power_low, k, values[k][:group], values[k][group:])
    for q in range(chip_high.shape[0]):

        def store(k, done, q=q):
            if k == 0:
                store_left(chip_high, chip_low, q, done[:group], done[group:])

        linear_part(q + 1, groups, group, index_ref, (high_ref, low_ref, edge_ref), values, split, store)


def own_map_kernel(place_ref, index_ref, high_ref, low_ref, edge_ref, power_high, power_low, _, map_high, map_low,
                   *, groups, group):
    rows = lax.broadcasted_iota(jnp.int32, (2 * group, group), 0)
    columns = lax.broadcasted_iota(jnp.int32, (2 * group, group), 1)
    split = [(power_high[k, :, 0:group], power_low[k, :, 0:group]) for k in range(groups)]
    values = [high.astype(f32) + low.astype(f32) for high, low in split]
    values.append((rows == columns).astype(f32))

    def store(k, done):
        store_left(map_high, map_low, k, done[:group], done[group:])

    linear_part(place_ref[0] // 2, groups, group, index_ref, (high_ref, low_ref, edge_ref), values, split, store)


def linear_part(chip, groups, group, index_ref, tables, values, split, store):
    open_state, step = second_groups(chip, groups, index_ref, tables)
    state = halves(open_state(*last_row(values[groups - 1], group)))
    for k in reversed(range(groups)):
        before = last_row(values[k - 1], group) if k else None
        done = step(k, split[k], state, before, first_row(values[k + 1], group))
        state = halves(done)
        store(k, done)


def scan_kernel(place_ref, high_ref, low_ref, power_high, power_low, chip_high, chip_low, *refs, chips, group):
    pieces, outs, (held, rows) = refs[:chips], refs[-chips - 2 : -2], refs[-2:]
    chip = place_ref[0] // 2
    last = high_ref.shape[0] - 1
    size = 4 * group
    for offset in range(chips):
        held[chip ^ offset] = pieces[offset][...]
    keep = (power_high[0], power_low[0])
    rows[0] = jnp.zeros_like(rows[0])
    for q in range(chips - 1, 0, -1):
        first = halves(held[q, 0 : 2 * group, :])
        for part in range(2):
            tail = slice((part + 1) * group - 16, (part + 1) * group)
            row = product((high_ref[last, tail, :], low_ref[last, tail, :]), first)[15:16]
            rows[q, part : part + 1, :] = held[q - 1, size + part : size + part + 1, :] + row
        if q > 1:
            second = halves(held[q, 2 * group : size, :])
            held[q - 1, 0 : 2 * group, :] = held[q - 1, 0 : 2 * group, :] + product(keep, first)
            held[q - 1, 2 * group : size, :] = (
                held[q - 1, 2 * group : size, :]
                + product((chip_high[q - 2], chip_low[q - 2]), first)
                + product(keep, second)
            )
    held[0] = jnp.zeros_like(held[0])
    for offset in range(chips):
        target = chip ^ offset
        outs[offset][0:size, :] = held[(target + 1) % chips, 0:size, :]
        outs[offset][size : size + 8, :] = rows[target]


def close_sweep_kernel(place_ref, index_ref, edge_ref, power_high, power_low, map_high, map_low, local_ref, base_ref,
                       near_ref, far_ref, _, own_ref, other_ref, image_ref, pair, result, *, groups, group, part_of, second_pair):
    device = place_ref[0]
    chip, core = device // 2, device % 2
    pair[chip % 2] = near_ref[...]
    pair[1 - chip % 2] = far_ref[...]

    def carried(start, count):
        return jnp.concatenate([pair[0, start : start + count, :], pair[1, start : start + count, :]], axis=1)

    first = halves(carried(0, 2 * group))
    second = halves(carried(2 * group, 2 * group))
    half = groups // 2
    for k in reversed(range(groups)):
        done = local_ref[k] + (
            product((map_high[k], map_low[k]), first) + product((power_high[k], power_low[k]), second)
        )
        if k == 0:
            level = index_ref[1, chip * groups]
            base = 4 * group
            done = add_edge(done, edge_ref, level, 0, carried(base, 8)[0:1], carried(base, 8)[1:2])
        rows = slice((k % half) * group, (k % half + 1) * group)
        result[k // half, 0, rows, :] = done[:group]
        result[k // half, 1, rows, :] = done[group:]
    own_ref[...] = result[core]
    other_ref[...] = result[1 - core]
    image_ref[...] = jnp.zeros_like(image_ref)

    @pl.when((chip // 2 == part_of) & ((chip % 2) ^ (chip // 2) == second_pair))
    def _():
        for i in range(half):
            k = core * half + i
            columns = slice(i * group, (i + 1) * group)
            square = base_ref[core, i] + product(
                (power_high[k, 0:group, :], power_low[k, 0:group, :]), [item[:, columns] for item in first]
            )
            image_ref[:, columns] = diagonal_of(square)


def diagonal_of(square):
    rows = lax.broadcasted_iota(jnp.int32, square.shape, 0)
    columns = lax.broadcasted_iota(jnp.int32, square.shape, 1)
    return jnp.sum(jnp.where(rows == columns, square, 0.0), axis=0, keepdims=True)


def last_pass_kernel(place_ref, index_ref, high_ref, low_ref, edge_ref, *refs, half, step, group):
    owns, comes = refs[0:2], refs[2:4]
    if half:
        out_ref, state_ref, column_ref, image_ref, field, result, sems = refs[4:]
    else:
        carry_ref, beside_ref, _, *images = refs[4:-5]
        out_ref, image_ref, field, result, sems = refs[-5:]
    device = place_ref[0]
    chip, core = device // 2, device % 2
    block = owns[0].shape[-1]
    width = field.shape[-1]
    count = width // group
    low = half * count
    for second_pair in range(2):
        for ref, side in ((owns[second_pair], core), (comes[second_pair], 1 - core)):
            start = pl.multiple_of(((chip // 2 ^ second_pair) * 2 + side) * block, block)
            for part in range(2):
                field[part, :, pl.ds(start, block)] = ref[part]
    first = count + 1 if half else 0
    copies = []

    def read(k):
        return [field[part, :, (k - low) * group : (k - low + 1) * group] for part in range(2)]

    def write(k, solved):
        if half and k == low:
            state_ref[...] = solved
            return
        where = k - first
        result[where, 0] = solved[:, :group]
        result[where, 1] = solved[:, group:]
        copy = pltpu.make_async_copy(
            result.at[where], out_ref.at[0, :, :, k * group : (k + 1) * group], sems.at[where]
        )
        copy.start()
        copies.append(copy)

    tables = (high_ref, low_ref, edge_ref)
    following, above = None, None
    if half:
        for part, value in enumerate(read(low)):
            column_ref[part] = jnp.broadcast_to(value[:, 0:1], column_ref.shape[1:])
    else:
        level = index_ref[step, count]
        solved = carry_ref[...]
        for part, value in enumerate(read(count - 1)):
            solved = solved + value[:, group - 1 : group] * edge_ref[level, part : part + 1, :]
        write(count, solved)
        following = halves(solved)
        above = [beside_ref[part, :, 0:1] for part in range(2)]
    line_groups(read, lambda k: index_ref[step, k], tables, low, low + count, following, None, above, write)
    if half:
        image_ref[...] = jnp.zeros_like(image_ref)
    else:
        image_ref[1:2] = images[0][...]
        image_ref[0:1] = sum((item[...] for item in images[2:]), images[1][...])
    row = image_ref.shape[0] - 1
    for i in range(block // group):
        mine = device * (block // group) + i
        here = mine > count if half else mine <= count

        @pl.when(here)
        def _():
            square = result[jnp.where(here, mine - first, 0), 0, i * group : (i + 1) * group, :]
            image_ref[row : row + 1, i * group : (i + 1) * group] = diagonal_of(square)

    for copy in copies:
        copy.wait()


def last_pass(place, recv_index, tables, owns, comes, half, passed, shape, step, group):
    rows, length = shape[2:]
    width = length // 2
    count = width // group
    block = owns[0].shape[-1]
    args = [place, recv_index, *tables, *owns, *comes]
    any_space = pl.BlockSpec(memory_space=pl.ANY)
    specs = [smem()] * 2 + [vmem()] * 7
    outs = [whole(shape)]
    out_specs = [any_space]
    aliases = {}
    results = count - 1 if half else count + 1
    if half:
        outs += [whole((rows, 2 * group)), whole((2, rows, group))]
        out_specs += [vmem()] * 2
    else:
        migrated, state, column, *images = passed
        args += [state, column, migrated, *images]
        specs += [vmem(), vmem(), any_space] + [vmem()] * len(images)
        aliases = {len(args) - 1 - len(images): 0}
    return pl.pallas_call(
        functools.partial(last_pass_kernel, half=half, step=step, group=group),
        out_shape=outs + [whole((1 if half else 2, block))],
        in_specs=specs,
        out_specs=out_specs + [vmem()],
        scratch_shapes=[
            pltpu.VMEM((2, rows, width), f32),
            pltpu.VMEM((results, 2, rows, group), f32),
            pltpu.SemaphoreType.DMA((results,)),
        ],
        input_output_aliases=aliases,
        compiler_params=params(24),
        cost_estimate=cost(rows * width * group * 24, 8 * rows * width * 2),
    )(*args)


def sum_over(value, axis, count):
    reach = 1
    while reach < count:
        value = value + lax.ppermute(value, axis, [(i, i ^ reach) for i in range(count)])
        reach *= 2
    return value


def fast_shards(wavefield, inv_table, couple_table, rhs_table, recv_index, shot_index, *, devices, freqs):
    levels, _, group, _ = inv_table.shape[1:]
    rows, _ = wavefield.shape[2:]
    block = rows
    chips = devices // 2
    groups = 2 * rows // group
    device = lax.axis_index("plane")
    place = device.reshape(1).astype(jnp.int32)
    double = 2 * group
    partner = [(d, d ^ 1) for d in range(devices)]

    edge = edge_row(place, wavefield)
    swap = [(d, d + 1) for d in range(1, devices - 1, 2)] + [(d + 1, d) for d in range(1, devices - 1, 2)]
    halo = lax.ppermute(edge, "plane", swap)
    right = make_tables(right_table_kernel, rhs_table, inv_table[0], couple_table[0], (levels, 4, double))

    left = make_tables(left_table_kernel, rhs_table, inv_table[0], couple_table[0], (levels, 2, double, group))

    wide = block // 2
    piece = whole((4 * group + 8, wide))
    local = whole((groups, double, block))
    base = whole((2, groups // 2, group, group))
    matrices = whole((groups, double, double), bf16)
    middle = whole((chips - 2, double, double), bf16)
    powers = []

    def make_powers(ready):
        powers.extend(
            pl.pallas_call(
                functools.partial(power_kernel, groups=groups, group=group),
                out_shape=[matrices] * 2 + [middle] * 2,
                in_specs=[smem()] + [vmem()] * 3 + [anywhere()],
                out_specs=[vmem()] * 4,
                compiler_params=params(20),
                cost_estimate=cost(groups * group * group * group * 64, 4 * 1024 * 1024),
            )(shot_index, *left, ready)
        )
        return powers[0]

    keep, come = {}, {}
    locals_, bases, theirs = {}, {}, {}

    def first(half, carry, ready):
        result = first_pass(place, recv_index, wavefield, halo, right, half, carry, ready, block, group)
        *carry, keep[half], send = result
        come[half] = lax.ppermute(send, "plane", partner)
        return carry

    def open_sweep(half, second_pair, ready):
        spec = pltpu.PrefetchScalarGridSpec(
            num_scalar_prefetch=2,
            grid=(1,),
            in_specs=[vmem()] * 3
            + [pl.BlockSpec((1,) + keep[half].shape[1:], lambda i, at, _: ((at[0] // 4) ^ second_pair, 0, 0, 0))] * 2
            + [anywhere()],
            out_specs=[vmem()] * 4,
            scratch_shapes=[pltpu.VMEM((2,) + piece.shape, f32)],
        )
        name = "%d_%d" % (half, second_pair)
        near, far, locals_[name], bases[name] = pl.pallas_call(
            functools.partial(open_sweep_kernel, groups=groups, group=group),
            grid_spec=spec,
            out_shape=[piece, piece, local, base],
            compiler_params=params(24),
            cost_estimate=cost(groups * group * block * group * 48, 8 * groups * group * block * 3),
        )(place, shot_index, *left, keep[half], come[half], ready)
        for offset, item in ((2 * second_pair + 1, far), (2 * second_pair, near)):
            moves = [(d, d ^ (2 * offset)) for d in range(devices)]
            theirs[half, offset] = lax.ppermute(item, "plane", moves) if offset else item
        return near

    (carry,) = first(1, None, None)
    after = open_sweep(1, 1, carry)
    first(0, carry, after)
    after = open_sweep(1, 0, keep[0])
    after = open_sweep(0, 1, after)
    after = open_sweep(0, 0, after)
    after = make_powers(after)
    power_high, power_low, chip_high, chip_low = powers
    came = {}
    for half in (1, 0):
        carries = pl.pallas_call(
            functools.partial(scan_kernel, chips=chips, group=group),
            out_shape=[piece] * chips,
            in_specs=[smem()] + [vmem()] * (6 + chips) + [anywhere()],
            out_specs=[vmem()] * chips,
            scratch_shapes=[pltpu.VMEM((chips,) + piece.shape, f32), pltpu.VMEM((chips, 8, wide), f32)],
            compiler_params=params(20),
            cost_estimate=cost(3 * group * group * wide * 24, 4 * 1024 * 1024),
        )(place, left[0], left[1], power_high, power_low, chip_high, chip_low, *[theirs[half, o] for o in range(chips)], after)
        after = carries[0]
        if half:
            map_high, map_low = pl.pallas_call(
                functools.partial(own_map_kernel, groups=groups, group=group),
                out_shape=[matrices] * 2,
                in_specs=[smem()] * 2 + [vmem()] * 5 + [anywhere()],
                out_specs=[vmem()] * 2,
                compiler_params=params(20),
                cost_estimate=cost(groups * group * group * group * 32, 4 * 1024 * 1024),
            )(place, shot_index, *left, power_high, power_low, after)
            after = map_high
        for offset in (3, 1, 2, 0):
            moves = [(d, d ^ (2 * offset)) for d in range(devices)]
            came[half, offset] = lax.ppermute(carries[offset], "plane", moves) if offset else carries[0]

    images, image_last = [], None
    passed = None
    part = whole((2, rows, block))
    for half in (1, 0):
        owns, comes = [], []
        for second_pair in (0, 1):
            name = "%d_%d" % (half, second_pair)
            own, other, image = pl.pallas_call(
                functools.partial(
                    close_sweep_kernel, groups=groups, group=group, part_of=half, second_pair=second_pair
                ),
                out_shape=[part, part, whole((1, block))],
                in_specs=[smem()] * 2 + [vmem()] * 9 + [anywhere()],
                out_specs=[vmem()] * 3,
                scratch_shapes=[pltpu.VMEM((2,) + piece.shape, f32), pltpu.VMEM((2, 2, rows, block), f32)],
                compiler_params=params(20),
                cost_estimate=cost(groups * group * block * group * 24, 8 * groups * group * block * 2),
            )(
                place, shot_index, left[2], power_high, power_low, map_high, map_low, locals_[name], bases[name],
                came[half, 2 * second_pair], came[half, 2 * second_pair + 1], after,
            )
            after = image
            owns.append(own)
            comes.append(lax.ppermute(other, "plane", partner))
            images.append(image)
        if not half:
            passed = [*passed, image_last, *images]
        *passed, image_last = last_pass(place, recv_index, right, owns, comes, half, passed, wavefield.shape, 1, group)
        after = image_last
    image_last = sum_over(image_last, "freq", freqs)
    return passed[0], image_last


def solution(mesh):
    placed = (
        P("freq", None, "plane", None),
        P("freq", None, None, None, None),
        P("freq", None, None, None),
        P("freq", None, None),
        P(),
        P(),
    )
    devices = mesh.shape["plane"]
    freqs = mesh.shape["freq"]

    def body(*arrays):
        if devices == 8 and arrays[0].shape[2] == 2 * GROUP and arrays[0].shape[0] == 1 and freqs & (freqs - 1) == 0:
            return fast_shards(*arrays, devices=devices, freqs=freqs)
        return shards(*arrays)

    return jax.shard_map(
        body,
        mesh=mesh,
        in_specs=placed,
        out_specs=(P("freq", None, "plane", None), P(None, "plane")),
        check_vma=False,
    )
```

```python
import functools

import jax
import jax.numpy as jnp
from jax import lax
from jax.experimental import pallas as pl
from jax.experimental.pallas import tpu as pltpu
from jax.sharding import PartitionSpec as P

NX = 2048
GROUP = 128
DEPTHS = 2


highest = lax.Precision.HIGHEST


def complex_product(form, mat_re, mat_im, vec_re, vec_im):
    real_part = jnp.einsum(form, mat_re, vec_re, precision=highest) - jnp.einsum(
        form, mat_im, vec_im, precision=highest
    )
    imag_part = jnp.einsum(form, mat_re, vec_im, precision=highest) + jnp.einsum(
        form, mat_im, vec_re, precision=highest
    )
    return (real_part, imag_part)


def select_rows(index, table):
    levels = jnp.arange(table.shape[1], dtype=jnp.int32)
    one_hot = (index[:, None] == levels[None, :]).astype(jnp.float32)
    return jnp.einsum("kv,fv...->fk...", one_hot, table, precision=highest)


def coupling_powers(couple_table, group_count):
    power_re = couple_table[:, 0]
    power_im = couple_table[:, 1]
    powers = []
    reach = 1
    while reach < group_count:
        powers.append((power_re, power_im))
        power_re, power_im = complex_product("fab,fbc->fac", power_re, power_im, power_re, power_im)
        reach = reach * 2
    return powers


def shifted_up(values, reach, group_axis):
    count = values.shape[group_axis]
    kept = lax.slice_in_dim(values, reach, count, axis=group_axis)
    zero_shape = list(values.shape)
    zero_shape[group_axis] = reach
    return jnp.concatenate([kept, jnp.zeros(zero_shape, values.dtype)], axis=group_axis)


def line_pass(wave_field, index, inv_table, rhs_table, powers, along_last):
    line_axis = 3 if along_last else 2
    freqs = wave_field.shape[0]
    length = wave_field.shape[line_axis]
    group_count = length // GROUP
    inv_sel = select_rows(index, inv_table)
    rhs_sel = select_rows(index, rhs_table)
    pad_widths = [(0, 0), (0, 0), (0, 0), (0, 0)]
    pad_widths[line_axis] = (1, 1)
    padded = jnp.pad(wave_field, pad_widths)
    beside = lax.slice_in_dim(padded, 0, length, axis=line_axis) + lax.slice_in_dim(
        padded, 2, length + 2, axis=line_axis
    )
    second = beside - 2.0 * wave_field
    if along_last:
        shape = (freqs, wave_field.shape[2], group_count, GROUP)
        coef_re = rhs_sel[:, None, :, 0, None]
        coef_im = rhs_sel[:, None, :, 1, None]
        local_form = "fkab,flkb->flka"
        power_form = "fab,flkb->flka"
        group_axis = 2
    else:
        shape = (freqs, group_count, GROUP, wave_field.shape[3])
        coef_re = rhs_sel[:, :, 0, None, None]
        coef_im = rhs_sel[:, :, 1, None, None]
        local_form = "fkab,fkbm->fkam"
        power_form = "fab,fkbm->fkam"
        group_axis = 1
    base_re = wave_field[:, 0].reshape(shape)
    base_im = wave_field[:, 1].reshape(shape)
    second_re = second[:, 0].reshape(shape)
    second_im = second[:, 1].reshape(shape)
    source_re = base_re + coef_re * second_re - coef_im * second_im
    source_im = base_im + coef_re * second_im + coef_im * second_re
    solved_re, solved_im = complex_product(
        local_form, inv_sel[:, :, 0], inv_sel[:, :, 1], source_re, source_im
    )
    reach = 1
    for power_re, power_im in powers:
        add_re, add_im = complex_product(
            power_form,
            power_re,
            power_im,
            shifted_up(solved_re, reach, group_axis),
            shifted_up(solved_im, reach, group_axis),
        )
        solved_re = solved_re + add_re
        solved_im = solved_im + add_im
        reach = reach * 2
    out_shape = (freqs,) + wave_field.shape[2:]
    return jnp.stack([solved_re.reshape(out_shape), solved_im.reshape(out_shape)], axis=1)


def to_columns(wave_field):
    return lax.all_to_all(wave_field, "plane", split_axis=3, concat_axis=2, tiled=True)


def to_rows(wave_field):
    return lax.all_to_all(wave_field, "plane", split_axis=2, concat_axis=3, tiled=True)


def diagonal_rows(wave_field, first_row):
    count = wave_field.shape[2]
    block = lax.dynamic_slice_in_dim(wave_field[:, 0], first_row, count, axis=2)
    return jnp.sum(jnp.diagonal(block, axis1=1, axis2=2), axis=0)


def diagonal_columns(wave_field, first_row):
    count = wave_field.shape[3]
    block = lax.dynamic_slice_in_dim(wave_field[:, 0], first_row, count, axis=1)
    return jnp.sum(jnp.diagonal(block, axis1=1, axis2=2), axis=0)


def image_part(partial_value):
    return lax.psum(partial_value, "freq")


def shards(wavefield, inv_table, couple_table, rhs_table, recv_index, shot_index):
    powers = coupling_powers(couple_table, NX // GROUP)
    row_count = wavefield.shape[2]
    first_row = lax.axis_index("plane") * row_count
    wave_field = wavefield
    parts = []
    for step_index in range(DEPTHS):
        if step_index % 2 == 0:
            wave_field = line_pass(
                wave_field, recv_index[step_index], inv_table, rhs_table, powers, True
            )
            wave_field = to_columns(wave_field)
            wave_field = line_pass(
                wave_field, shot_index[step_index], inv_table, rhs_table, powers, False
            )
            parts.append(image_part(diagonal_columns(wave_field, first_row)))
        else:
            wave_field = line_pass(
                wave_field, shot_index[step_index], inv_table, rhs_table, powers, False
            )
            wave_field = to_rows(wave_field)
            wave_field = line_pass(
                wave_field, recv_index[step_index], inv_table, rhs_table, powers, True
            )
            parts.append(image_part(diagonal_rows(wave_field, first_row)))
    stacked = jnp.stack(parts)
    return (wave_field, stacked)


f32 = jnp.float32
bf16 = jnp.bfloat16


def halves(value):
    high = value.astype(bf16)
    low = (value - high.astype(f32)).astype(bf16)
    return high, low


def mul(left, right):
    return jnp.dot(left, right, preferred_element_type=f32)


def product(left, right):
    (left_high, left_low), (right_high, right_low) = left, right
    return mul(left_high, right_high) + mul(left_low, right_high) + mul(left_high, right_low)


def params(mebibytes):
    return pltpu.CompilerParams(vmem_limit_bytes=mebibytes * 1024 * 1024)


def whole(shape, dtype=f32):
    return jax.ShapeDtypeStruct(shape, dtype)


def smem():
    return pl.BlockSpec(memory_space=pltpu.SMEM)


def vmem():
    return pl.BlockSpec(memory_space=pltpu.VMEM)


def anywhere():
    return pl.BlockSpec(memory_space=pl.ANY)


def cost(macs, size):
    return pl.CostEstimate(flops=2 * macs, bytes_accessed=size, transcendentals=0)


def folded(level, inv_ref, rhs_ref):
    mat_re, mat_im = inv_ref[level, 0], inv_ref[level, 1]
    coef_re, coef_im = rhs_ref[0, level, 0], rhs_ref[0, level, 1]
    group = mat_re.shape[-1]
    lane = lax.broadcasted_iota(jnp.int32, mat_re.shape, 1)

    def differences(mat):
        low_side = jnp.where(lane == 0, 0.0, pltpu.roll(mat, 1, 1))
        high_side = jnp.where(lane == group - 1, 0.0, pltpu.roll(mat, group - 1, 1))
        return low_side + high_side - 2.0 * mat

    diff_re, diff_im = differences(mat_re), differences(mat_im)
    inner_re = mat_re + coef_re * diff_re - coef_im * diff_im
    inner_im = mat_im + coef_re * diff_im + coef_im * diff_re
    scaled_re = coef_re * mat_re - coef_im * mat_im
    scaled_im = coef_re * mat_im + coef_im * mat_re
    return inner_re, inner_im, scaled_re, scaled_im


def store_left(high_ref, low_ref, index, mat_re, mat_im):
    group = mat_re.shape[-1]
    blocks = ((mat_re, -mat_im), (mat_im, mat_re))
    for i in range(2):
        for j in range(2):
            where = (index, slice(i * group, (i + 1) * group), slice(j * group, (j + 1) * group))
            high_ref[where], low_ref[where] = halves(blocks[i][j])


def left_table_kernel(rhs_ref, inv_ref, couple_ref, high_ref, low_ref, edge_ref):
    levels, _, group, _ = inv_ref.shape
    for level in range(levels):
        inner_re, inner_im, scaled_re, scaled_im = folded(level, inv_ref, rhs_ref)
        store_left(high_ref, low_ref, level, inner_re, inner_im)
        for part, scaled in enumerate((scaled_re, scaled_im)):
            rows = slice(part * group, (part + 1) * group)
            edge_ref[level, 0, rows, :] = jnp.broadcast_to(scaled[:, 0:1], (group, group))
            edge_ref[level, 1, rows, :] = jnp.broadcast_to(scaled[:, group - 1 : group], (group, group))
    store_left(high_ref, low_ref, levels, couple_ref[0], couple_ref[1])


def right_table_kernel(rhs_ref, inv_ref, couple_ref, high_ref, low_ref, edge_ref):
    levels, _, group, _ = inv_ref.shape
    for level in range(levels + 1):
        if level < levels:
            inner_re, inner_im, scaled_re, scaled_im = folded(level, inv_ref, rhs_ref)
            scaled_re, scaled_im = scaled_re.T, scaled_im.T
            for side, row in enumerate((0, group - 1)):
                edge_re, edge_im = scaled_re[row : row + 1], scaled_im[row : row + 1]
                edge_ref[level, 2 * side : 2 * side + 1, :] = jnp.concatenate([edge_re, edge_im], axis=1)
                edge_ref[level, 2 * side + 1 : 2 * side + 2, :] = jnp.concatenate([-edge_im, edge_re], axis=1)
        else:
            inner_re, inner_im = couple_ref[0], couple_ref[1]
        turned_re, turned_im = inner_re.T, inner_im.T
        store_left(high_ref, low_ref, level, turned_re, -turned_im)


def make_tables(kernel, rhs, inv_table, couple_table, edge_shape):
    levels, _, group, _ = inv_table.shape
    shape = whole((levels + 1, 2 * group, 2 * group), bf16)
    return pl.pallas_call(
        kernel,
        out_shape=[shape, shape, whole(edge_shape)],
        in_specs=[smem(), vmem(), vmem()],
        out_specs=[vmem()] * 3,
        compiler_params=params(16),
        cost_estimate=cost(10**10, 4 * 1024 * 1024),
    )(rhs, inv_table, couple_table)


def edge_row_kernel(place_ref, field_ref, row_ref, held, sem):
    rows = field_ref.shape[2]
    odd = place_ref[0] % 2
    start = pl.multiple_of(odd * (rows - 8), 8)
    copy = pltpu.make_async_copy(field_ref.at[0, :, pl.ds(start, 8), :], held, sem)
    copy.start()
    copy.wait()
    for part in range(2):
        row_ref[0, part] = jnp.where(odd == 1, held[part, 7:8, :], held[part, 0:1, :])


def edge_row(place, field):
    length = field.shape[3]
    return pl.pallas_call(
        edge_row_kernel,
        out_shape=whole((1, 2, 1, length)),
        in_specs=[smem(), anywhere()],
        out_specs=vmem(),
        scratch_shapes=[pltpu.VMEM((2, 8, length), f32), pltpu.SemaphoreType.DMA],
        compiler_params=params(60),
        cost_estimate=cost(10**10, 1024 * 1024),
    )(place, field)


def line_groups(read, level_of, tables, low, high, following, below, above, write):
    high_ref, low_ref, edge_ref = tables
    last = high_ref.shape[0] - 1
    couple = (high_ref[last], low_ref[last])
    for k in reversed(range(low, high)):
        level = level_of(k)
        value_re, value_im = read(k)
        group = value_re.shape[1]
        solved = product(halves(jnp.concatenate([value_re, value_im], axis=1)), (high_ref[level], low_ref[level]))
        if following is not None:
            solved = solved + product(following, couple)
        before = [item[:, group - 1 : group] for item in read(k - 1)] if k > low else below
        for side, column in ((0, before), (1, above)):
            if column is not None:
                for part in range(2):
                    row = edge_ref[level, 2 * side + part : 2 * side + part + 1, :]
                    solved = solved + column[part] * row
        write(k, solved)
        following = halves(solved)
        above = [value_re[:, 0:1], value_im[:, 0:1]]


def rows_with_halo(field_ref, halo_ref, part, columns, halo_columns):
    row = jnp.broadcast_to(halo_ref[0, part, :, halo_columns], (8, columns.stop - columns.start))
    return jnp.concatenate([field_ref[0, part, :, columns], row], axis=0)


def first_pass_kernel(place_ref, index_ref, field_ref, beside_ref, halo_ref, high_ref, low_ref, edge_ref, *refs,
                      half, group, block):
    if half:
        carry_ref, keep_ref, send_ref, own = None, refs[1], refs[2], refs[3]
        state_ref = refs[0]
    else:
        carry_ref, _, keep_ref, send_ref, own = refs
        state_ref = None
    width = field_ref.shape[-1]
    count = width // group
    low = half * count
    core = place_ref[0] % 2

    def read(k):
        columns = slice((k - low) * group, (k - low + 1) * group)
        wide = slice(k * group, (k + 1) * group)
        return [rows_with_halo(field_ref, halo_ref, part, columns, wide) for part in range(2)]

    inside = slice(0, group)
    wide = slice((low - 1) * group, low * group) if half else slice(count * group, (count + 1) * group)
    beyond = [rows_with_halo(beside_ref, halo_ref, part, inside, wide) for part in range(2)]
    if half:
        below, above, following = [item[:, group - 1 : group] for item in beyond], None, None
    else:
        below, above, following = None, [item[:, 0:1] for item in beyond], halves(carry_ref[...])

    def write(k, solved):
        start = (k - low) * group
        b, inner = start // block, start % block
        own[b % 2, b // 2, 0, :, inner : inner + group] = solved[:, :group]
        own[b % 2, b // 2, 1, :, inner : inner + group] = solved[:, group:]
        if half and k == low:
            state_ref[...] = solved

    line_groups(
        read, lambda k: index_ref[0, k], (high_ref, low_ref, edge_ref), low, low + count, following, below, above, write
    )
    keep_ref[...] = own[core]
    send_ref[...] = own[1 - core]


def first_pass(place, recv_index, field, halo, tables, half, carry, after, block, group):
    rows, length = field.shape[2:]
    width = length // 2
    lines = rows + 8
    count = width // group
    shape = (width // (2 * block), 2, lines, block)
    beside = count - 1 if half else count
    args = [place, recv_index, field, field, halo, *tables]
    specs = [
        smem(), smem(),
        pl.BlockSpec((1, 2, rows, width), lambda i: (0, 0, 0, half)),
        pl.BlockSpec((1, 2, rows, group), lambda i: (0, 0, 0, beside)),
    ] + [vmem()] * 4
    outs = [whole(shape)] * 2
    if half:
        outs = [whole((lines, 2 * group))] + outs
    else:
        args += [carry, after]
        specs += [vmem(), anywhere()]
    return pl.pallas_call(
        functools.partial(first_pass_kernel, half=half, group=group, block=block),
        grid=(1,),
        out_shape=outs,
        in_specs=specs,
        out_specs=[vmem()] * len(outs),
        scratch_shapes=[pltpu.VMEM((2,) + shape, f32)],
        compiler_params=params(36),
        cost_estimate=cost(lines * width * group * 24, 8 * lines * width * 2),
    )(*args)


def add_edge(solved, edge_ref, level, side, row_re, row_im):
    group = edge_ref.shape[-1]
    wide = row_re.shape[-1]
    column = [edge_ref[level, side, part * group : (part + 1) * group, :] for part in range(2)]
    if wide > group:
        column = [jnp.concatenate([item] * (wide // group), axis=1) for item in column]
    term_re = column[0] * row_re - column[1] * row_im
    term_im = column[0] * row_im + column[1] * row_re
    both = jnp.concatenate([term_re, term_im], axis=0)
    return both if solved is None else solved + both


def second_groups(chip, groups, index_ref, tables):
    high_ref, low_ref, edge_ref = tables
    last = high_ref.shape[0] - 1
    couple = (high_ref[last], low_ref[last])
    base = chip * groups
    total = index_ref.shape[1]

    def open_state(row_re, row_im):
        after = base + groups
        level = index_ref[1, jnp.minimum(after, total - 1)]
        inside = jnp.where(after < total, 1.0, 0.0)
        return add_edge(None, edge_ref, level, 0, row_re * inside, row_im * inside)

    def step(k, value, following, before, after):
        level = index_ref[1, base + k]
        solved = product((high_ref[level], low_ref[level]), value)
        solved = solved + product(couple, following)
        if before is not None:
            solved = add_edge(solved, edge_ref, level, 0, *before)
        if after is not None:
            solved = add_edge(solved, edge_ref, level, 1, *after)
        return solved

    return open_state, step


def first_row(value, group):
    return value[0:1], value[group : group + 1]


def last_row(value, group):
    return value[group - 1 : group], value[2 * group - 1 : 2 * group]


def open_sweep_kernel(place_ref, index_ref, high_ref, low_ref, edge_ref, keep_ref, come_ref, _, near_ref, far_ref, local_ref,
                      base_ref, pair, *, groups, group):
    device = place_ref[0]
    chip, core = device // 2, device % 2
    tables = (high_ref, low_ref, edge_ref)
    last = high_ref.shape[0] - 1
    couple = (high_ref[last], low_ref[last])
    half = groups // 2
    lines = half * group
    width = keep_ref.shape[-1]

    def rows(upper, start, count):
        mine = upper == core
        return [
            jnp.where(mine, keep_ref[0, part, start : start + count, :], come_ref[0, part, start : start + count, :])
            for part in range(2)
        ]

    def store_pair(where, value):
        for sub in range(2):
            pair[sub, where, :] = value[:, sub * (width // 2) : (sub + 1) * (width // 2)]

    def given(k):
        return rows(k // half, (k % half) * group, group)

    open_state, step = second_groups(chip, groups, index_ref, tables)
    above = [item[0:1] for item in rows(1, lines, 8)]
    solved = following = state = None
    value = given(groups - 1)
    earlier = None
    for k in reversed(range(groups)):
        level = index_ref[0, chip * groups + k]
        below_value = given(k - 1) if k else None
        before = [item[group - 1 : group] for item in below_value] if k else [item[0:1] for item in rows(0, lines, 8)]
        now = product((high_ref[level], low_ref[level]), halves(jnp.concatenate(value, axis=0)))
        if following is not None:
            now = now + product(couple, following)
        now = add_edge(now, edge_ref, level, 0, *before)
        now = add_edge(now, edge_ref, level, 1, *above)
        above = [item[0:1] for item in value]
        value = below_value
        base_ref[k // half, k % half] = now[:group, (k % half) * group : (k % half + 1) * group]
        if k == groups - 1:
            row_re, row_im = last_row(now, group)
            store_pair(
                slice(4 * group, 4 * group + 8),
                jnp.concatenate([row_re, row_im, jnp.zeros((6, width), f32)], axis=0),
            )
            state = halves(open_state(row_re, row_im))
        else:
            done = step(k + 1, following, state, last_row(now, group), first_row(earlier, group) if earlier is not None else None)
            local_ref[k + 1] = done
            state = halves(done)
        earlier = solved
        solved = now
        following = halves(now)
    done = step(0, following, state, None, first_row(earlier, group))
    local_ref[0] = done
    store_pair(slice(0, 2 * group), solved)
    store_pair(slice(2 * group, 4 * group), done)
    near_ref[...] = pair[chip % 2]
    far_ref[...] = pair[1 - chip % 2]


def unit_rows(group):
    rows = lax.broadcasted_iota(jnp.int32, (group, 2 * group), 0)
    columns = lax.broadcasted_iota(jnp.int32, (group, 2 * group), 1)
    return (rows == columns).astype(f32)


def store_turned(high_ref, low_ref, index, turned):
    group = turned.shape[0]
    store_left(high_ref, low_ref, index, turned[:, :group].T, turned[:, group:].T)


def power_kernel(index_ref, high_ref, low_ref, edge_ref, _, power_high, power_low, turned_ref, chip_high, chip_low,
                 *, groups, group):
    tables = (high_ref, low_ref, edge_ref)
    last = high_ref.shape[0] - 1
    couple = (high_ref[last], low_ref[last])
    values = [None] * groups + [unit_rows(group)]
    for k in reversed(range(groups)):
        values[k] = product(halves(values[k + 1]), couple)
        store_turned(power_high, power_low, k, values[k])
        turned_ref[k] = values[k]
    split = [halves(value) for value in values]
    for q in range(chip_high.shape[0]):

        def store(k, done, q=q):
            if k == 0:
                store_turned(chip_high, chip_low, q, done)

        linear_part(q + 1, groups, group, index_ref, tables, values, split, store)


def own_map_kernel(place_ref, index_ref, high_ref, low_ref, edge_ref, turned_ref, _, map_high, map_low, *, groups, group):
    values = [turned_ref[k] for k in range(groups)] + [unit_rows(group)]
    split = [halves(value) for value in values]

    def store(k, done):
        store_turned(map_high, map_low, k, done)

    linear_part(place_ref[0] // 2, groups, group, index_ref, (high_ref, low_ref, edge_ref), values, split, store)


def linear_part(chip, groups, group, index_ref, tables, values, split, store):
    high_ref, low_ref, edge_ref = tables
    last = high_ref.shape[0] - 1
    couple = (high_ref[last], low_ref[last])
    base, total = chip * groups, index_ref.shape[1]

    def edge(level, side, column_re, column_im):
        rows = [edge_ref[level, 2 * side + part : 2 * side + part + 1, :] for part in range(2)]
        return column_re * rows[0] + column_im * rows[1]

    def first_column(value):
        return value[:, 0:1], value[:, group : group + 1]

    def last_column(value):
        return value[:, group - 1 : group], value[:, 2 * group - 1 : 2 * group]

    after = base + groups
    inside = jnp.where(after < total, 1.0, 0.0)
    done = edge(index_ref[1, jnp.minimum(after, total - 1)], 0, *last_column(values[groups - 1])) * inside
    for k in reversed(range(groups)):
        level = index_ref[1, base + k]
        done = product(split[k], (high_ref[level], low_ref[level])) + product(halves(done), couple)
        if k:
            done = done + edge(level, 0, *last_column(values[k - 1]))
        done = done + edge(level, 1, *first_column(values[k + 1]))
        store(k, done)


def scan_kernel(place_ref, high_ref, low_ref, power_high, power_low, chip_high, chip_low, *refs, chips, group):
    pieces, outs, (held, rows) = refs[:chips], refs[-chips - 2 : -2], refs[-2:]
    chip = place_ref[0] // 2
    last = high_ref.shape[0] - 1
    size = 4 * group
    for offset in range(chips):
        held[chip ^ offset] = pieces[offset][...]
    keep = (power_high[0], power_low[0])
    rows[0] = jnp.zeros_like(rows[0])
    for q in range(chips - 1, 0, -1):
        first = halves(held[q, 0 : 2 * group, :])
        for part in range(2):
            tail = slice((part + 1) * group - 16, (part + 1) * group)
            row = product((high_ref[last, tail, :], low_ref[last, tail, :]), first)[15:16]
            rows[q, part : part + 1, :] = held[q - 1, size + part : size + part + 1, :] + row
        if q > 1:
            second = halves(held[q, 2 * group : size, :])
            held[q - 1, 0 : 2 * group, :] = held[q - 1, 0 : 2 * group, :] + product(keep, first)
            held[q - 1, 2 * group : size, :] = (
                held[q - 1, 2 * group : size, :]
                + product((chip_high[q - 2], chip_low[q - 2]), first)
                + product(keep, second)
            )
    held[0] = jnp.zeros_like(held[0])
    for offset in range(chips):
        target = chip ^ offset
        outs[offset][0:size, :] = held[(target + 1) % chips, 0:size, :]
        outs[offset][size : size + 8, :] = rows[target]


def close_sweep_kernel(place_ref, index_ref, edge_ref, power_high, power_low, map_high, map_low, local_ref, base_ref,
                       near_ref, far_ref, _, out_ref, *refs, groups, group, part_of, second_pair):
    image_ref, pair = refs if len(refs) == 2 else (None, refs[0])
    device = place_ref[0]
    chip, core = device // 2, device % 2
    side = core if image_ref is not None else 1 - core
    pair[chip % 2] = near_ref[...]
    pair[1 - chip % 2] = far_ref[...]

    def carried(start, count):
        return jnp.concatenate([pair[0, start : start + count, :], pair[1, start : start + count, :]], axis=1)

    first = halves(carried(0, 2 * group))
    second = halves(carried(2 * group, 2 * group))
    half = groups // 2
    for i in reversed(range(half)):
        k = side * half + i
        done = local_ref[k] + (
            product((map_high[k], map_low[k]), first) + product((power_high[k], power_low[k]), second)
        )
        if i == 0:
            level = index_ref[1, chip * groups]
            inside = jnp.where(side == 0, 1.0, 0.0)
            rows = carried(4 * group, 8) * inside
            done = add_edge(done, edge_ref, level, 0, rows[0:1], rows[1:2])
        out_ref[0, i * group : (i + 1) * group, :] = done[:group]
        out_ref[1, i * group : (i + 1) * group, :] = done[group:]
    if image_ref is None:
        return
    image_ref[...] = jnp.zeros_like(image_ref)

    @pl.when((chip // 2 == part_of) & ((chip % 2) ^ (chip // 2) == second_pair))
    def _():
        for i in range(half):
            k = core * half + i
            columns = slice(i * group, (i + 1) * group)
            square = base_ref[core, i] + product(
                (power_high[k, 0:group, :], power_low[k, 0:group, :]), [item[:, columns] for item in first]
            )
            image_ref[:, columns] = diagonal_of(square)


def diagonal_of(square):
    rows = lax.broadcasted_iota(jnp.int32, square.shape, 0)
    columns = lax.broadcasted_iota(jnp.int32, square.shape, 1)
    return jnp.sum(jnp.where(rows == columns, square, 0.0), axis=0, keepdims=True)


def last_pass_kernel(place_ref, index_ref, high_ref, low_ref, edge_ref, *refs, half, step, group):
    owns, comes = refs[0:2], refs[2:4]
    if half:
        out_ref, state_ref, column_ref, image_ref, result, sems = refs[4:]
    else:
        carry_ref, beside_ref, *images = refs[4:-2]
        result, image_ref = refs[-2:]
    device = place_ref[0]
    chip, core = device // 2, device % 2
    block = owns[0].shape[-1]
    count = 4 * block // group
    low = half * count
    first = count + 1 if half else 0
    copies = []

    ready = {}

    def read(k):
        if k not in ready:
            q, inner = (k - low) * group // block, (k - low) * group % block
            columns = slice(inner, inner + group)
            ready[k] = [
                jnp.where(chip // 2 == q // 2, *(
                    jnp.where(core == q % 2, owns[item][part, :, columns], comes[item][part, :, columns])
                    for item in range(2)
                ))
                for part in range(2)
            ]
        return ready[k]

    def write(k, solved):
        if half and k == low:
            state_ref[...] = solved
            return
        where = k - first
        result[where, 0] = solved[:, :group]
        result[where, 1] = solved[:, group:]
        if not half:
            return
        copy = pltpu.make_async_copy(
            result.at[where], out_ref.at[0, :, :, k * group : (k + 1) * group], sems.at[where]
        )
        copy.start()
        copies.append(copy)

    tables = (high_ref, low_ref, edge_ref)
    following, above = None, None
    if half:
        for part, value in enumerate(read(low)):
            column_ref[part] = jnp.broadcast_to(value[:, 0:1], column_ref.shape[1:])
    else:
        level = index_ref[step, count]
        solved = carry_ref[...]
        for part, value in enumerate(read(count - 1)):
            solved = solved + value[:, group - 1 : group] * edge_ref[level, part : part + 1, :]
        write(count, solved)
        following = halves(solved)
        above = [beside_ref[part, :, 0:1] for part in range(2)]
    line_groups(read, lambda k: index_ref[step, k], tables, low, low + count, following, None, above, write)
    if half:
        image_ref[...] = jnp.zeros_like(image_ref)
    else:
        image_ref[1:2] = images[0][...]
        image_ref[0:1] = sum((item[...] for item in images[2:]), images[1][...])
    row = image_ref.shape[0] - 1
    for i in range(block // group):
        mine = device * (block // group) + i
        here = mine > count if half else mine <= count

        @pl.when(here)
        def _():
            square = result[jnp.where(here, mine - first, 0), 0, i * group : (i + 1) * group, :]
            image_ref[row : row + 1, i * group : (i + 1) * group] = diagonal_of(square)

    for copy in copies:
        copy.wait()


def last_pass(place, recv_index, tables, owns, comes, half, passed, shape, step, group):
    rows, length = shape[2:]
    width = length // 2
    count = width // group
    block = owns[0].shape[-1]
    args = [place, recv_index, *tables, *owns, *comes]
    specs = [smem()] * 2 + [vmem()] * 7
    results = whole((count - 1 if half else count + 1, 2, rows, group))
    scratch = []
    if half:
        outs = [whole(shape), whole((rows, 2 * group)), whole((2, rows, group))]
        out_specs = [anywhere(), vmem(), vmem()]
        scratch = [pltpu.VMEM(results.shape, f32), pltpu.SemaphoreType.DMA((count - 1,))]
    else:
        args += passed
        specs += [vmem()] * len(passed)
        outs = [results]
        out_specs = [vmem()]
    return pl.pallas_call(
        functools.partial(last_pass_kernel, half=half, step=step, group=group),
        out_shape=outs + [whole((1 if half else 2, block))],
        in_specs=specs,
        out_specs=out_specs + [vmem()],
        scratch_shapes=scratch,
        compiler_params=params(24),
        cost_estimate=cost(rows * width * group * 24, 8 * rows * width * 2),
    )(*args)


def store_kernel(groups_ref, _, out_ref, sems):
    group = groups_ref.shape[-1]
    copies = [
        pltpu.make_async_copy(groups_ref.at[k], out_ref.at[0, :, :, k * group : (k + 1) * group], sems.at[k])
        for k in range(groups_ref.shape[0])
    ]
    for copy in copies:
        copy.start()
    for copy in copies:
        copy.wait()


def store_groups(pieces, migrated):
    return pl.pallas_call(
        store_kernel,
        out_shape=whole(migrated.shape),
        in_specs=[anywhere(), anywhere()],
        out_specs=anywhere(),
        scratch_shapes=[pltpu.SemaphoreType.DMA((pieces.shape[0],))],
        input_output_aliases={1: 0},
        cost_estimate=cost(0, 8 * 1024 * 1024),
        compiler_params=params(4),
    )(pieces, migrated)


def sum_over(value, axis, count):
    reach = 1
    while reach < count:
        value = value + lax.ppermute(value, axis, [(i, i ^ reach) for i in range(count)])
        reach *= 2
    return value


def fast_shards(wavefield, inv_table, couple_table, rhs_table, recv_index, shot_index, *, devices, freqs):
    levels, _, group, _ = inv_table.shape[1:]
    rows, _ = wavefield.shape[2:]
    block = rows
    chips = devices // 2
    groups = 2 * rows // group
    device = lax.axis_index("plane")
    place = device.reshape(1).astype(jnp.int32)
    double = 2 * group
    partner = [(d, d ^ 1) for d in range(devices)]

    edge = edge_row(place, wavefield)
    swap = [(d, d + 1) for d in range(1, devices - 1, 2)] + [(d + 1, d) for d in range(1, devices - 1, 2)]
    halo = lax.ppermute(edge, "plane", swap)
    right = make_tables(right_table_kernel, rhs_table, inv_table[0], couple_table[0], (levels, 4, double))

    left = make_tables(left_table_kernel, rhs_table, inv_table[0], couple_table[0], (levels, 2, double, group))

    wide = block // 2
    piece = whole((4 * group + 8, wide))
    local = whole((groups, double, block))
    base = whole((2, groups // 2, group, group))
    matrices = whole((groups, double, double), bf16)
    middle = whole((chips - 2, double, double), bf16)
    powers = []

    def make_powers(ready):
        powers.extend(
            pl.pallas_call(
                functools.partial(power_kernel, groups=groups, group=group),
                out_shape=[matrices] * 2 + [whole((groups, group, double))] + [middle] * 2,
                in_specs=[smem()] + [vmem()] * 3 + [anywhere()],
                out_specs=[vmem()] * 5,
                compiler_params=params(20),
                cost_estimate=cost(groups * group * group * group * 64, 4 * 1024 * 1024),
            )(shot_index, *right, ready)
        )
        return powers[0]

    keep, come = {}, {}
    locals_, bases, theirs = {}, {}, {}

    def first(half, carry, ready):
        result = first_pass(place, recv_index, wavefield, halo, right, half, carry, ready, block, group)
        *carry, keep[half], send = result
        come[half] = lax.ppermute(send, "plane", partner)
        return carry

    def open_sweep(half, second_pair, ready):
        spec = pltpu.PrefetchScalarGridSpec(
            num_scalar_prefetch=2,
            grid=(1,),
            in_specs=[vmem()] * 3
            + [pl.BlockSpec((1,) + keep[half].shape[1:], lambda i, at, _: ((at[0] // 4) ^ second_pair, 0, 0, 0))] * 2
            + [anywhere()],
            out_specs=[vmem()] * 4,
            scratch_shapes=[pltpu.VMEM((2,) + piece.shape, f32)],
        )
        name = "%d_%d" % (half, second_pair)
        near, far, locals_[name], bases[name] = pl.pallas_call(
            functools.partial(open_sweep_kernel, groups=groups, group=group),
            grid_spec=spec,
            out_shape=[piece, piece, local, base],
            compiler_params=params(24),
            cost_estimate=cost(groups * group * block * group * 48, 8 * groups * group * block * 3),
        )(place, shot_index, *left, keep[half], come[half], ready)
        for offset, item in ((2 * second_pair + 1, far), (2 * second_pair, near)):
            moves = [(d, d ^ (2 * offset)) for d in range(devices)]
            theirs[half, offset] = lax.ppermute(item, "plane", moves) if offset else item
        return near

    (carry,) = first(1, None, None)
    after = open_sweep(1, 1, carry)
    first(0, carry, after)
    after = open_sweep(1, 0, keep[0])
    after = open_sweep(0, 1, after)
    after = open_sweep(0, 0, after)
    after = make_powers(after)
    power_high, power_low, power_turned, chip_high, chip_low = powers
    came = {}
    for half in (1, 0):
        carries = pl.pallas_call(
            functools.partial(scan_kernel, chips=chips, group=group),
            out_shape=[piece] * chips,
            in_specs=[smem()] + [vmem()] * (6 + chips) + [anywhere()],
            out_specs=[vmem()] * chips,
            scratch_shapes=[pltpu.VMEM((chips,) + piece.shape, f32), pltpu.VMEM((chips, 8, wide), f32)],
            compiler_params=params(20),
            cost_estimate=cost(3 * group * group * wide * 24, 4 * 1024 * 1024),
        )(place, left[0], left[1], power_high, power_low, chip_high, chip_low, *[theirs[half, o] for o in range(chips)], after)
        after = carries[0]
        if half:
            map_high, map_low = pl.pallas_call(
                functools.partial(own_map_kernel, groups=groups, group=group),
                out_shape=[matrices] * 2,
                in_specs=[smem()] * 2 + [vmem()] * 4 + [anywhere()],
                out_specs=[vmem()] * 2,
                compiler_params=params(20),
                cost_estimate=cost(groups * group * group * group * 32, 4 * 1024 * 1024),
            )(place, shot_index, *right, power_turned, after)
            after = map_high
        for offset in (3, 1, 2, 0):
            moves = [(d, d ^ (2 * offset)) for d in range(devices)]
            came[half, offset] = lax.ppermute(carries[offset], "plane", moves) if offset else carries[0]

    images, image_last = [], None
    passed = None
    part = whole((2, rows, block))
    for half in (1, 0):
        owns, comes = [], []
        for second_pair in (0, 1):
            name = "%d_%d" % (half, second_pair)
            for kind in ("far", "near"):
                outs = [part] + ([whole((1, block))] if kind == "near" else [])
                result = pl.pallas_call(
                    functools.partial(
                        close_sweep_kernel, groups=groups, group=group, part_of=half, second_pair=second_pair
                    ),
                    out_shape=outs,
                    in_specs=[smem()] * 2 + [vmem()] * 9 + [anywhere()],
                    out_specs=[vmem()] * len(outs),
                    scratch_shapes=[pltpu.VMEM((2,) + piece.shape, f32)],
                    compiler_params=params(20),
                    cost_estimate=cost(groups * group * block * group * 12, 4 * groups * group * block * 2),
                )(
                    place, shot_index, left[2], power_high, power_low, map_high, map_low, locals_[name], bases[name],
                    came[half, 2 * second_pair], came[half, 2 * second_pair + 1], after,
                )
                after = result[-1]
                if kind == "far":
                    comes.append(lax.ppermute(result[0], "plane", partner))
            owns.append(result[0])
            images.append(result[1])
        if not half:
            migrated, *passed = *passed, image_last, *images
        *passed, image_last = last_pass(place, recv_index, right, owns, comes, half, passed, wavefield.shape, 1, group)
        after = image_last
    migrated = store_groups(passed[0], migrated)
    image_last = sum_over(image_last, "freq", freqs)
    return migrated, image_last


def solution(mesh):
    placed = (
        P("freq", None, "plane", None),
        P("freq", None, None, None, None),
        P("freq", None, None, None),
        P("freq", None, None),
        P(),
        P(),
    )
    devices = mesh.shape["plane"]
    freqs = mesh.shape["freq"]

    def body(*arrays):
        if devices == 8 and arrays[0].shape[2] == 2 * GROUP and arrays[0].shape[0] == 1 and freqs & (freqs - 1) == 0:
            return fast_shards(*arrays, devices=devices, freqs=freqs)
        return shards(*arrays)

    return jax.shard_map(
        body,
        mesh=mesh,
        in_specs=placed,
        out_specs=(P("freq", None, "plane", None), P(None, "plane")),
        check_vma=False,
    )
```

```python
import functools

import jax
import jax.numpy as jnp
from jax import lax
from jax.experimental import pallas as pl
from jax.experimental.pallas import tpu as pltpu
from jax.sharding import PartitionSpec as P

NX = 2048
GROUP = 128
DEPTHS = 2


highest = lax.Precision.HIGHEST


def complex_product(form, mat_re, mat_im, vec_re, vec_im):
    real_part = jnp.einsum(form, mat_re, vec_re, precision=highest) - jnp.einsum(
        form, mat_im, vec_im, precision=highest
    )
    imag_part = jnp.einsum(form, mat_re, vec_im, precision=highest) + jnp.einsum(
        form, mat_im, vec_re, precision=highest
    )
    return (real_part, imag_part)


def select_rows(index, table):
    levels = jnp.arange(table.shape[1], dtype=jnp.int32)
    one_hot = (index[:, None] == levels[None, :]).astype(jnp.float32)
    return jnp.einsum("kv,fv...->fk...", one_hot, table, precision=highest)


def coupling_powers(couple_table, group_count):
    power_re = couple_table[:, 0]
    power_im = couple_table[:, 1]
    powers = []
    reach = 1
    while reach < group_count:
        powers.append((power_re, power_im))
        power_re, power_im = complex_product("fab,fbc->fac", power_re, power_im, power_re, power_im)
        reach = reach * 2
    return powers


def shifted_up(values, reach, group_axis):
    count = values.shape[group_axis]
    kept = lax.slice_in_dim(values, reach, count, axis=group_axis)
    zero_shape = list(values.shape)
    zero_shape[group_axis] = reach
    return jnp.concatenate([kept, jnp.zeros(zero_shape, values.dtype)], axis=group_axis)


def line_pass(wave_field, index, inv_table, rhs_table, powers, along_last):
    line_axis = 3 if along_last else 2
    freqs = wave_field.shape[0]
    length = wave_field.shape[line_axis]
    group_count = length // GROUP
    inv_sel = select_rows(index, inv_table)
    rhs_sel = select_rows(index, rhs_table)
    pad_widths = [(0, 0), (0, 0), (0, 0), (0, 0)]
    pad_widths[line_axis] = (1, 1)
    padded = jnp.pad(wave_field, pad_widths)
    beside = lax.slice_in_dim(padded, 0, length, axis=line_axis) + lax.slice_in_dim(
        padded, 2, length + 2, axis=line_axis
    )
    second = beside - 2.0 * wave_field
    if along_last:
        shape = (freqs, wave_field.shape[2], group_count, GROUP)
        coef_re = rhs_sel[:, None, :, 0, None]
        coef_im = rhs_sel[:, None, :, 1, None]
        local_form = "fkab,flkb->flka"
        power_form = "fab,flkb->flka"
        group_axis = 2
    else:
        shape = (freqs, group_count, GROUP, wave_field.shape[3])
        coef_re = rhs_sel[:, :, 0, None, None]
        coef_im = rhs_sel[:, :, 1, None, None]
        local_form = "fkab,fkbm->fkam"
        power_form = "fab,fkbm->fkam"
        group_axis = 1
    base_re = wave_field[:, 0].reshape(shape)
    base_im = wave_field[:, 1].reshape(shape)
    second_re = second[:, 0].reshape(shape)
    second_im = second[:, 1].reshape(shape)
    source_re = base_re + coef_re * second_re - coef_im * second_im
    source_im = base_im + coef_re * second_im + coef_im * second_re
    solved_re, solved_im = complex_product(
        local_form, inv_sel[:, :, 0], inv_sel[:, :, 1], source_re, source_im
    )
    reach = 1
    for power_re, power_im in powers:
        add_re, add_im = complex_product(
            power_form,
            power_re,
            power_im,
            shifted_up(solved_re, reach, group_axis),
            shifted_up(solved_im, reach, group_axis),
        )
        solved_re = solved_re + add_re
        solved_im = solved_im + add_im
        reach = reach * 2
    out_shape = (freqs,) + wave_field.shape[2:]
    return jnp.stack([solved_re.reshape(out_shape), solved_im.reshape(out_shape)], axis=1)


def to_columns(wave_field):
    return lax.all_to_all(wave_field, "plane", split_axis=3, concat_axis=2, tiled=True)


def to_rows(wave_field):
    return lax.all_to_all(wave_field, "plane", split_axis=2, concat_axis=3, tiled=True)


def diagonal_rows(wave_field, first_row):
    count = wave_field.shape[2]
    block = lax.dynamic_slice_in_dim(wave_field[:, 0], first_row, count, axis=2)
    return jnp.sum(jnp.diagonal(block, axis1=1, axis2=2), axis=0)


def diagonal_columns(wave_field, first_row):
    count = wave_field.shape[3]
    block = lax.dynamic_slice_in_dim(wave_field[:, 0], first_row, count, axis=1)
    return jnp.sum(jnp.diagonal(block, axis1=1, axis2=2), axis=0)


def image_part(partial_value):
    return lax.psum(partial_value, "freq")


def shards(wavefield, inv_table, couple_table, rhs_table, recv_index, shot_index):
    powers = coupling_powers(couple_table, NX // GROUP)
    row_count = wavefield.shape[2]
    first_row = lax.axis_index("plane") * row_count
    wave_field = wavefield
    parts = []
    for step_index in range(DEPTHS):
        if step_index % 2 == 0:
            wave_field = line_pass(
                wave_field, recv_index[step_index], inv_table, rhs_table, powers, True
            )
            wave_field = to_columns(wave_field)
            wave_field = line_pass(
                wave_field, shot_index[step_index], inv_table, rhs_table, powers, False
            )
            parts.append(image_part(diagonal_columns(wave_field, first_row)))
        else:
            wave_field = line_pass(
                wave_field, shot_index[step_index], inv_table, rhs_table, powers, False
            )
            wave_field = to_rows(wave_field)
            wave_field = line_pass(
                wave_field, recv_index[step_index], inv_table, rhs_table, powers, True
            )
            parts.append(image_part(diagonal_rows(wave_field, first_row)))
    stacked = jnp.stack(parts)
    return (wave_field, stacked)


f32 = jnp.float32
bf16 = jnp.bfloat16


def halves(value):
    high = value.astype(bf16)
    low = (value - high.astype(f32)).astype(bf16)
    return high, low


def mul(left, right):
    return jnp.dot(left, right, preferred_element_type=f32)


def product(left, right):
    (left_high, left_low), (right_high, right_low) = left, right
    return mul(left_high, right_high) + mul(left_low, right_high) + mul(left_high, right_low)


def params(mebibytes):
    return pltpu.CompilerParams(vmem_limit_bytes=mebibytes * 1024 * 1024)


def whole(shape, dtype=f32):
    return jax.ShapeDtypeStruct(shape, dtype)


def smem():
    return pl.BlockSpec(memory_space=pltpu.SMEM)


def vmem():
    return pl.BlockSpec(memory_space=pltpu.VMEM)


def anywhere():
    return pl.BlockSpec(memory_space=pl.ANY)


def cost(macs, size):
    return pl.CostEstimate(flops=2 * macs, bytes_accessed=size, transcendentals=0)


def folded(level, inv_ref, rhs_ref):
    mat_re, mat_im = inv_ref[level, 0], inv_ref[level, 1]
    coef_re, coef_im = rhs_ref[0, level, 0], rhs_ref[0, level, 1]
    group = mat_re.shape[-1]
    lane = lax.broadcasted_iota(jnp.int32, mat_re.shape, 1)

    def differences(mat):
        low_side = jnp.where(lane == 0, 0.0, pltpu.roll(mat, 1, 1))
        high_side = jnp.where(lane == group - 1, 0.0, pltpu.roll(mat, group - 1, 1))
        return low_side + high_side - 2.0 * mat

    diff_re, diff_im = differences(mat_re), differences(mat_im)
    inner_re = mat_re + coef_re * diff_re - coef_im * diff_im
    inner_im = mat_im + coef_re * diff_im + coef_im * diff_re
    scaled_re = coef_re * mat_re - coef_im * mat_im
    scaled_im = coef_re * mat_im + coef_im * mat_re
    return inner_re, inner_im, scaled_re, scaled_im


def store_left(high_ref, low_ref, index, mat_re, mat_im):
    group = mat_re.shape[-1]
    blocks = ((mat_re, -mat_im), (mat_im, mat_re))
    for i in range(2):
        for j in range(2):
            where = (index, slice(i * group, (i + 1) * group), slice(j * group, (j + 1) * group))
            high_ref[where], low_ref[where] = halves(blocks[i][j])


def left_table_kernel(rhs_ref, inv_ref, couple_ref, high_ref, low_ref, edge_ref):
    levels, _, group, _ = inv_ref.shape
    for level in range(levels):
        inner_re, inner_im, scaled_re, scaled_im = folded(level, inv_ref, rhs_ref)
        store_left(high_ref, low_ref, level, inner_re, inner_im)
        for part, scaled in enumerate((scaled_re, scaled_im)):
            rows = slice(part * group, (part + 1) * group)
            edge_ref[level, 0, rows, :] = jnp.broadcast_to(scaled[:, 0:1], (group, group))
            edge_ref[level, 1, rows, :] = jnp.broadcast_to(scaled[:, group - 1 : group], (group, group))
    store_left(high_ref, low_ref, levels, couple_ref[0], couple_ref[1])


def right_table_kernel(rhs_ref, inv_ref, couple_ref, high_ref, low_ref, edge_ref):
    levels, _, group, _ = inv_ref.shape
    for level in range(levels + 1):
        if level < levels:
            inner_re, inner_im, scaled_re, scaled_im = folded(level, inv_ref, rhs_ref)
            scaled_re, scaled_im = scaled_re.T, scaled_im.T
            for side, row in enumerate((0, group - 1)):
                edge_re, edge_im = scaled_re[row : row + 1], scaled_im[row : row + 1]
                edge_ref[level, 2 * side : 2 * side + 1, :] = jnp.concatenate([edge_re, edge_im], axis=1)
                edge_ref[level, 2 * side + 1 : 2 * side + 2, :] = jnp.concatenate([-edge_im, edge_re], axis=1)
        else:
            inner_re, inner_im = couple_ref[0], couple_ref[1]
        turned_re, turned_im = inner_re.T, inner_im.T
        store_left(high_ref, low_ref, level, turned_re, -turned_im)


def make_tables(kernel, rhs, inv_table, couple_table, edge_shape):
    levels, _, group, _ = inv_table.shape
    shape = whole((levels + 1, 2 * group, 2 * group), bf16)
    return pl.pallas_call(
        kernel,
        out_shape=[shape, shape, whole(edge_shape)],
        in_specs=[smem(), vmem(), vmem()],
        out_specs=[vmem()] * 3,
        compiler_params=params(16),
        cost_estimate=cost(10**10, 4 * 1024 * 1024),
    )(rhs, inv_table, couple_table)


def edge_row_kernel(place_ref, field_ref, row_ref, held, sem):
    rows = field_ref.shape[2]
    odd = place_ref[0] % 2
    start = pl.multiple_of(odd * (rows - 8), 8)
    copy = pltpu.make_async_copy(field_ref.at[0, :, pl.ds(start, 8), :], held, sem)
    copy.start()
    copy.wait()
    for part in range(2):
        row_ref[0, part] = jnp.where(odd == 1, held[part, 7:8, :], held[part, 0:1, :])


def edge_row(place, field):
    length = field.shape[3]
    return pl.pallas_call(
        edge_row_kernel,
        out_shape=whole((1, 2, 1, length)),
        in_specs=[smem(), anywhere()],
        out_specs=vmem(),
        scratch_shapes=[pltpu.VMEM((2, 8, length), f32), pltpu.SemaphoreType.DMA],
        compiler_params=params(60),
        cost_estimate=cost(10**10, 1024 * 1024),
    )(place, field)


def line_groups(read, level_of, tables, low, high, following, below, above, write):
    high_ref, low_ref, edge_ref = tables
    last = high_ref.shape[0] - 1
    couple = (high_ref[last], low_ref[last])
    for k in reversed(range(low, high)):
        level = level_of(k)
        value_re, value_im = read(k)
        group = value_re.shape[1]
        solved = product(halves(jnp.concatenate([value_re, value_im], axis=1)), (high_ref[level], low_ref[level]))
        if following is not None:
            solved = solved + product(following, couple)
        before = [item[:, group - 1 : group] for item in read(k - 1)] if k > low else below
        for side, column in ((0, before), (1, above)):
            if column is not None:
                for part in range(2):
                    row = edge_ref[level, 2 * side + part : 2 * side + part + 1, :]
                    solved = solved + column[part] * row
        write(k, solved)
        following = halves(solved)
        above = [value_re[:, 0:1], value_im[:, 0:1]]


def rows_with_halo(field_ref, halo_ref, part, columns, halo_columns):
    row = jnp.broadcast_to(halo_ref[0, part, :, halo_columns], (8, columns.stop - columns.start))
    return jnp.concatenate([field_ref[0, part, :, columns], row], axis=0)


def first_pass_kernel(place_ref, index_ref, field_ref, beside_ref, halo_ref, high_ref, low_ref, edge_ref, *refs,
                      half, group, block):
    if half:
        carry_ref, keep_ref, send_ref, odd = None, refs[1], refs[2], refs[3]
        state_ref = refs[0]
    else:
        carry_ref, _, keep_ref, send_ref, odd = refs
        state_ref = None
    width = field_ref.shape[-1]
    count = width // group
    low = half * count
    core = place_ref[0] % 2

    def read(k):
        columns = slice((k - low) * group, (k - low + 1) * group)
        wide = slice(k * group, (k + 1) * group)
        return [rows_with_halo(field_ref, halo_ref, part, columns, wide) for part in range(2)]

    inside = slice(0, group)
    wide = slice((low - 1) * group, low * group) if half else slice(count * group, (count + 1) * group)
    beyond = [rows_with_halo(beside_ref, halo_ref, part, inside, wide) for part in range(2)]
    if half:
        below, above, following = [item[:, group - 1 : group] for item in beyond], None, None
    else:
        below, above, following = None, [item[:, 0:1] for item in beyond], halves(carry_ref[...])

    def write(k, solved):
        start = (k - low) * group
        b, inner = start // block, start % block
        columns = slice(inner, inner + group)
        for part in range(2):
            value = solved[:, part * group : (part + 1) * group]
            if b % 2:
                odd[b // 2, part, :, columns] = value
            else:
                other = odd[b // 2, part, :, columns]
                keep_ref[b // 2, part, :, columns] = jnp.where(core == 0, value, other)
                send_ref[b // 2, part, :, columns] = jnp.where(core == 0, other, value)
        if half and k == low:
            state_ref[...] = solved

    line_groups(
        read, lambda k: index_ref[0, k], (high_ref, low_ref, edge_ref), low, low + count, following, below, above, write
    )


def first_pass(place, recv_index, field, halo, tables, half, carry, after, block, group):
    rows, length = field.shape[2:]
    width = length // 2
    lines = rows + 8
    count = width // group
    shape = (width // (2 * block), 2, lines, block)
    beside = count - 1 if half else count
    args = [place, recv_index, field, field, halo, *tables]
    specs = [
        smem(), smem(),
        pl.BlockSpec((1, 2, rows, width), lambda i: (0, 0, 0, half)),
        pl.BlockSpec((1, 2, rows, group), lambda i: (0, 0, 0, beside)),
    ] + [vmem()] * 4
    outs = [whole(shape)] * 2
    if half:
        outs = [whole((lines, 2 * group))] + outs
    else:
        args += [carry, after]
        specs += [vmem(), anywhere()]
    return pl.pallas_call(
        functools.partial(first_pass_kernel, half=half, group=group, block=block),
        grid=(1,),
        out_shape=outs,
        in_specs=specs,
        out_specs=[vmem()] * len(outs),
        scratch_shapes=[pltpu.VMEM(shape, f32)],
        compiler_params=params(36),
        cost_estimate=cost(lines * width * group * 24, 8 * lines * width * 2),
    )(*args)


def add_edge(solved, edge_ref, level, side, row_re, row_im):
    group = edge_ref.shape[-1]
    wide = row_re.shape[-1]
    column = [edge_ref[level, side, part * group : (part + 1) * group, :] for part in range(2)]
    if wide > group:
        column = [jnp.concatenate([item] * (wide // group), axis=1) for item in column]
    term_re = column[0] * row_re - column[1] * row_im
    term_im = column[0] * row_im + column[1] * row_re
    both = jnp.concatenate([term_re, term_im], axis=0)
    return both if solved is None else solved + both


def second_groups(chip, groups, index_ref, tables):
    high_ref, low_ref, edge_ref = tables
    last = high_ref.shape[0] - 1
    couple = (high_ref[last], low_ref[last])
    base = chip * groups
    total = index_ref.shape[1]

    def open_state(row_re, row_im):
        after = base + groups
        level = index_ref[1, jnp.minimum(after, total - 1)]
        inside = jnp.where(after < total, 1.0, 0.0)
        return add_edge(None, edge_ref, level, 0, row_re * inside, row_im * inside)

    def step(k, value, following, before, after):
        level = index_ref[1, base + k]
        solved = product((high_ref[level], low_ref[level]), value)
        solved = solved + product(couple, following)
        if before is not None:
            solved = add_edge(solved, edge_ref, level, 0, *before)
        if after is not None:
            solved = add_edge(solved, edge_ref, level, 1, *after)
        return solved

    return open_state, step


def first_row(value, group):
    return value[0:1], value[group : group + 1]


def last_row(value, group):
    return value[group - 1 : group], value[2 * group - 1 : 2 * group]


def open_sweep_kernel(place_ref, index_ref, high_ref, low_ref, edge_ref, keep_ref, come_ref, _, near_ref, far_ref, local_ref,
                      base_ref, *, groups, group):
    device = place_ref[0]
    chip, core = device // 2, device % 2
    tables = (high_ref, low_ref, edge_ref)
    last = high_ref.shape[0] - 1
    couple = (high_ref[last], low_ref[last])
    half = groups // 2
    lines = half * group
    width = keep_ref.shape[-1]

    def rows(upper, start, count):
        mine = upper == core
        return [
            jnp.where(mine, keep_ref[0, part, start : start + count, :], come_ref[0, part, start : start + count, :])
            for part in range(2)
        ]

    def store_pair(where, value):
        low_side, high_side = value[:, : width // 2], value[:, width // 2 :]
        near_ref[where, :] = jnp.where(chip % 2 == 0, low_side, high_side)
        far_ref[where, :] = jnp.where(chip % 2 == 0, high_side, low_side)

    def given(k):
        return rows(k // half, (k % half) * group, group)

    open_state, step = second_groups(chip, groups, index_ref, tables)
    above = [item[0:1] for item in rows(1, lines, 8)]
    solved = following = state = None
    value = given(groups - 1)
    earlier = None
    for k in reversed(range(groups)):
        level = index_ref[0, chip * groups + k]
        below_value = given(k - 1) if k else None
        before = [item[group - 1 : group] for item in below_value] if k else [item[0:1] for item in rows(0, lines, 8)]
        now = product((high_ref[level], low_ref[level]), halves(jnp.concatenate(value, axis=0)))
        if following is not None:
            now = now + product(couple, following)
        now = add_edge(now, edge_ref, level, 0, *before)
        now = add_edge(now, edge_ref, level, 1, *above)
        above = [item[0:1] for item in value]
        value = below_value
        base_ref[k // half, k % half] = now[:group, (k % half) * group : (k % half + 1) * group]
        if k == groups - 1:
            row_re, row_im = last_row(now, group)
            store_pair(
                slice(4 * group, 4 * group + 8),
                jnp.concatenate([row_re, row_im, jnp.zeros((6, width), f32)], axis=0),
            )
            state = halves(open_state(row_re, row_im))
        else:
            done = step(k + 1, following, state, last_row(now, group), first_row(earlier, group) if earlier is not None else None)
            local_ref[k + 1] = done
            state = halves(done)
        earlier = solved
        solved = now
        following = halves(now)
    done = step(0, following, state, None, first_row(earlier, group))
    local_ref[0] = done
    store_pair(slice(0, 2 * group), solved)
    store_pair(slice(2 * group, 4 * group), done)


def unit_rows(group):
    rows = lax.broadcasted_iota(jnp.int32, (group, 2 * group), 0)
    columns = lax.broadcasted_iota(jnp.int32, (group, 2 * group), 1)
    return (rows == columns).astype(f32)


def store_turned(high_ref, low_ref, index, turned):
    group = turned.shape[0]
    store_left(high_ref, low_ref, index, turned[:, :group].T, turned[:, group:].T)


def power_kernel(index_ref, high_ref, low_ref, edge_ref, _, power_high, power_low, turned_ref, chip_high, chip_low,
                 *, groups, group):
    tables = (high_ref, low_ref, edge_ref)
    last = high_ref.shape[0] - 1
    couple = (high_ref[last], low_ref[last])
    values = [None] * groups + [unit_rows(group)]
    for k in reversed(range(groups)):
        values[k] = product(halves(values[k + 1]), couple)
        store_turned(power_high, power_low, k, values[k])
        turned_ref[k] = values[k]
    split = [halves(value) for value in values]
    for q in range(chip_high.shape[0]):

        def store(k, done, q=q):
            if k == 0:
                store_turned(chip_high, chip_low, q, done)

        linear_part(q + 1, groups, group, index_ref, tables, values, split, store)


def own_map_kernel(place_ref, index_ref, high_ref, low_ref, edge_ref, turned_ref, _, map_high, map_low, *, groups, group):
    values = [turned_ref[k] for k in range(groups)] + [unit_rows(group)]
    split = [halves(value) for value in values]

    def store(k, done):
        store_turned(map_high, map_low, k, done)

    linear_part(place_ref[0] // 2, groups, group, index_ref, (high_ref, low_ref, edge_ref), values, split, store)


def linear_part(chip, groups, group, index_ref, tables, values, split, store):
    high_ref, low_ref, edge_ref = tables
    last = high_ref.shape[0] - 1
    couple = (high_ref[last], low_ref[last])
    base, total = chip * groups, index_ref.shape[1]

    def edge(level, side, column_re, column_im):
        rows = [edge_ref[level, 2 * side + part : 2 * side + part + 1, :] for part in range(2)]
        return column_re * rows[0] + column_im * rows[1]

    def first_column(value):
        return value[:, 0:1], value[:, group : group + 1]

    def last_column(value):
        return value[:, group - 1 : group], value[:, 2 * group - 1 : 2 * group]

    after = base + groups
    inside = jnp.where(after < total, 1.0, 0.0)
    done = edge(index_ref[1, jnp.minimum(after, total - 1)], 0, *last_column(values[groups - 1])) * inside
    for k in reversed(range(groups)):
        level = index_ref[1, base + k]
        done = product(split[k], (high_ref[level], low_ref[level])) + product(halves(done), couple)
        if k:
            done = done + edge(level, 0, *last_column(values[k - 1]))
        done = done + edge(level, 1, *first_column(values[k + 1]))
        store(k, done)


def scan_kernel(place_ref, high_ref, low_ref, power_high, power_low, chip_high, chip_low, *refs, chips, group):
    pieces, outs, (held, rows) = refs[:chips], refs[-chips - 2 : -2], refs[-2:]
    chip = place_ref[0] // 2
    last = high_ref.shape[0] - 1
    size = 4 * group
    for offset in range(chips):
        held[chip ^ offset] = pieces[offset][...]
    keep = (power_high[0], power_low[0])
    rows[0] = jnp.zeros_like(rows[0])
    for q in range(chips - 1, 0, -1):
        first = halves(held[q, 0 : 2 * group, :])
        for part in range(2):
            tail = slice((part + 1) * group - 16, (part + 1) * group)
            row = product((high_ref[last, tail, :], low_ref[last, tail, :]), first)[15:16]
            rows[q, part : part + 1, :] = held[q - 1, size + part : size + part + 1, :] + row
        if q > 1:
            second = halves(held[q, 2 * group : size, :])
            held[q - 1, 0 : 2 * group, :] = held[q - 1, 0 : 2 * group, :] + product(keep, first)
            held[q - 1, 2 * group : size, :] = (
                held[q - 1, 2 * group : size, :]
                + product((chip_high[q - 2], chip_low[q - 2]), first)
                + product(keep, second)
            )
    held[0] = jnp.zeros_like(held[0])
    for offset in range(chips):
        target = chip ^ offset
        outs[offset][0:size, :] = held[(target + 1) % chips, 0:size, :]
        outs[offset][size : size + 8, :] = rows[target]


def close_sweep_kernel(place_ref, index_ref, edge_ref, power_high, power_low, map_high, map_low, local_ref, base_ref,
                       near_ref, far_ref, _, out_ref, *refs, groups, group, part_of, second_pair):
    image_ref, pair = refs if len(refs) == 2 else (None, refs[0])
    device = place_ref[0]
    chip, core = device // 2, device % 2
    side = core if image_ref is not None else 1 - core
    pair[chip % 2] = near_ref[...]
    pair[1 - chip % 2] = far_ref[...]

    def carried(start, count):
        return jnp.concatenate([pair[0, start : start + count, :], pair[1, start : start + count, :]], axis=1)

    first = halves(carried(0, 2 * group))
    second = halves(carried(2 * group, 2 * group))
    half = groups // 2
    for i in reversed(range(half)):
        k = side * half + i
        done = local_ref[k] + (
            product((map_high[k], map_low[k]), first) + product((power_high[k], power_low[k]), second)
        )
        if i == 0:
            level = index_ref[1, chip * groups]
            inside = jnp.where(side == 0, 1.0, 0.0)
            rows = carried(4 * group, 8) * inside
            done = add_edge(done, edge_ref, level, 0, rows[0:1], rows[1:2])
        out_ref[0, i * group : (i + 1) * group, :] = done[:group]
        out_ref[1, i * group : (i + 1) * group, :] = done[group:]
    if image_ref is None:
        return
    image_ref[...] = jnp.zeros_like(image_ref)

    @pl.when((chip // 2 == part_of) & ((chip % 2) ^ (chip // 2) == second_pair))
    def _():
        for i in range(half):
            k = core * half + i
            columns = slice(i * group, (i + 1) * group)
            square = base_ref[core, i] + product(
                (power_high[k, 0:group, :], power_low[k, 0:group, :]), [item[:, columns] for item in first]
            )
            image_ref[:, columns] = diagonal_of(square)


def diagonal_of(square):
    rows = lax.broadcasted_iota(jnp.int32, square.shape, 0)
    columns = lax.broadcasted_iota(jnp.int32, square.shape, 1)
    return jnp.sum(jnp.where(rows == columns, square, 0.0), axis=0, keepdims=True)


def last_pass_kernel(place_ref, index_ref, high_ref, low_ref, edge_ref, *refs, half, step, group):
    owns, comes = refs[0:2], refs[2:4]
    if half:
        out_ref, state_ref, column_ref, image_ref, result, sems = refs[4:]
    else:
        carry_ref, beside_ref, *images = refs[4:-2]
        result, image_ref = refs[-2:]
    device = place_ref[0]
    chip, core = device // 2, device % 2
    block = owns[0].shape[-1]
    count = 4 * block // group
    low = half * count
    first = count + 1 if half else 0
    copies = []

    ready = {}

    def read(k):
        if k not in ready:
            q, inner = (k - low) * group // block, (k - low) * group % block
            columns = slice(inner, inner + group)
            ready[k] = [
                jnp.where(chip // 2 == q // 2, *(
                    jnp.where(core == q % 2, owns[item][part, :, columns], comes[item][part, :, columns])
                    for item in range(2)
                ))
                for part in range(2)
            ]
        return ready[k]

    def write(k, solved):
        if half and k == low:
            state_ref[...] = solved
            return
        where = k - first
        result[where, 0] = solved[:, :group]
        result[where, 1] = solved[:, group:]
        if not half:
            return
        copy = pltpu.make_async_copy(
            result.at[where], out_ref.at[0, :, :, k * group : (k + 1) * group], sems.at[where]
        )
        copy.start()
        copies.append(copy)

    tables = (high_ref, low_ref, edge_ref)
    following, above = None, None
    if half:
        for part, value in enumerate(read(low)):
            column_ref[part] = jnp.broadcast_to(value[:, 0:1], column_ref.shape[1:])
    else:
        level = index_ref[step, count]
        solved = carry_ref[...]
        for part, value in enumerate(read(count - 1)):
            solved = solved + value[:, group - 1 : group] * edge_ref[level, part : part + 1, :]
        write(count, solved)
        following = halves(solved)
        above = [beside_ref[part, :, 0:1] for part in range(2)]
    line_groups(read, lambda k: index_ref[step, k], tables, low, low + count, following, None, above, write)
    if half:
        image_ref[...] = jnp.zeros_like(image_ref)
    else:
        image_ref[1:2] = images[0][...]
        image_ref[0:1] = sum((item[...] for item in images[2:]), images[1][...])
    row = image_ref.shape[0] - 1
    for i in range(block // group):
        mine = device * (block // group) + i
        here = mine > count if half else mine <= count
        square = result[jnp.where(here, mine - first, 0), 0, i * group : (i + 1) * group, :]
        columns = slice(i * group, (i + 1) * group)
        image_ref[row : row + 1, columns] = jnp.where(here, diagonal_of(square), image_ref[row : row + 1, columns])

    for copy in copies:
        copy.wait()


def last_pass(place, recv_index, tables, owns, comes, half, passed, shape, step, group):
    rows, length = shape[2:]
    width = length // 2
    count = width // group
    block = owns[0].shape[-1]
    args = [place, recv_index, *tables, *owns, *comes]
    specs = [smem()] * 2 + [vmem()] * 7
    results = whole((count - 1 if half else count + 1, 2, rows, group))
    scratch = []
    if half:
        outs = [whole(shape), whole((rows, 2 * group)), whole((2, rows, group))]
        out_specs = [anywhere(), vmem(), vmem()]
        scratch = [pltpu.VMEM(results.shape, f32), pltpu.SemaphoreType.DMA((count - 1,))]
    else:
        args += passed
        specs += [vmem()] * len(passed)
        outs = [results]
        out_specs = [vmem()]
    return pl.pallas_call(
        functools.partial(last_pass_kernel, half=half, step=step, group=group),
        out_shape=outs + [whole((1 if half else 2, block))],
        in_specs=specs,
        out_specs=out_specs + [vmem()],
        scratch_shapes=scratch,
        compiler_params=params(24),
        cost_estimate=cost(rows * width * group * 24, 8 * rows * width * 2),
    )(*args)


def store_kernel(groups_ref, _, out_ref, sems):
    group = groups_ref.shape[-1]
    copies = [
        pltpu.make_async_copy(groups_ref.at[k], out_ref.at[0, :, :, k * group : (k + 1) * group], sems.at[k])
        for k in range(groups_ref.shape[0])
    ]
    for copy in copies:
        copy.start()
    for copy in copies:
        copy.wait()


def store_groups(pieces, migrated):
    return pl.pallas_call(
        store_kernel,
        out_shape=whole(migrated.shape),
        in_specs=[anywhere(), anywhere()],
        out_specs=anywhere(),
        scratch_shapes=[pltpu.SemaphoreType.DMA((pieces.shape[0],))],
        input_output_aliases={1: 0},
        cost_estimate=cost(0, 8 * 1024 * 1024),
        compiler_params=params(4),
    )(pieces, migrated)


def sum_over(value, axis, count):
    reach = 1
    while reach < count:
        value = value + lax.ppermute(value, axis, [(i, i ^ reach) for i in range(count)])
        reach *= 2
    return value


def fast_shards(wavefield, inv_table, couple_table, rhs_table, recv_index, shot_index, *, devices, freqs):
    levels, _, group, _ = inv_table.shape[1:]
    rows, _ = wavefield.shape[2:]
    block = rows
    chips = devices // 2
    groups = 2 * rows // group
    device = lax.axis_index("plane")
    place = device.reshape(1).astype(jnp.int32)
    double = 2 * group
    partner = [(d, d ^ 1) for d in range(devices)]

    edge = edge_row(place, wavefield)
    swap = [(d, d + 1) for d in range(1, devices - 1, 2)] + [(d + 1, d) for d in range(1, devices - 1, 2)]
    halo = lax.ppermute(edge, "plane", swap)
    right = make_tables(right_table_kernel, rhs_table, inv_table[0], couple_table[0], (levels, 4, double))

    left = make_tables(left_table_kernel, rhs_table, inv_table[0], couple_table[0], (levels, 2, double, group))

    wide = block // 2
    piece = whole((4 * group + 8, wide))
    local = whole((groups, double, block))
    base = whole((2, groups // 2, group, group))
    matrices = whole((groups, double, double), bf16)
    middle = whole((chips - 2, double, double), bf16)
    powers = []

    def make_powers(ready):
        powers.extend(
            pl.pallas_call(
                functools.partial(power_kernel, groups=groups, group=group),
                out_shape=[matrices] * 2 + [whole((groups, group, double))] + [middle] * 2,
                in_specs=[smem()] + [vmem()] * 3 + [anywhere()],
                out_specs=[vmem()] * 5,
                compiler_params=params(20),
                cost_estimate=cost(groups * group * group * group * 64, 4 * 1024 * 1024),
            )(shot_index, *right, ready)
        )
        return powers[0]

    keep, come = {}, {}
    locals_, bases, theirs = {}, {}, {}

    def first(half, carry, ready):
        result = first_pass(place, recv_index, wavefield, halo, right, half, carry, ready, block, group)
        *carry, keep[half], send = result
        come[half] = lax.ppermute(send, "plane", partner)
        return carry

    def open_sweep(half, second_pair, ready):
        spec = pltpu.PrefetchScalarGridSpec(
            num_scalar_prefetch=2,
            grid=(1,),
            in_specs=[vmem()] * 3
            + [pl.BlockSpec((1,) + keep[half].shape[1:], lambda i, at, _: ((at[0] // 4) ^ second_pair, 0, 0, 0))] * 2
            + [anywhere()],
            out_specs=[vmem()] * 4,
        )
        name = "%d_%d" % (half, second_pair)
        near, far, locals_[name], bases[name] = pl.pallas_call(
            functools.partial(open_sweep_kernel, groups=groups, group=group),
            grid_spec=spec,
            out_shape=[piece, piece, local, base],
            compiler_params=params(24),
            cost_estimate=cost(groups * group * block * group * 48, 8 * groups * group * block * 3),
        )(place, shot_index, *left, keep[half], come[half], ready)
        for offset, item in ((2 * second_pair + 1, far), (2 * second_pair, near)):
            moves = [(d, d ^ (2 * offset)) for d in range(devices)]
            theirs[half, offset] = lax.ppermute(item, "plane", moves) if offset else item
        return near

    (carry,) = first(1, None, None)
    after = open_sweep(1, 1, carry)
    first(0, carry, after)
    after = open_sweep(1, 0, keep[0])
    after = open_sweep(0, 1, after)
    after = open_sweep(0, 0, after)
    after = make_powers(after)
    power_high, power_low, power_turned, chip_high, chip_low = powers
    came = {}
    for half in (1, 0):
        carries = pl.pallas_call(
            functools.partial(scan_kernel, chips=chips, group=group),
            out_shape=[piece] * chips,
            in_specs=[smem()] + [vmem()] * (6 + chips) + [anywhere()],
            out_specs=[vmem()] * chips,
            scratch_shapes=[pltpu.VMEM((chips,) + piece.shape, f32), pltpu.VMEM((chips, 8, wide), f32)],
            compiler_params=params(20),
            cost_estimate=cost(3 * group * group * wide * 24, 4 * 1024 * 1024),
        )(place, left[0], left[1], power_high, power_low, chip_high, chip_low, *[theirs[half, o] for o in range(chips)], after)
        after = carries[0]
        if half:
            map_high, map_low = pl.pallas_call(
                functools.partial(own_map_kernel, groups=groups, group=group),
                out_shape=[matrices] * 2,
                in_specs=[smem()] * 2 + [vmem()] * 4 + [anywhere()],
                out_specs=[vmem()] * 2,
                compiler_params=params(20),
                cost_estimate=cost(groups * group * group * group * 32, 4 * 1024 * 1024),
            )(place, shot_index, *right, power_turned, after)
            after = map_high
        for offset in (3, 1, 2, 0):
            moves = [(d, d ^ (2 * offset)) for d in range(devices)]
            came[half, offset] = lax.ppermute(carries[offset], "plane", moves) if offset else carries[0]

    images, image_last = [], None
    passed = None
    part = whole((2, rows, block))
    for half in (1, 0):
        owns, comes = [], []
        for second_pair in (0, 1):
            name = "%d_%d" % (half, second_pair)
            for kind in ("far", "near"):
                outs = [part] + ([whole((1, block))] if kind == "near" else [])
                result = pl.pallas_call(
                    functools.partial(
                        close_sweep_kernel, groups=groups, group=group, part_of=half, second_pair=second_pair
                    ),
                    out_shape=outs,
                    in_specs=[smem()] * 2 + [vmem()] * 9 + [anywhere()],
                    out_specs=[vmem()] * len(outs),
                    scratch_shapes=[pltpu.VMEM((2,) + piece.shape, f32)],
                    compiler_params=params(20),
                    cost_estimate=cost(groups * group * block * group * 12, 4 * groups * group * block * 2),
                )(
                    place, shot_index, left[2], power_high, power_low, map_high, map_low, locals_[name], bases[name],
                    came[half, 2 * second_pair], came[half, 2 * second_pair + 1], after,
                )
                after = result[-1]
                if kind == "far":
                    comes.append(lax.ppermute(result[0], "plane", partner))
            owns.append(result[0])
            images.append(result[1])
        if not half:
            migrated, *passed = *passed, image_last, *images
        *passed, image_last = last_pass(place, recv_index, right, owns, comes, half, passed, wavefield.shape, 1, group)
        after = image_last
    migrated = store_groups(passed[0], migrated)
    image_last = sum_over(image_last, "freq", freqs)
    return migrated, image_last


def solution(mesh):
    placed = (
        P("freq", None, "plane", None),
        P("freq", None, None, None, None),
        P("freq", None, None, None),
        P("freq", None, None),
        P(),
        P(),
    )
    devices = mesh.shape["plane"]
    freqs = mesh.shape["freq"]

    def body(*arrays):
        if devices == 8 and arrays[0].shape[2] == 2 * GROUP and arrays[0].shape[0] == 1 and freqs & (freqs - 1) == 0:
            return fast_shards(*arrays, devices=devices, freqs=freqs)
        return shards(*arrays)

    return jax.shard_map(
        body,
        mesh=mesh,
        in_specs=placed,
        out_specs=(P("freq", None, "plane", None), P(None, "plane")),
        check_vma=False,
    )
```

```python
import functools

import jax
import jax.numpy as jnp
from jax import lax
from jax.experimental import pallas as pl
from jax.experimental.pallas import tpu as pltpu
from jax.sharding import PartitionSpec as P

NX = 2048
GROUP = 128
DEPTHS = 2


highest = lax.Precision.HIGHEST


def complex_product(form, mat_re, mat_im, vec_re, vec_im):
    real_part = jnp.einsum(form, mat_re, vec_re, precision=highest) - jnp.einsum(
        form, mat_im, vec_im, precision=highest
    )
    imag_part = jnp.einsum(form, mat_re, vec_im, precision=highest) + jnp.einsum(
        form, mat_im, vec_re, precision=highest
    )
    return (real_part, imag_part)


def select_rows(index, table):
    levels = jnp.arange(table.shape[1], dtype=jnp.int32)
    one_hot = (index[:, None] == levels[None, :]).astype(jnp.float32)
    return jnp.einsum("kv,fv...->fk...", one_hot, table, precision=highest)


def coupling_powers(couple_table, group_count):
    power_re = couple_table[:, 0]
    power_im = couple_table[:, 1]
    powers = []
    reach = 1
    while reach < group_count:
        powers.append((power_re, power_im))
        power_re, power_im = complex_product("fab,fbc->fac", power_re, power_im, power_re, power_im)
        reach = reach * 2
    return powers


def shifted_up(values, reach, group_axis):
    count = values.shape[group_axis]
    kept = lax.slice_in_dim(values, reach, count, axis=group_axis)
    zero_shape = list(values.shape)
    zero_shape[group_axis] = reach
    return jnp.concatenate([kept, jnp.zeros(zero_shape, values.dtype)], axis=group_axis)


def line_pass(wave_field, index, inv_table, rhs_table, powers, along_last):
    line_axis = 3 if along_last else 2
    freqs = wave_field.shape[0]
    length = wave_field.shape[line_axis]
    group_count = length // GROUP
    inv_sel = select_rows(index, inv_table)
    rhs_sel = select_rows(index, rhs_table)
    pad_widths = [(0, 0), (0, 0), (0, 0), (0, 0)]
    pad_widths[line_axis] = (1, 1)
    padded = jnp.pad(wave_field, pad_widths)
    beside = lax.slice_in_dim(padded, 0, length, axis=line_axis) + lax.slice_in_dim(
        padded, 2, length + 2, axis=line_axis
    )
    second = beside - 2.0 * wave_field
    if along_last:
        shape = (freqs, wave_field.shape[2], group_count, GROUP)
        coef_re = rhs_sel[:, None, :, 0, None]
        coef_im = rhs_sel[:, None, :, 1, None]
        local_form = "fkab,flkb->flka"
        power_form = "fab,flkb->flka"
        group_axis = 2
    else:
        shape = (freqs, group_count, GROUP, wave_field.shape[3])
        coef_re = rhs_sel[:, :, 0, None, None]
        coef_im = rhs_sel[:, :, 1, None, None]
        local_form = "fkab,fkbm->fkam"
        power_form = "fab,fkbm->fkam"
        group_axis = 1
    base_re = wave_field[:, 0].reshape(shape)
    base_im = wave_field[:, 1].reshape(shape)
    second_re = second[:, 0].reshape(shape)
    second_im = second[:, 1].reshape(shape)
    source_re = base_re + coef_re * second_re - coef_im * second_im
    source_im = base_im + coef_re * second_im + coef_im * second_re
    solved_re, solved_im = complex_product(
        local_form, inv_sel[:, :, 0], inv_sel[:, :, 1], source_re, source_im
    )
    reach = 1
    for power_re, power_im in powers:
        add_re, add_im = complex_product(
            power_form,
            power_re,
            power_im,
            shifted_up(solved_re, reach, group_axis),
            shifted_up(solved_im, reach, group_axis),
        )
        solved_re = solved_re + add_re
        solved_im = solved_im + add_im
        reach = reach * 2
    out_shape = (freqs,) + wave_field.shape[2:]
    return jnp.stack([solved_re.reshape(out_shape), solved_im.reshape(out_shape)], axis=1)


def to_columns(wave_field):
    return lax.all_to_all(wave_field, "plane", split_axis=3, concat_axis=2, tiled=True)


def to_rows(wave_field):
    return lax.all_to_all(wave_field, "plane", split_axis=2, concat_axis=3, tiled=True)


def diagonal_rows(wave_field, first_row):
    count = wave_field.shape[2]
    block = lax.dynamic_slice_in_dim(wave_field[:, 0], first_row, count, axis=2)
    return jnp.sum(jnp.diagonal(block, axis1=1, axis2=2), axis=0)


def diagonal_columns(wave_field, first_row):
    count = wave_field.shape[3]
    block = lax.dynamic_slice_in_dim(wave_field[:, 0], first_row, count, axis=1)
    return jnp.sum(jnp.diagonal(block, axis1=1, axis2=2), axis=0)


def image_part(partial_value):
    return lax.psum(partial_value, "freq")


def shards(wavefield, inv_table, couple_table, rhs_table, recv_index, shot_index):
    powers = coupling_powers(couple_table, NX // GROUP)
    row_count = wavefield.shape[2]
    first_row = lax.axis_index("plane") * row_count
    wave_field = wavefield
    parts = []
    for step_index in range(DEPTHS):
        if step_index % 2 == 0:
            wave_field = line_pass(
                wave_field, recv_index[step_index], inv_table, rhs_table, powers, True
            )
            wave_field = to_columns(wave_field)
            wave_field = line_pass(
                wave_field, shot_index[step_index], inv_table, rhs_table, powers, False
            )
            parts.append(image_part(diagonal_columns(wave_field, first_row)))
        else:
            wave_field = line_pass(
                wave_field, shot_index[step_index], inv_table, rhs_table, powers, False
            )
            wave_field = to_rows(wave_field)
            wave_field = line_pass(
                wave_field, recv_index[step_index], inv_table, rhs_table, powers, True
            )
            parts.append(image_part(diagonal_rows(wave_field, first_row)))
    stacked = jnp.stack(parts)
    return (wave_field, stacked)


f32 = jnp.float32
bf16 = jnp.bfloat16


def halves(value):
    high = value.astype(bf16)
    low = (value - high.astype(f32)).astype(bf16)
    return high, low


def mul(left, right):
    return jnp.dot(left, right, preferred_element_type=f32)


def product(left, right):
    (left_high, left_low), (right_high, right_low) = left, right
    return mul(left_high, right_high) + mul(left_low, right_high) + mul(left_high, right_low)


def params(mebibytes):
    return pltpu.CompilerParams(vmem_limit_bytes=mebibytes * 1024 * 1024)


def whole(shape, dtype=f32):
    return jax.ShapeDtypeStruct(shape, dtype)


def smem():
    return pl.BlockSpec(memory_space=pltpu.SMEM)


def vmem():
    return pl.BlockSpec(memory_space=pltpu.VMEM)


def anywhere():
    return pl.BlockSpec(memory_space=pl.ANY)


def cost(macs, size):
    return pl.CostEstimate(flops=2 * macs, bytes_accessed=size, transcendentals=0)


def folded(level, inv_ref, rhs_ref):
    mat_re, mat_im = inv_ref[level, 0], inv_ref[level, 1]
    coef_re, coef_im = rhs_ref[0, level, 0], rhs_ref[0, level, 1]
    group = mat_re.shape[-1]
    lane = lax.broadcasted_iota(jnp.int32, mat_re.shape, 1)

    def differences(mat):
        low_side = jnp.where(lane == 0, 0.0, pltpu.roll(mat, 1, 1))
        high_side = jnp.where(lane == group - 1, 0.0, pltpu.roll(mat, group - 1, 1))
        return low_side + high_side - 2.0 * mat

    diff_re, diff_im = differences(mat_re), differences(mat_im)
    inner_re = mat_re + coef_re * diff_re - coef_im * diff_im
    inner_im = mat_im + coef_re * diff_im + coef_im * diff_re
    scaled_re = coef_re * mat_re - coef_im * mat_im
    scaled_im = coef_re * mat_im + coef_im * mat_re
    return inner_re, inner_im, scaled_re, scaled_im


def store_left(high_ref, low_ref, index, mat_re, mat_im):
    group = mat_re.shape[-1]
    blocks = ((mat_re, -mat_im), (mat_im, mat_re))
    for i in range(2):
        for j in range(2):
            where = (index, slice(i * group, (i + 1) * group), slice(j * group, (j + 1) * group))
            high_ref[where], low_ref[where] = halves(blocks[i][j])


def left_table_kernel(rhs_ref, inv_ref, couple_ref, high_ref, low_ref, edge_ref):
    levels, _, group, _ = inv_ref.shape
    for level in range(levels):
        inner_re, inner_im, scaled_re, scaled_im = folded(level, inv_ref, rhs_ref)
        store_left(high_ref, low_ref, level, inner_re, inner_im)
        for part, scaled in enumerate((scaled_re, scaled_im)):
            rows = slice(part * group, (part + 1) * group)
            edge_ref[level, 0, rows, :] = jnp.broadcast_to(scaled[:, 0:1], (group, group))
            edge_ref[level, 1, rows, :] = jnp.broadcast_to(scaled[:, group - 1 : group], (group, group))
    store_left(high_ref, low_ref, levels, couple_ref[0], couple_ref[1])


def right_table_kernel(rhs_ref, inv_ref, couple_ref, high_ref, low_ref, edge_ref):
    levels, _, group, _ = inv_ref.shape
    for level in range(levels + 1):
        if level < levels:
            inner_re, inner_im, scaled_re, scaled_im = folded(level, inv_ref, rhs_ref)
            scaled_re, scaled_im = scaled_re.T, scaled_im.T
            for side, row in enumerate((0, group - 1)):
                edge_re, edge_im = scaled_re[row : row + 1], scaled_im[row : row + 1]
                edge_ref[level, 2 * side : 2 * side + 1, :] = jnp.concatenate([edge_re, edge_im], axis=1)
                edge_ref[level, 2 * side + 1 : 2 * side + 2, :] = jnp.concatenate([-edge_im, edge_re], axis=1)
        else:
            inner_re, inner_im = couple_ref[0], couple_ref[1]
        turned_re, turned_im = inner_re.T, inner_im.T
        store_left(high_ref, low_ref, level, turned_re, -turned_im)


def make_tables(kernel, rhs, inv_table, couple_table, edge_shape):
    levels, _, group, _ = inv_table.shape
    shape = whole((levels + 1, 2 * group, 2 * group), bf16)
    return pl.pallas_call(
        kernel,
        out_shape=[shape, shape, whole(edge_shape)],
        in_specs=[smem(), vmem(), vmem()],
        out_specs=[vmem()] * 3,
        compiler_params=params(16),
        cost_estimate=cost(10**10, 4 * 1024 * 1024),
    )(rhs, inv_table, couple_table)


def edge_row_kernel(place_ref, field_ref, row_ref, held, sem):
    rows = field_ref.shape[2]
    odd = place_ref[0] % 2
    start = pl.multiple_of(odd * (rows - 8), 8)
    copy = pltpu.make_async_copy(field_ref.at[0, :, pl.ds(start, 8), :], held, sem)
    copy.start()
    copy.wait()
    for part in range(2):
        row_ref[0, part] = jnp.where(odd == 1, held[part, 7:8, :], held[part, 0:1, :])


def edge_row(place, field):
    length = field.shape[3]
    return pl.pallas_call(
        edge_row_kernel,
        out_shape=whole((1, 2, 1, length)),
        in_specs=[smem(), anywhere()],
        out_specs=vmem(),
        scratch_shapes=[pltpu.VMEM((2, 8, length), f32), pltpu.SemaphoreType.DMA],
        compiler_params=params(60),
        cost_estimate=cost(10**10, 1024 * 1024),
    )(place, field)


def line_groups(read, level_of, tables, low, high, following, below, above, write):
    high_ref, low_ref, edge_ref = tables
    last = high_ref.shape[0] - 1
    couple = (high_ref[last], low_ref[last])
    for k in reversed(range(low, high)):
        level = level_of(k)
        value_re, value_im = read(k)
        group = value_re.shape[1]
        solved = product(halves(jnp.concatenate([value_re, value_im], axis=1)), (high_ref[level], low_ref[level]))
        if following is not None:
            solved = solved + product(following, couple)
        before = [item[:, group - 1 : group] for item in read(k - 1)] if k > low else below
        for side, column in ((0, before), (1, above)):
            if column is not None:
                for part in range(2):
                    row = edge_ref[level, 2 * side + part : 2 * side + part + 1, :]
                    solved = solved + column[part] * row
        write(k, solved)
        following = halves(solved)
        above = [value_re[:, 0:1], value_im[:, 0:1]]


def rows_with_halo(field_ref, halo_ref, part, columns, halo_columns):
    row = jnp.broadcast_to(halo_ref[0, part, :, halo_columns], (8, columns.stop - columns.start))
    return jnp.concatenate([field_ref[0, part, :, columns], row], axis=0)


def first_pass_kernel(place_ref, index_ref, field_ref, beside_ref, halo_ref, high_ref, low_ref, edge_ref, *refs,
                      half, group, block):
    if half:
        carry_ref, keep_ref, send_ref, odd = None, refs[1], refs[2], refs[3]
        state_ref = refs[0]
    else:
        carry_ref, _, keep_ref, send_ref, odd = refs
        state_ref = None
    width = field_ref.shape[-1]
    count = width // group
    low = half * count
    core = place_ref[0] % 2

    def read(k):
        columns = slice((k - low) * group, (k - low + 1) * group)
        wide = slice(k * group, (k + 1) * group)
        return [rows_with_halo(field_ref, halo_ref, part, columns, wide) for part in range(2)]

    inside = slice(0, group)
    wide = slice((low - 1) * group, low * group) if half else slice(count * group, (count + 1) * group)
    beyond = [rows_with_halo(beside_ref, halo_ref, part, inside, wide) for part in range(2)]
    if half:
        below, above, following = [item[:, group - 1 : group] for item in beyond], None, None
    else:
        below, above, following = None, [item[:, 0:1] for item in beyond], halves(carry_ref[...])

    def write(k, solved):
        start = (k - low) * group
        b, inner = start // block, start % block
        columns = slice(inner, inner + group)
        for part in range(2):
            value = solved[:, part * group : (part + 1) * group]
            if b % 2:
                odd[b // 2, part, :, columns] = value
            else:
                other = odd[b // 2, part, :, columns]
                keep_ref[b // 2, part, :, columns] = jnp.where(core == 0, value, other)
                send_ref[b // 2, part, :, columns] = jnp.where(core == 0, other, value)
        if half and k == low:
            state_ref[...] = solved

    line_groups(
        read, lambda k: index_ref[0, k], (high_ref, low_ref, edge_ref), low, low + count, following, below, above, write
    )


def first_pass(place, recv_index, field, halo, tables, half, carry, after, block, group):
    rows, length = field.shape[2:]
    width = length // 2
    lines = rows + 8
    count = width // group
    shape = (width // (2 * block), 2, lines, block)
    beside = count - 1 if half else count
    args = [place, recv_index, field, field, halo, *tables]
    specs = [
        smem(), smem(),
        pl.BlockSpec((1, 2, rows, width), lambda i: (0, 0, 0, half)),
        pl.BlockSpec((1, 2, rows, group), lambda i: (0, 0, 0, beside)),
    ] + [vmem()] * 4
    outs = [whole(shape)] * 2
    if half:
        outs = [whole((lines, 2 * group))] + outs
    else:
        args += [carry, after]
        specs += [vmem(), anywhere()]
    return pl.pallas_call(
        functools.partial(first_pass_kernel, half=half, group=group, block=block),
        grid=(1,),
        out_shape=outs,
        in_specs=specs,
        out_specs=[vmem()] * len(outs),
        scratch_shapes=[pltpu.VMEM(shape, f32)],
        compiler_params=params(36),
        cost_estimate=cost(lines * width * group * 24, 8 * lines * width * 2),
    )(*args)


def add_edge(solved, edge_ref, level, side, row_re, row_im):
    group = edge_ref.shape[-1]
    wide = row_re.shape[-1]
    column = [edge_ref[level, side, part * group : (part + 1) * group, :] for part in range(2)]
    if wide > group:
        column = [jnp.concatenate([item] * (wide // group), axis=1) for item in column]
    term_re = column[0] * row_re - column[1] * row_im
    term_im = column[0] * row_im + column[1] * row_re
    both = jnp.concatenate([term_re, term_im], axis=0)
    return both if solved is None else solved + both


def second_groups(chip, groups, index_ref, tables):
    high_ref, low_ref, edge_ref = tables
    last = high_ref.shape[0] - 1
    couple = (high_ref[last], low_ref[last])
    base = chip * groups
    total = index_ref.shape[1]

    def open_state(row_re, row_im):
        after = base + groups
        level = index_ref[1, jnp.minimum(after, total - 1)]
        inside = jnp.where(after < total, 1.0, 0.0)
        return add_edge(None, edge_ref, level, 0, row_re * inside, row_im * inside)

    def step(k, value, following, before, after):
        level = index_ref[1, base + k]
        solved = product((high_ref[level], low_ref[level]), value)
        solved = solved + product(couple, following)
        if before is not None:
            solved = add_edge(solved, edge_ref, level, 0, *before)
        if after is not None:
            solved = add_edge(solved, edge_ref, level, 1, *after)
        return solved

    return open_state, step


def first_row(value, group):
    return value[0:1], value[group : group + 1]


def last_row(value, group):
    return value[group - 1 : group], value[2 * group - 1 : 2 * group]


def open_sweep_kernel(place_ref, index_ref, high_ref, low_ref, edge_ref, keep_ref, come_ref, _, near_ref, far_ref, local_ref,
                      base_ref, *, groups, group):
    device = place_ref[0]
    chip, core = device // 2, device % 2
    tables = (high_ref, low_ref, edge_ref)
    last = high_ref.shape[0] - 1
    couple = (high_ref[last], low_ref[last])
    half = groups // 2
    lines = half * group
    width = keep_ref.shape[-1]

    def rows(upper, start, count):
        mine = upper == core
        return [
            jnp.where(mine, keep_ref[0, part, start : start + count, :], come_ref[0, part, start : start + count, :])
            for part in range(2)
        ]

    def store_pair(where, value):
        low_side, high_side = value[:, : width // 2], value[:, width // 2 :]
        near_ref[where, :] = jnp.where(chip % 2 == 0, low_side, high_side)
        far_ref[where, :] = jnp.where(chip % 2 == 0, high_side, low_side)

    def given(k):
        return rows(k // half, (k % half) * group, group)

    open_state, step = second_groups(chip, groups, index_ref, tables)
    above = [item[0:1] for item in rows(1, lines, 8)]
    solved = following = state = None
    value = given(groups - 1)
    earlier = None
    for k in reversed(range(groups)):
        level = index_ref[0, chip * groups + k]
        below_value = given(k - 1) if k else None
        before = [item[group - 1 : group] for item in below_value] if k else [item[0:1] for item in rows(0, lines, 8)]
        now = product((high_ref[level], low_ref[level]), halves(jnp.concatenate(value, axis=0)))
        if following is not None:
            now = now + product(couple, following)
        now = add_edge(now, edge_ref, level, 0, *before)
        now = add_edge(now, edge_ref, level, 1, *above)
        above = [item[0:1] for item in value]
        value = below_value
        base_ref[k // half, k % half] = now[:group, (k % half) * group : (k % half + 1) * group]
        if k == groups - 1:
            row_re, row_im = last_row(now, group)
            store_pair(
                slice(4 * group, 4 * group + 8),
                jnp.concatenate([row_re, row_im, jnp.zeros((6, width), f32)], axis=0),
            )
            state = halves(open_state(row_re, row_im))
        else:
            done = step(k + 1, following, state, last_row(now, group), first_row(earlier, group) if earlier is not None else None)
            local_ref[k + 1] = done
            state = halves(done)
        earlier = solved
        solved = now
        following = halves(now)
    done = step(0, following, state, None, first_row(earlier, group))
    local_ref[0] = done
    store_pair(slice(0, 2 * group), solved)
    store_pair(slice(2 * group, 4 * group), done)


def unit_rows(group):
    rows = lax.broadcasted_iota(jnp.int32, (group, 2 * group), 0)
    columns = lax.broadcasted_iota(jnp.int32, (group, 2 * group), 1)
    return (rows == columns).astype(f32)


def store_turned(high_ref, low_ref, index, turned):
    group = turned.shape[0]
    store_left(high_ref, low_ref, index, turned[:, :group].T, turned[:, group:].T)


def power_kernel(index_ref, high_ref, low_ref, edge_ref, _, power_high, power_low, turned_ref, chip_high, chip_low,
                 *, groups, group):
    tables = (high_ref, low_ref, edge_ref)
    last = high_ref.shape[0] - 1
    couple = (high_ref[last], low_ref[last])
    values = [None] * groups + [unit_rows(group)]
    for k in reversed(range(groups)):
        values[k] = product(halves(values[k + 1]), couple)
        store_turned(power_high, power_low, k, values[k])
        turned_ref[k] = values[k]
    split = [halves(value) for value in values]
    for q in range(chip_high.shape[0]):

        def store(k, done, q=q):
            if k == 0:
                store_turned(chip_high, chip_low, q, done)

        linear_part(q + 1, groups, group, index_ref, tables, values, split, store)


def own_map_kernel(place_ref, index_ref, high_ref, low_ref, edge_ref, turned_ref, _, map_high, map_low, *, groups, group):
    values = [turned_ref[k] for k in range(groups)] + [unit_rows(group)]
    split = [halves(value) for value in values]

    def store(k, done):
        store_turned(map_high, map_low, k, done)

    linear_part(place_ref[0] // 2, groups, group, index_ref, (high_ref, low_ref, edge_ref), values, split, store)


def linear_part(chip, groups, group, index_ref, tables, values, split, store):
    high_ref, low_ref, edge_ref = tables
    last = high_ref.shape[0] - 1
    couple = (high_ref[last], low_ref[last])
    base, total = chip * groups, index_ref.shape[1]

    def edge(level, side, column_re, column_im):
        rows = [edge_ref[level, 2 * side + part : 2 * side + part + 1, :] for part in range(2)]
        return column_re * rows[0] + column_im * rows[1]

    def first_column(value):
        return value[:, 0:1], value[:, group : group + 1]

    def last_column(value):
        return value[:, group - 1 : group], value[:, 2 * group - 1 : 2 * group]

    after = base + groups
    inside = jnp.where(after < total, 1.0, 0.0)
    done = edge(index_ref[1, jnp.minimum(after, total - 1)], 0, *last_column(values[groups - 1])) * inside
    for k in reversed(range(groups)):
        level = index_ref[1, base + k]
        done = product(split[k], (high_ref[level], low_ref[level])) + product(halves(done), couple)
        if k:
            done = done + edge(level, 0, *last_column(values[k - 1]))
        done = done + edge(level, 1, *first_column(values[k + 1]))
        store(k, done)


def scan_kernel(place_ref, high_ref, low_ref, power_high, power_low, chip_high, chip_low, *refs, chips, group):
    pieces, outs, (held, rows) = refs[:chips], refs[-chips - 2 : -2], refs[-2:]
    chip = place_ref[0] // 2
    last = high_ref.shape[0] - 1
    size = 4 * group
    for offset in range(chips):
        held[chip ^ offset] = pieces[offset][...]
    keep = (power_high[0], power_low[0])
    rows[0] = jnp.zeros_like(rows[0])
    for q in range(chips - 1, 0, -1):
        first = halves(held[q, 0 : 2 * group, :])
        for part in range(2):
            tail = slice((part + 1) * group - 16, (part + 1) * group)
            row = product((high_ref[last, tail, :], low_ref[last, tail, :]), first)[15:16]
            rows[q, part : part + 1, :] = held[q - 1, size + part : size + part + 1, :] + row
        if q > 1:
            second = halves(held[q, 2 * group : size, :])
            held[q - 1, 0 : 2 * group, :] = held[q - 1, 0 : 2 * group, :] + product(keep, first)
            held[q - 1, 2 * group : size, :] = (
                held[q - 1, 2 * group : size, :]
                + product((chip_high[q - 2], chip_low[q - 2]), first)
                + product(keep, second)
            )
    held[0] = jnp.zeros_like(held[0])
    for offset in range(chips):
        target = chip ^ offset
        outs[offset][0:size, :] = held[(target + 1) % chips, 0:size, :]
        outs[offset][size : size + 8, :] = rows[target]


def close_sweep_kernel(place_ref, index_ref, edge_ref, power_high, power_low, map_high, map_low, local_ref, base_ref,
                       near_ref, far_ref, _, out_ref, *refs, groups, group, part_of, second_pair):
    image_ref = refs[0] if refs else None
    device = place_ref[0]
    chip, core = device // 2, device % 2
    side = core if image_ref is not None else 1 - core
    even = chip % 2 == 0

    def carried(start, count):
        near, far = near_ref[start : start + count, :], far_ref[start : start + count, :]
        return jnp.concatenate([jnp.where(even, near, far), jnp.where(even, far, near)], axis=1)

    first = halves(carried(0, 2 * group))
    second = halves(carried(2 * group, 2 * group))
    half = groups // 2
    for i in reversed(range(half)):
        k = side * half + i
        done = local_ref[k] + (
            product((map_high[k], map_low[k]), first) + product((power_high[k], power_low[k]), second)
        )
        if i == 0:
            level = index_ref[1, chip * groups]
            inside = jnp.where(side == 0, 1.0, 0.0)
            rows = carried(4 * group, 8) * inside
            done = add_edge(done, edge_ref, level, 0, rows[0:1], rows[1:2])
        out_ref[0, i * group : (i + 1) * group, :] = done[:group]
        out_ref[1, i * group : (i + 1) * group, :] = done[group:]
    if image_ref is None:
        return
    image_ref[...] = jnp.zeros_like(image_ref)

    @pl.when((chip // 2 == part_of) & ((chip % 2) ^ (chip // 2) == second_pair))
    def _():
        for i in range(half):
            k = core * half + i
            columns = slice(i * group, (i + 1) * group)
            square = base_ref[core, i] + product(
                (power_high[k, 0:group, :], power_low[k, 0:group, :]), [item[:, columns] for item in first]
            )
            image_ref[:, columns] = diagonal_of(square)


def diagonal_of(square):
    rows = lax.broadcasted_iota(jnp.int32, square.shape, 0)
    columns = lax.broadcasted_iota(jnp.int32, square.shape, 1)
    return jnp.sum(jnp.where(rows == columns, square, 0.0), axis=0, keepdims=True)


def last_pass_kernel(place_ref, index_ref, high_ref, low_ref, edge_ref, *refs, half, step, group):
    owns, comes = refs[0:2], refs[2:4]
    if half:
        out_ref, state_ref, column_ref, image_ref, result, sems = refs[4:]
    else:
        carry_ref, beside_ref, *images = refs[4:-2]
        result, image_ref = refs[-2:]
    device = place_ref[0]
    chip, core = device // 2, device % 2
    block = owns[0].shape[-1]
    count = 4 * block // group
    low = half * count
    first = count + 1 if half else 0
    copies = []

    ready = {}

    def read(k):
        if k not in ready:
            q, inner = (k - low) * group // block, (k - low) * group % block
            columns = slice(inner, inner + group)
            ready[k] = [
                jnp.where(chip // 2 == q // 2, *(
                    jnp.where(core == q % 2, owns[item][part, :, columns], comes[item][part, :, columns])
                    for item in range(2)
                ))
                for part in range(2)
            ]
        return ready[k]

    def write(k, solved):
        if half and k == low:
            state_ref[...] = solved
            return
        where = k - first
        result[where, 0] = solved[:, :group]
        result[where, 1] = solved[:, group:]
        if not half:
            return
        copy = pltpu.make_async_copy(
            result.at[where], out_ref.at[0, :, :, k * group : (k + 1) * group], sems.at[where]
        )
        copy.start()
        copies.append(copy)

    tables = (high_ref, low_ref, edge_ref)
    following, above = None, None
    if half:
        for part, value in enumerate(read(low)):
            column_ref[part] = jnp.broadcast_to(value[:, 0:1], column_ref.shape[1:])
    else:
        level = index_ref[step, count]
        solved = carry_ref[...]
        for part, value in enumerate(read(count - 1)):
            solved = solved + value[:, group - 1 : group] * edge_ref[level, part : part + 1, :]
        write(count, solved)
        following = halves(solved)
        above = [beside_ref[part, :, 0:1] for part in range(2)]
    line_groups(read, lambda k: index_ref[step, k], tables, low, low + count, following, None, above, write)
    if half:
        image_ref[...] = jnp.zeros_like(image_ref)
    else:
        image_ref[1:2] = images[0][...]
        image_ref[0:1] = sum((item[...] for item in images[2:]), images[1][...])
    row = image_ref.shape[0] - 1
    for i in range(block // group):
        mine = device * (block // group) + i
        here = mine > count if half else mine <= count
        square = result[jnp.where(here, mine - first, 0), 0, i * group : (i + 1) * group, :]
        columns = slice(i * group, (i + 1) * group)
        image_ref[row : row + 1, columns] = jnp.where(here, diagonal_of(square), image_ref[row : row + 1, columns])

    for copy in copies:
        copy.wait()


def last_pass(place, recv_index, tables, owns, comes, half, passed, shape, step, group):
    rows, length = shape[2:]
    width = length // 2
    count = width // group
    block = owns[0].shape[-1]
    args = [place, recv_index, *tables, *owns, *comes]
    specs = [smem()] * 2 + [vmem()] * 7
    results = whole((count - 1 if half else count + 1, 2, rows, group))
    scratch = []
    if half:
        outs = [whole(shape), whole((rows, 2 * group)), whole((2, rows, group))]
        out_specs = [anywhere(), vmem(), vmem()]
        scratch = [pltpu.VMEM(results.shape, f32), pltpu.SemaphoreType.DMA((count - 1,))]
    else:
        args += passed
        specs += [vmem()] * len(passed)
        outs = [results]
        out_specs = [vmem()]
    return pl.pallas_call(
        functools.partial(last_pass_kernel, half=half, step=step, group=group),
        out_shape=outs + [whole((1 if half else 2, block))],
        in_specs=specs,
        out_specs=out_specs + [vmem()],
        scratch_shapes=scratch,
        compiler_params=params(24),
        cost_estimate=cost(rows * width * group * 24, 8 * rows * width * 2),
    )(*args)


def store_kernel(groups_ref, _, out_ref, sems):
    group = groups_ref.shape[-1]
    copies = [
        pltpu.make_async_copy(groups_ref.at[k], out_ref.at[0, :, :, k * group : (k + 1) * group], sems.at[k])
        for k in range(groups_ref.shape[0])
    ]
    for copy in copies:
        copy.start()
    for copy in copies:
        copy.wait()


def store_groups(pieces, migrated):
    return pl.pallas_call(
        store_kernel,
        out_shape=whole(migrated.shape),
        in_specs=[anywhere(), anywhere()],
        out_specs=anywhere(),
        scratch_shapes=[pltpu.SemaphoreType.DMA((pieces.shape[0],))],
        input_output_aliases={1: 0},
        cost_estimate=cost(0, 8 * 1024 * 1024),
        compiler_params=params(4),
    )(pieces, migrated)


def sum_over(value, axis, count):
    reach = 1
    while reach < count:
        value = value + lax.ppermute(value, axis, [(i, i ^ reach) for i in range(count)])
        reach *= 2
    return value


def fast_shards(wavefield, inv_table, couple_table, rhs_table, recv_index, shot_index, *, devices, freqs):
    levels, _, group, _ = inv_table.shape[1:]
    rows, _ = wavefield.shape[2:]
    block = rows
    chips = devices // 2
    groups = 2 * rows // group
    device = lax.axis_index("plane")
    place = device.reshape(1).astype(jnp.int32)
    double = 2 * group
    partner = [(d, d ^ 1) for d in range(devices)]

    edge = edge_row(place, wavefield)
    swap = [(d, d + 1) for d in range(1, devices - 1, 2)] + [(d + 1, d) for d in range(1, devices - 1, 2)]
    halo = lax.ppermute(edge, "plane", swap)
    right = make_tables(right_table_kernel, rhs_table, inv_table[0], couple_table[0], (levels, 4, double))

    left = make_tables(left_table_kernel, rhs_table, inv_table[0], couple_table[0], (levels, 2, double, group))

    wide = block // 2
    piece = whole((4 * group + 8, wide))
    local = whole((groups, double, block))
    base = whole((2, groups // 2, group, group))
    matrices = whole((groups, double, double), bf16)
    middle = whole((chips - 2, double, double), bf16)
    powers = []

    def make_powers(ready):
        powers.extend(
            pl.pallas_call(
                functools.partial(power_kernel, groups=groups, group=group),
                out_shape=[matrices] * 2 + [whole((groups, group, double))] + [middle] * 2,
                in_specs=[smem()] + [vmem()] * 3 + [anywhere()],
                out_specs=[vmem()] * 5,
                compiler_params=params(20),
                cost_estimate=cost(groups * group * group * group * 64, 4 * 1024 * 1024),
            )(shot_index, *right, ready)
        )
        return powers[0]

    keep, come = {}, {}
    locals_, bases, theirs = {}, {}, {}

    def first(half, carry, ready):
        result = first_pass(place, recv_index, wavefield, halo, right, half, carry, ready, block, group)
        *carry, keep[half], send = result
        come[half] = lax.ppermute(send, "plane", partner)
        return carry

    def open_sweep(half, second_pair, ready):
        spec = pltpu.PrefetchScalarGridSpec(
            num_scalar_prefetch=2,
            grid=(1,),
            in_specs=[vmem()] * 3
            + [pl.BlockSpec((1,) + keep[half].shape[1:], lambda i, at, _: ((at[0] // 4) ^ second_pair, 0, 0, 0))] * 2
            + [anywhere()],
            out_specs=[vmem()] * 4,
        )
        name = "%d_%d" % (half, second_pair)
        near, far, locals_[name], bases[name] = pl.pallas_call(
            functools.partial(open_sweep_kernel, groups=groups, group=group),
            grid_spec=spec,
            out_shape=[piece, piece, local, base],
            compiler_params=params(24),
            cost_estimate=cost(groups * group * block * group * 48, 8 * groups * group * block * 3),
        )(place, shot_index, *left, keep[half], come[half], ready)
        for offset, item in ((2 * second_pair + 1, far), (2 * second_pair, near)):
            moves = [(d, d ^ (2 * offset)) for d in range(devices)]
            theirs[half, offset] = lax.ppermute(item, "plane", moves) if offset else item
        return near

    (carry,) = first(1, None, None)
    after = open_sweep(1, 1, carry)
    first(0, carry, after)
    after = open_sweep(1, 0, keep[0])
    after = open_sweep(0, 1, after)
    after = open_sweep(0, 0, after)
    after = make_powers(after)
    power_high, power_low, power_turned, chip_high, chip_low = powers
    came = {}
    for half in (1, 0):
        carries = pl.pallas_call(
            functools.partial(scan_kernel, chips=chips, group=group),
            out_shape=[piece] * chips,
            in_specs=[smem()] + [vmem()] * (6 + chips) + [anywhere()],
            out_specs=[vmem()] * chips,
            scratch_shapes=[pltpu.VMEM((chips,) + piece.shape, f32), pltpu.VMEM((chips, 8, wide), f32)],
            compiler_params=params(20),
            cost_estimate=cost(3 * group * group * wide * 24, 4 * 1024 * 1024),
        )(place, left[0], left[1], power_high, power_low, chip_high, chip_low, *[theirs[half, o] for o in range(chips)], after)
        after = carries[0]
        if half:
            map_high, map_low = pl.pallas_call(
                functools.partial(own_map_kernel, groups=groups, group=group),
                out_shape=[matrices] * 2,
                in_specs=[smem()] * 2 + [vmem()] * 4 + [anywhere()],
                out_specs=[vmem()] * 2,
                compiler_params=params(20),
                cost_estimate=cost(groups * group * group * group * 32, 4 * 1024 * 1024),
            )(place, shot_index, *right, power_turned, after)
            after = map_high
        for offset in (3, 1, 2, 0):
            moves = [(d, d ^ (2 * offset)) for d in range(devices)]
            came[half, offset] = lax.ppermute(carries[offset], "plane", moves) if offset else carries[0]

    images, image_last = [], None
    passed = None
    part = whole((2, rows, block))
    for half in (1, 0):
        owns, comes = [], []
        for second_pair in (0, 1):
            name = "%d_%d" % (half, second_pair)
            for kind in ("far", "near"):
                outs = [part] + ([whole((1, block))] if kind == "near" else [])
                result = pl.pallas_call(
                    functools.partial(
                        close_sweep_kernel, groups=groups, group=group, part_of=half, second_pair=second_pair
                    ),
                    out_shape=outs,
                    in_specs=[smem()] * 2 + [vmem()] * 9 + [anywhere()],
                    out_specs=[vmem()] * len(outs),
                    compiler_params=params(20),
                    cost_estimate=cost(groups * group * block * group * 12, 4 * groups * group * block * 2),
                )(
                    place, shot_index, left[2], power_high, power_low, map_high, map_low, locals_[name], bases[name],
                    came[half, 2 * second_pair], came[half, 2 * second_pair + 1], after,
                )
                after = result[-1]
                if kind == "far":
                    comes.append(lax.ppermute(result[0], "plane", partner))
            owns.append(result[0])
            images.append(result[1])
        if not half:
            migrated, *passed = *passed, image_last, *images
        *passed, image_last = last_pass(place, recv_index, right, owns, comes, half, passed, wavefield.shape, 1, group)
        after = image_last
    migrated = store_groups(passed[0], migrated)
    image_last = sum_over(image_last, "freq", freqs)
    return migrated, image_last


def solution(mesh):
    placed = (
        P("freq", None, "plane", None),
        P("freq", None, None, None, None),
        P("freq", None, None, None),
        P("freq", None, None),
        P(),
        P(),
    )
    devices = mesh.shape["plane"]
    freqs = mesh.shape["freq"]

    def body(*arrays):
        if devices == 8 and arrays[0].shape[2] == 2 * GROUP and arrays[0].shape[0] == 1 and freqs & (freqs - 1) == 0:
            return fast_shards(*arrays, devices=devices, freqs=freqs)
        return shards(*arrays)

    return jax.shard_map(
        body,
        mesh=mesh,
        in_specs=placed,
        out_specs=(P("freq", None, "plane", None), P(None, "plane")),
        check_vma=False,
    )
```
